32 devices in a mesh: dp: 8 (over y, x, core), tensor: 4 (over z).
Axes of the slice: x: 2, y: 2, z: 4, core: 2. Of those that a mesh axis runs over, the one named last changes fastest.
Arguments:
- tokens: bfloat16 [16, 1024, 512], P('dp'), may hold values from -6 to 6
- cotangent: bfloat16 [16, 1024, 512], P('dp'), may hold values from -6 to 6
- lengths: int32 [16], replicated, may hold values from 1 to 1024, 12288 in all
- dealing: int32 [16], replicated, may hold values from 0 to 15, each once
- ln1_gain: float32 [512], replicated, may hold values from 0.5 to 1.5
- ln1_bias: float32 [512], replicated, may hold values from -2 to 2
- w_query: bfloat16 [512, 512], P(None, 'tensor'), may hold values from -0.25 to 0.25
- b_query: float32 [512], P('tensor'), may hold values from -3 to 3
- w_key: bfloat16 [512, 512], P(None, 'tensor'), may hold values from -0.25 to 0.25
- w_value: bfloat16 [512, 512], P(None, 'tensor'), may hold values from -0.25 to 0.25
- b_value: float32 [512], P('tensor'), may hold values from -3 to 3
- w_out: bfloat16 [512, 512], P('tensor'), may hold values from -1.5 to 1.5
- b_out: float32 [512], replicated, may hold values from -2 to 2
- ln2_gain: float32 [512], replicated, may hold values from 0.5 to 1.5
- ln2_bias: float32 [512], replicated, may hold values from -2 to 2
- w_up: bfloat16 [512, 2048], P(None, 'tensor'), may hold values from -0.25 to 0.25
- b_up: float32 [2048], P('tensor'), may hold values from -3 to 3
- w_down: bfloat16 [2048, 512], P('tensor'), may hold values from -0.125 to 0.125
- b_down: float32 [512], replicated, may hold values from -2 to 2
Outputs:
- output: bfloat16 [16, 1024, 512], P('dp')
- grad_tokens: bfloat16 [16, 1024, 512], P('dp')
- grad_ln1_gain: float32 [512], replicated
- grad_ln1_bias: float32 [512], replicated
- grad_w_query: float32 [512, 512], P(None, 'tensor')
- grad_b_query: float32 [512], P('tensor')
- grad_w_key: float32 [512, 512], P(None, 'tensor')
- grad_w_value: float32 [512, 512], P(None, 'tensor')
- grad_b_value: float32 [512], P('tensor')
- grad_w_out: float32 [512, 512], P('tensor')
- grad_b_out: float32 [512], replicated
- grad_ln2_gain: float32 [512], replicated
- grad_ln2_bias: float32 [512], replicated
- grad_w_up: float32 [512, 2048], P(None, 'tensor')
- grad_b_up: float32 [2048], P('tensor')
- grad_w_down: float32 [2048, 512], P('tensor')
- grad_b_down: float32 [512], replicated
The draws below stay inside these ranges and needn't reach their ends.
Inputs may be any that keep to these rules, and one draw needn't show every extreme that they name: `lengths`: the live tokens of each input sequence; the longest has 1024. A permutation of the 16 sequence numbers; dealt slot p takes input sequence dealing[p], dealt slots lie along dp in order as the input sequences do.
All inputs are finite; a program needn't handle non-finite values.
Results may differ from the reference program's by a relative error of at most 0.03.
Values may be sent and summed in bfloat16 or wider, within the bound.
No kernel may reach another device: no remote copies, remote signals or barrier semaphores. Data moves between devices by JAX's collectives and lax.ppermute only.
A program may use at most 128 MiB of HBM per device.

```python
import math
import jax
import jax.numpy as jnp
import numpy as np
from jax import lax

D = 512
HEADS = 8
HEAD_SIZE = 64
FF = 2048
BLOCK = 16
SEQ_LEN = 1024
SEQS = 16


def shard_levels(key, shape, split, low, high):
    factor_of = 1.0
    for position, parts in split:
        steps = jax.random.uniform(jax.random.fold_in(jax.random.fold_in(key, 6), position), (parts,), jnp.float32, low / len(split), high / len(split))
        factor_of = factor_of * jnp.repeat(jnp.exp(steps), shape[position] // parts).reshape((-1,) + (1,) * (len(shape) - 1 - position))
    return factor_of


def split_up(number_of, total, limit, skew):
    weights = [(1 << 20) // math.isqrt(grade ** skew) + 1 for grade in range(2, number_of + 1)]
    surplus, given = total - limit - (number_of - 1), [1] * (number_of - 1)
    while surplus > 0:
        free = [i for i in range(number_of - 1) if given[i] < limit]
        pool, remaining = sum([weights[i] for i in free]), surplus
        for i in free:
            addition = min(limit - given[i], max(1, remaining * weights[i] // pool), surplus)
            given[i] = given[i] + addition
            surplus = surplus - addition
    return np.array([limit] + given)


def ragged(stream_key, number_of, total, limit, slope):
    if number_of == 2:
        one = jax.random.randint(stream_key, (), max(1, total - limit), min(limit, total - 1) + 1)
        return jnp.stack([one, total - one])
    tallies = jnp.asarray(split_up(number_of, total, limit, slope), jnp.int32)
    pairs = (number_of - 1) // 2
    source_of, receiver = tallies[1:1 + 2 * pairs:2], tallies[2:2 + 2 * pairs:2]
    slack = jnp.minimum(source_of - 1, limit - receiver)
    moved = jax.random.randint(jax.random.fold_in(stream_key, 1), (pairs,), 0, 1 << 20) % (slack + 1)
    tallies = tallies.at[1:1 + 2 * pairs:2].set(source_of - moved).at[2:2 + 2 * pairs:2].set(receiver + moved)
    return tallies[jax.random.permutation(jax.random.fold_in(stream_key, 2), number_of)]


def gaussian(stream_key, extent, spread, bound, split=(), kind=jnp.bfloat16):
    values = spread * jax.random.normal(stream_key, extent, jnp.float32)
    if split:
        values = values * shard_levels(stream_key, extent, split, -0.22, 0.18)
    return jnp.clip(values, -bound, bound).astype(kind)


def setup_inputs(seed: int = 0) -> dict:
    arg_keys = jax.random.split(jax.random.key(seed), 20)
    tokens = gaussian(arg_keys[0], (SEQS, SEQ_LEN, D), 1.0, 6.0, ((0, 8),))
    cotangent = gaussian(arg_keys[1], (SEQS, SEQ_LEN, D), 1.0, 6.0, ((0, 8),))
    lengths = ragged(arg_keys[2], SEQS, SEQS * SEQ_LEN * 3 // 4, SEQ_LEN, 2).astype(jnp.int32)
    dealing = jax.random.permutation(arg_keys[3], SEQS).astype(jnp.int32)
    ln1_gain = jnp.clip(1.0 + 0.1 * jax.random.normal(arg_keys[4], (D,), jnp.float32), 0.5, 1.5)
    ln1_bias = gaussian(arg_keys[5], (D,), 0.3, 2.0, (), jnp.float32)
    w_query = gaussian(arg_keys[6], (D, D), D ** -0.5, 0.25, ((1, 4),))
    b_query = gaussian(arg_keys[7], (D,), 0.5, 3.0, ((0, 4),), jnp.float32)
    w_key = gaussian(arg_keys[8], (D, D), D ** -0.5, 0.25, ((1, 4),))
    w_value = gaussian(arg_keys[9], (D, D), D ** -0.5, 0.25, ((1, 4),))
    b_value = gaussian(arg_keys[10], (D,), 0.5, 3.0, ((0, 4),), jnp.float32)
    w_out = gaussian(arg_keys[11], (D, D), (D // 32) ** -0.5, 1.5, ((0, 4),))
    b_out = gaussian(arg_keys[12], (D,), 0.3, 2.0, (), jnp.float32)
    ln2_gain = jnp.clip(1.0 + 0.1 * jax.random.normal(arg_keys[13], (D,), jnp.float32), 0.5, 1.5)
    ln2_bias = gaussian(arg_keys[14], (D,), 0.3, 2.0, (), jnp.float32)
    w_up = gaussian(arg_keys[15], (D, FF), D ** -0.5, 0.25, ((1, 4),))
    b_up = gaussian(arg_keys[16], (FF,), 0.5, 3.0, ((0, 4),), jnp.float32)
    w_down = gaussian(arg_keys[17], (FF, D), FF ** -0.5, 0.125, ((0, 4),))
    b_down = gaussian(arg_keys[18], (D,), 0.3, 2.0, (), jnp.float32)
    return {"tokens": tokens, "cotangent": cotangent, "lengths": lengths, "dealing": dealing, "ln1_gain": ln1_gain, "ln1_bias": ln1_bias, "w_query": w_query, "b_query": b_query, "w_key": w_key, "w_value": w_value, "b_value": b_value, "w_out": w_out, "b_out": b_out, "ln2_gain": ln2_gain, "ln2_bias": ln2_bias, "w_up": w_up, "b_up": b_up, "w_down": w_down, "b_down": b_down}


@jax.custom_vjp
def low(v):
    return lax.optimization_barrier(v.astype(jnp.bfloat16)).astype(jnp.float32)

@jax.custom_vjp
def low_back(v):
    return v

def low_keep(v):
    return (low(v), None)

def low_pass(kept, grad):
    return (grad,)

def back_keep(v):
    return (v, None)

def back_low(kept, grad):
    return (low(grad),)
low.defvjp(low_keep, low_pass)
low_back.defvjp(back_keep, back_low)
eps_norm = 1e-05
inv_root_two = 0.7071067811865476

def dot_exact(left, right):
    return jnp.dot(left, right, precision=lax.Precision.HIGHEST, preferred_element_type=jnp.float32)

def einsum_exact(form, left, right):
    return jnp.einsum(form, left, right, precision=lax.Precision.HIGHEST, preferred_element_type=jnp.float32)

def level_groups(length):
    groups = []
    group_size = 2
    while length // group_size >= 2 * BLOCK:
        groups.append(group_size)
        group_size = group_size * 2
    return groups

def pool_sum(values, group_size):
    dims_in = values.shape
    return lax.optimization_barrier(jnp.sum(values.reshape(dims_in[:-2] + (dims_in[-2] // group_size, group_size, dims_in[-1])), axis=-2))

def padded_rows(level_parts):
    dims_in = level_parts[0].shape
    padding = jnp.zeros(dims_in[:-2] + (2 * BLOCK, dims_in[-1]), jnp.float32)
    return jnp.concatenate(level_parts + [padding], axis=-2)

def block_view(stacked):
    dims_in = stacked.shape
    return stacked.reshape(dims_in[:-2] + (dims_in[-2] // 128, 128, dims_in[-1]))

def interpolate(stacked, length):
    fine_rows = stacked[..., 0, :, :]
    offset = 0
    for group_size in level_groups(length):
        level_rows = length // group_size
        fine_rows = fine_rows + jnp.repeat(stacked[..., 1, offset:offset + level_rows, :], group_size, axis=-2)
        offset = offset + level_rows
    return fine_rows

def tile_masks():
    token_positions = jnp.arange(128)
    same_pair = token_positions[:, None] // (2 * BLOCK) == token_positions[None, :] // (2 * BLOCK)
    halves_apart = token_positions[:, None] // BLOCK != token_positions[None, :] // BLOCK
    return jnp.stack([same_pair, same_pair & halves_apart]).astype(jnp.float32)[:, None]

def attention_apply(query_rows, key_row_block, value_row_block, validity_mask, attention_score_scale):
    length = query_rows.shape[-2]
    valid_column = validity_mask[:, None]
    keys_live = key_row_block * valid_column
    values_live = value_row_block * valid_column
    coarse_query, coarse_key, coarse_value, coarse_block_count = ([], [], [], [])
    for group_size in level_groups(length):
        counts = pool_sum(valid_column, group_size)
        floors = jnp.maximum(counts, 1.0)
        coarse_query.append(pool_sum(query_rows, group_size) / group_size)
        coarse_key.append(pool_sum(keys_live, group_size) / floors)
        coarse_value.append(pool_sum(values_live, group_size) / floors)
        coarse_block_count.append(counts)
    stack_query = jnp.stack([query_rows, low(padded_rows(coarse_query))], axis=-3)
    stack_key = jnp.stack([keys_live, low(padded_rows(coarse_key))], axis=-3)
    stack_value = jnp.stack([values_live, low(padded_rows(coarse_value))], axis=-3)
    key_weight_matrix = jnp.stack([validity_mask, padded_rows(coarse_block_count)[..., 0]], axis=-2)
    scores = low_back(einsum_exact('...qe,...ke->...qk', block_view(stack_query), block_view(stack_key)) * attention_score_scale)
    dims_in = key_weight_matrix.shape
    weight_tiles = key_weight_matrix.reshape(dims_in[:-1] + (dims_in[-1] // 128, 1, 128))
    prob_rows = jnp.exp(scores) * tile_masks() * weight_tiles
    numerators = low_back(einsum_exact('...qk,...ke->...qe', low(prob_rows), block_view(stack_value)))
    totals = lax.optimization_barrier(jnp.sum(prob_rows, axis=-1))
    numerators = numerators.reshape(stack_value.shape)
    totals = totals.reshape(stack_value.shape[:-1])
    fine_numer = interpolate(numerators, length)
    fine_total = interpolate(totals[..., None], length)
    return fine_numer / fine_total

def norm_forward(values, gain, shift):
    centred = values - lax.optimization_barrier(jnp.mean(values, axis=-1, keepdims=True))
    return centred * lax.rsqrt(lax.optimization_barrier(jnp.mean(centred * centred, axis=-1, keepdims=True)) + eps_norm) * gain + shift

def encoder_layer_forward(layer_parameters, input_tokens, validity_mask):
    gain_one, shift_one, w_query, b_query, w_key, w_value, b_value, w_out, b_out, gain_two, shift_two, w_up, b_up, w_down, b_down = layer_parameters
    length = input_tokens.shape[0]
    normed = low(norm_forward(input_tokens, gain_one, shift_one))
    query_rows = low(low_back(dot_exact(normed, w_query) + b_query))
    key_row_block = low(low_back(dot_exact(normed, w_key)))
    value_row_block = low(low_back(dot_exact(normed, w_value) + b_value))

    def split_into_heads(values):
        return values.reshape(length, HEADS, HEAD_SIZE).transpose(1, 0, 2)
    attention_mixture = attention_apply(split_into_heads(query_rows), split_into_heads(key_row_block), split_into_heads(value_row_block), validity_mask, HEAD_SIZE ** (-0.5))
    attention_mixture = low(low_back(attention_mixture.transpose(1, 0, 2).reshape(length, HEADS * HEAD_SIZE)))
    hidden = input_tokens + low_back(dot_exact(attention_mixture, w_out)) + b_out
    normed_two = low(norm_forward(hidden, gain_two, shift_two))
    pre_act = low_back(dot_exact(normed_two, w_up) + b_up)
    activated = low(0.5 * pre_act * (1.0 + lax.erf(pre_act * inv_root_two)))
    return hidden + low_back(dot_exact(activated, w_down)) + b_down

def reference(tokens, cotangent, lengths, dealing, ln1_gain, ln1_bias, w_query, b_query, w_key, w_value, b_value, w_out, b_out, ln2_gain, ln2_bias, w_up, b_up, w_down, b_down):
    layer_parameters = tuple((member.astype(jnp.float32) for member in (ln1_gain, ln1_bias, w_query, b_query, w_key, w_value, b_value, w_out, b_out, ln2_gain, ln2_bias, w_up, b_up, w_down, b_down)))
    token_positions = jnp.arange(SEQ_LEN, dtype=jnp.int32)

    def one_sequence(running, seq_item):
        sequence_tokens, seq_cotangent, sequence_length = seq_item
        validity_mask = (token_positions < sequence_length).astype(jnp.float32)
        layer_output, backward_function = jax.vjp(lambda weight_table, input_tokens: encoder_layer_forward(weight_table, input_tokens, validity_mask), layer_parameters, sequence_tokens.astype(jnp.float32))
        grad_params, grad_inputs = backward_function(seq_cotangent.astype(jnp.float32))
        running = tuple((prior + extra for prior, extra in zip(running, grad_params)))
        return (running, (layer_output.astype(jnp.bfloat16), grad_inputs.astype(jnp.bfloat16)))
    zero_grads = tuple((jnp.zeros_like(member) for member in layer_parameters))
    grads, (results, grad_tokens) = lax.scan(one_sequence, zero_grads, (tokens, cotangent, lengths))
    dealt_out = jnp.take(results, dealing, axis=0)
    return (dealt_out, grad_tokens, grads[0], grads[1], grads[2], grads[3], grads[4], grads[5], grads[6], grads[7], grads[8], grads[9], grads[10], grads[11], grads[12], grads[13], grads[14])
```

```python
import functools

import jax
import jax.numpy as jnp
from jax import lax
from jax.experimental import pallas as pl
from jax.experimental.pallas import tpu as pltpu
from jax.sharding import PartitionSpec as P

F32 = jnp.float32
BF16 = jnp.bfloat16
HEAD_SIZE = 64
BLOCK = 16
TILE = 128
EPS = 1e-05
INV_ROOT_TWO = 0.7071067811865476
INV_ROOT_TAU = 0.3989422804014327
SCALE = HEAD_SIZE ** (-0.5)


def mm(left, right):
    return lax.dot_general(left, right, (((1,), (0,)), ((), ())), preferred_element_type=F32)


def mm_nt(left, right):
    return lax.dot_general(left, right, (((1,), (1,)), ((), ())), preferred_element_type=F32)


def mm_tn(left, right):
    return lax.dot_general(left, right, (((0,), (0,)), ((), ())), preferred_element_type=F32)


def split_low(values):
    high = values.astype(BF16)
    return high, (values - high.astype(F32)).astype(BF16)


def mm_wide(left, values):
    high, low = split_low(values)
    return mm(left, high) + mm(left, low)


def iota(shape, axis):
    return lax.broadcasted_iota(jnp.int32, shape, axis)


def unit_rows(values):
    centred = values - jnp.mean(values, axis=-1, keepdims=True)
    inverse = lax.rsqrt(jnp.mean(centred * centred, axis=-1, keepdims=True) + EPS)
    return centred * inverse, inverse


def norm_back(grad, unit, inverse, gain):
    scaled = grad * gain
    return inverse * (
        scaled
        - jnp.mean(scaled, axis=-1, keepdims=True)
        - unit * jnp.mean(scaled * unit, axis=-1, keepdims=True)
    )


def level_shifts(rows):
    shifts = []
    shift = 1
    while (2 * rows) >> shift >= 2 * BLOCK:
        shifts.append(shift)
        shift += 1
    return shifts


def coarse_map(index, rows):
    shifts = level_shifts(rows)
    shift = jnp.zeros_like(index)
    start = jnp.zeros_like(index)
    offset = 0
    for s in shifts:
        here = index >= offset
        shift = jnp.where(here, s, shift)
        start = jnp.where(here, offset, start)
        offset += rows >> s
    other = index >= offset
    start = jnp.where(other, offset, start)
    return shift, index - start, other


def coarse_counts(index, rows, length, own, partner):
    shift, place, other = coarse_map(index, rows)
    base = jnp.where(other, partner, own)
    left = length - base - lax.shift_left(place, shift)
    return jnp.clip(left, 0, lax.shift_left(jnp.ones_like(shift), shift)).astype(F32), shift


def pool_matrix(rows):
    coarse = iota((rows, rows), 0)
    fine = iota((rows, rows), 1)
    shift, place, other = coarse_map(coarse, rows)
    hit = (lax.shift_right_logical(fine, shift) == place) & jnp.logical_not(other)
    return hit.astype(F32).astype(BF16)


def spread_matrix(rows):
    fine = iota((rows, rows), 0)
    coarse = iota((rows, rows), 1)
    shift, place, other = coarse_map(coarse, rows)
    hit = (lax.shift_right_logical(fine, shift) == place) & jnp.logical_not(other)
    return hit.astype(F32).astype(BF16)


def top_pool(rows):
    shift = level_shifts(rows)[-1]
    count = rows >> shift
    hit = lax.shift_right_logical(iota((count, rows), 1), shift) == iota((count, rows), 0)
    return hit.astype(F32).astype(BF16)


def head_masks(width=TILE):
    lane = iota((width, TILE), 1)
    first = (lane < HEAD_SIZE).astype(F32)
    return first.astype(BF16), (1.0 - first).astype(BF16)


def full_weight(ref, z, lanes):
    inner, outer = ref.shape[0], ref.shape[1]
    return jnp.concatenate(
        [ref[c, o, z, :, lanes] for o in range(outer) for c in range(inner)], axis=0
    )


def full_weight2(ref, z, which):
    inner, outer = ref.shape[0], ref.shape[1]
    return jnp.concatenate(
        [ref[c, o, z, which, :, :] for o in range(outer) for c in range(inner)], axis=0
    )


def norm_one_kernel(info, own_ref, other_ref, gain_ref, bias_ref, normed_ref, pooled_ref):
    rows = own_ref.shape[0]
    length, partner = info[0], info[2]
    gain, bias = gain_ref[...], bias_ref[...]
    unit, _ = unit_rows(own_ref[...].astype(F32))
    normed_ref[...] = (unit * gain + bias).astype(BF16)
    unit, _ = unit_rows(other_ref[...].astype(F32))
    normed = (unit * gain + bias).astype(BF16)
    pool = top_pool(rows)
    count = pool.shape[0]
    live = (iota((1, rows), 1) + partner < length).astype(F32)
    pool_live = (pool.astype(F32) * live).astype(BF16)
    sums = mm(pool_live, normed)
    counts = jnp.sum(pool_live.astype(F32), axis=-1, keepdims=True)
    mean_live = sums / jnp.maximum(counts, 1.0)
    mean_all = mm(pool, normed) * (count / rows)
    high, low = split_low(mean_all)
    pooled_ref[0 * count : 1 * count, :] = high
    pooled_ref[1 * count : 2 * count, :] = low
    high, low = split_low(mean_live)
    pooled_ref[2 * count : 3 * count, :] = high
    pooled_ref[3 * count : 4 * count, :] = low


def attend_kernel(
    info,
    normed_ref,
    pooled_ref,
    weight_ref,
    bias_ref,
    mixed_ref,
    mixed_wide_ref,
    total_ref,
    q_ref,
    k_ref,
    v_ref,
    prob_ref,
    pool_s,
    spread_s,
    weight_s,
    mask_s,
    numer_s,
):
    rows = normed_ref.shape[0]
    pairs = q_ref.shape[0]
    tiles = 2 * rows // TILE
    half_tiles = rows // TILE
    length, own, partner = info[0], info[1], info[2]
    pool_s[...] = pool_matrix(rows)
    spread_s[...] = spread_matrix(rows)
    lane = iota((1, 2 * TILE), 1) & (TILE - 1)
    for i in range(half_tiles):
        weight_s[i] = (lane + (own + i * TILE) < length).astype(F32)
        counts, _ = coarse_counts(lane + i * TILE, rows, length, own, partner)
        weight_s[half_tiles + i] = counts
    row_at = iota((TILE, 2 * TILE), 0)
    key_at = iota((TILE, 2 * TILE), 1) & (TILE - 1)
    pair_same = (row_at >> 5) == (key_at >> 5)
    apart = (row_at >> 4) != (key_at >> 4)
    mask_s[0] = pair_same.astype(F32)
    mask_s[1] = (pair_same & apart).astype(F32)
    live = (iota((rows, 1), 0) + own < length).astype(F32)
    counts, shift = coarse_counts(iota((rows, 1), 0), rows, length, own, partner)
    key_scale = 1.0 / jnp.maximum(counts, 1.0)
    query_scale = 1.0 / lax.shift_left(jnp.ones_like(shift), shift).astype(F32)
    top = pooled_ref.shape[0] // 4
    counts_other = counts[rows - top :]
    filled = counts_other / jnp.maximum(counts_other, 1.0)
    head_lane = (iota((TILE, TILE), 1) >= HEAD_SIZE).astype(F32)
    ones_second = head_lane.astype(BF16)
    ones_first = (1.0 - head_lane).astype(BF16)

    def one_pair(p, carry):
        weight = full_weight(weight_ref, p, slice(0, 3 * TILE))
        wide = mm(normed_ref[...], weight)
        bq = bias_ref[p, 0:1, :]
        bv = bias_ref[p, 1:2, :]
        query = (wide[:, :TILE] + bq).astype(BF16)
        key = (wide[:, TILE : 2 * TILE].astype(BF16).astype(F32) * live).astype(BF16)
        value = ((wide[:, 2 * TILE :] + bv).astype(BF16).astype(F32) * live).astype(BF16)
        extra = mm(pooled_ref[...], weight)
        q_other = extra[:top, :TILE] + extra[top : 2 * top, :TILE] + bq
        kv_other = extra[2 * top : 3 * top, TILE:] + extra[3 * top :, TILE:]
        k_other = kv_other[:, :TILE]
        v_other = kv_other[:, TILE:] + bv * filled
        q_ref[p, :rows, :] = query
        k_ref[p, :rows, :] = key
        v_ref[p, :rows, :] = value
        pool = pool_s[...]
        q_ref[p, rows:, :] = (mm(pool, query) * query_scale).astype(BF16)
        k_ref[p, rows:, :] = (mm(pool, key) * key_scale).astype(BF16)
        v_ref[p, rows:, :] = (mm(pool, value) * key_scale).astype(BF16)
        q_ref[p, 2 * rows - top :, :] = q_other.astype(BF16)
        k_ref[p, 2 * rows - top :, :] = k_other.astype(BF16)
        v_ref[p, 2 * rows - top :, :] = v_other.astype(BF16)

        def one_tile(i, inner):
            at = pl.ds(pl.multiple_of(i * TILE, TILE), TILE)
            q = q_ref[p, at, :]
            k = k_ref[p, at, :]
            v = v_ref[p, at, :]
            keys = jnp.concatenate([k * ones_first, k * ones_second], axis=0)
            score = mm_nt(q, keys) * SCALE
            mask = mask_s[jnp.where(i >= half_tiles, 1, 0)]
            prob = jnp.where(mask > 0.0, jnp.exp(score) * weight_s[i], 0.0).astype(BF16)
            prob_ref[p, i] = prob
            values = jnp.concatenate(
                [
                    jnp.concatenate([v * ones_first, ones_first], axis=1),
                    jnp.concatenate([v * ones_second, ones_second], axis=1),
                ],
                axis=0,
            )
            numer_s[at, :] = mm(prob, values)
            return inner

        lax.fori_loop(0, tiles, one_tile, 0, unroll=2)
        both = numer_s[:rows, :] + mm_wide(spread_s[...], numer_s[rows:, :])
        total = both[:, TILE:]
        mixed = both[:, :TILE] / total
        total_ref[p] = total
        mixed_wide_ref[p] = mixed
        mixed_ref[p] = mixed.astype(BF16)
        return carry

    lax.fori_loop(0, pairs, one_pair, 0)


def feed_kernel(
    own_ref,
    mixed_ref,
    weight_ref,
    ffn_ref,
    b_out_ref,
    gain_ref,
    shift_ref,
    b_up_ref,
    b_down_ref,
    out_ref,
    hidden_ref,
    normed_ref,
    act_ref,
    slope_ref,
):
    pairs = mixed_ref.shape[0]
    hidden = own_ref[...].astype(F32) + b_out_ref[...]
    for p in range(pairs):
        hidden = hidden + mm_nt(mixed_ref[p], full_weight(weight_ref, p, slice(3 * TILE, None)))
    hidden_ref[...] = hidden
    unit, _ = unit_rows(hidden)
    normed = (unit * gain_ref[...] + shift_ref[...]).astype(BF16)
    normed_ref[...] = normed
    result = hidden + b_down_ref[...]
    for z in range(pairs):
        pre = mm(normed, full_weight2(ffn_ref, z, 0)) + b_up_ref[z]
        half_erf = 0.5 + 0.5 * lax.erf(pre * INV_ROOT_TWO)
        act = (pre * half_erf).astype(BF16)
        act_ref[z] = act
        slope_ref[z] = (half_erf + pre * jnp.exp(-0.5 * pre * pre) * INV_ROOT_TAU).astype(BF16)
        result = result + mm(act, full_weight2(ffn_ref, z, 1))
    out_ref[...] = result.astype(BF16)


def feed_back_kernel(
    dy_ref,
    ffn_ref,
    weight_ref,
    slope_ref,
    hidden_ref,
    gain_ref,
    mixed_wide_ref,
    total_ref,
    grad_pre_ref,
    grad_hidden_ref,
    grad_hidden_low_ref,
    numer_ref,
    gtotal_ref,
    exchange_ref,
    vector_ref,
    b_up_ref,
):
    rows = dy_ref.shape[0]
    pairs = slope_ref.shape[0]
    dy = dy_ref[...]
    grad_normed = jnp.zeros((rows, dy.shape[1]), F32)
    for z in range(pairs):
        grad_act = mm_nt(dy, full_weight2(ffn_ref, z, 1))
        grad_pre = (grad_act * slope_ref[z].astype(F32)).astype(BF16)
        grad_pre_ref[z] = grad_pre
        b_up_ref[z] = jnp.sum(grad_pre.astype(F32), axis=0, keepdims=True)
        grad_normed = grad_normed + mm_nt(grad_pre, full_weight2(ffn_ref, z, 0))
    unit, inverse = unit_rows(hidden_ref[...])
    dy_wide = dy.astype(F32)
    vector_ref[0:1, :] = jnp.sum(grad_normed * unit, axis=0, keepdims=True)
    vector_ref[1:2, :] = jnp.sum(grad_normed, axis=0, keepdims=True)
    vector_ref[2:3, :] = jnp.sum(dy_wide, axis=0, keepdims=True)
    grad_hidden = dy_wide + norm_back(grad_normed, unit, inverse, gain_ref[...])
    vector_ref[3:4, :] = jnp.sum(grad_hidden, axis=0, keepdims=True)
    grad_hidden_ref[...] = grad_hidden
    low = grad_hidden.astype(BF16)
    grad_hidden_low_ref[...] = low
    pool = top_pool(rows)
    top = pool.shape[0]
    same = ((iota((TILE, TILE), 0) // HEAD_SIZE) == (iota((TILE, TILE), 1) // HEAD_SIZE)).astype(F32).astype(BF16)
    for p in range(pairs):
        grad_mixed = mm(low, full_weight(weight_ref, p, slice(3 * TILE, None))).astype(BF16).astype(F32)
        inv = 1.0 / total_ref[p]
        numer = grad_mixed * inv
        high, rest = split_low(grad_mixed * mixed_wide_ref[p])
        gtotal = -(mm(high, same) + mm(rest, same)) * inv
        numer_ref[p] = numer
        gtotal_ref[p] = gtotal
        exchange_ref[:top, p * TILE : (p + 1) * TILE] = mm_wide(pool, numer)
        exchange_ref[top:, p * TILE : (p + 1) * TILE] = mm_wide(pool, gtotal)


def feed_grads_kernel(normed_ref, act_ref, grad_pre_ref, dy_ref, out_ref):
    pairs = act_ref.shape[0]
    inner, outer, _, _, chunk, _ = out_ref.shape
    for z in range(pairs):
        up = mm_tn(normed_ref[...], grad_pre_ref[z]).astype(BF16)
        down = mm_tn(act_ref[z], dy_ref[...]).astype(BF16)
        for o in range(outer):
            for c in range(inner):
                at = (o * inner + c) * chunk
                out_ref[c, o, z, 0] = up[at : at + chunk]
                out_ref[c, o, z, 1] = down[at : at + chunk]


def attend_back_kernel(
    info,
    numer_ref,
    gtotal_ref,
    exchange_ref,
    q_ref,
    k_ref,
    v_ref,
    prob_ref,
    weight_ref,
    own_ref,
    gain_ref,
    grad_hidden_ref,
    grad_tokens_ref,
    grads_ref,
    vector_ref,
    b_qv_ref,
    pool_s,
    spread_s,
    numer_s,
    gtotal_s,
    gq_s,
    gk_s,
    gv_s,
    acc_s,
):
    rows = own_ref.shape[0]
    pairs = q_ref.shape[0]
    tiles = 2 * rows // TILE
    length, own, partner = info[0], info[1], info[2]
    pool_s[...] = pool_matrix(rows)
    spread_s[...] = spread_matrix(rows)
    live = (iota((rows, 1), 0) + own < length).astype(F32)
    counts, shift = coarse_counts(iota((rows, 1), 0), rows, length, own, partner)
    key_scale = SCALE / jnp.maximum(counts, 1.0)
    value_scale = 1.0 / jnp.maximum(counts, 1.0)
    query_scale = SCALE / lax.shift_left(jnp.ones_like(shift), shift).astype(F32)
    lane = iota((TILE, TILE), 1)
    second = (lane >= HEAD_SIZE).astype(F32)
    ones_second = second.astype(BF16)
    ones_first = (1.0 - second).astype(BF16)
    at_lane = lane & (HEAD_SIZE - 1)
    pick = (at_lane < 2).astype(F32)
    pick_first = (pick * (1.0 - second)).astype(BF16)
    pick_second = (pick * second).astype(BF16)
    is_low = at_lane == 1
    top = exchange_ref.shape[1] // 2
    acc_s[...] = jnp.zeros_like(acc_s)

    def one_pair(p, carry):
        pool = pool_s[...]
        numer = numer_ref[p]
        gtotal = gtotal_ref[p]
        numer_s[:rows, :] = numer.astype(BF16)
        numer_s[rows:, :] = mm_wide(pool, numer).astype(BF16)
        gtotal_s[:rows, :] = gtotal
        gtotal_s[rows:, :] = mm_wide(pool, gtotal)
        numer_s[2 * rows - top :, :] = exchange_ref[p, :top, :].astype(BF16)
        gtotal_s[2 * rows - top :, :] = exchange_ref[p, top:, :]

        def one_tile(i, inner):
            at = pl.ds(pl.multiple_of(i * TILE, TILE), TILE)
            q = q_ref[p, at, :]
            k = k_ref[p, at, :]
            v = v_ref[p, at, :]
            prob = prob_ref[p, i]
            numer = numer_s[at, :]
            gtotal = gtotal_s[at, :]
            high = gtotal.astype(BF16).astype(F32)
            mixed_total = jnp.where(is_low, gtotal - high, high).astype(BF16)
            left = jnp.concatenate([numer, mixed_total], axis=1)
            right = jnp.concatenate(
                [
                    jnp.concatenate([v * ones_first, pick_first], axis=1),
                    jnp.concatenate([v * ones_second, pick_second], axis=1),
                ],
                axis=0,
            )
            grad_prob = mm_nt(left, right)
            grad_score = (grad_prob * prob.astype(F32)).astype(BF16)
            keys = jnp.concatenate([k * ones_first, k * ones_second], axis=0)
            gq_s[at, :] = mm(grad_score, keys)
            gk = mm_tn(grad_score, q)
            gk_s[at, :] = jnp.where(lane < HEAD_SIZE, gk[:TILE], gk[TILE:])
            gv = mm_tn(prob, numer)
            gv_s[at, :] = jnp.where(lane < HEAD_SIZE, gv[:TILE], gv[TILE:])
            return inner

        lax.fori_loop(0, tiles, one_tile, 0, unroll=2)
        spread = spread_s[...]
        gq = gq_s[:rows, :] * SCALE + mm_wide(spread, gq_s[rows:, :] * query_scale)
        gk = (gk_s[:rows, :] * SCALE + mm_wide(spread, gk_s[rows:, :] * key_scale)) * live
        gv = (gv_s[:rows, :] + mm_wide(spread, gv_s[rows:, :] * value_scale)) * live
        gq, gk, gv = gq.astype(BF16), gk.astype(BF16), gv.astype(BF16)
        b_qv_ref[p, 0:1, :] = jnp.sum(gq.astype(F32), axis=0, keepdims=True)
        b_qv_ref[p, 1:2, :] = jnp.sum(gv.astype(F32), axis=0, keepdims=True)
        grads = jnp.concatenate([gq, gk, gv], axis=1)
        grads_ref[p] = grads
        acc_s[...] += mm_nt(grads, full_weight(weight_ref, p, slice(0, 3 * TILE)))
        return carry

    lax.fori_loop(0, pairs, one_pair, 0)
    unit, inverse = unit_rows(own_ref[...].astype(F32))
    grad_normed = acc_s[...]
    vector_ref[0:1, :] = jnp.sum(grad_normed * unit, axis=0, keepdims=True)
    vector_ref[1:2, :] = jnp.sum(grad_normed, axis=0, keepdims=True)
    grad_tokens_ref[...] = (
        grad_hidden_ref[...] + norm_back(grad_normed, unit, inverse, gain_ref[...])
    ).astype(BF16)


def attend_grads_kernel(normed_ref, grads_ref, grad_hidden_ref, mixed_ref, out_ref):
    pairs = grads_ref.shape[0]
    inner, outer, _, chunk, _ = out_ref.shape
    for z in range(pairs):
        qkv = mm_tn(normed_ref[...], grads_ref[z]).astype(BF16)
        back = mm_tn(grad_hidden_ref[...], mixed_ref[z]).astype(BF16)
        both = jnp.concatenate([qkv, back], axis=1)
        for o in range(outer):
            for c in range(inner):
                at = (o * inner + c) * chunk
                out_ref[c, o, z] = both[at : at + chunk]


VMEM_SPEC = pl.BlockSpec(memory_space=pltpu.VMEM)
SMEM_SPEC = pl.BlockSpec(memory_space=pltpu.SMEM)


def call(kernel, outs, scalars, args, scratch=(), limit=48, flops=0):
    return pl.pallas_call(
        kernel,
        out_shape=[jax.ShapeDtypeStruct(shape, dtype) for shape, dtype in outs],
        in_specs=[SMEM_SPEC] * len(scalars) + [VMEM_SPEC] * len(args),
        out_specs=[VMEM_SPEC] * len(outs),
        scratch_shapes=list(scratch),
        compiler_params=pltpu.CompilerParams(vmem_limit_bytes=limit << 20),
        cost_estimate=pl.CostEstimate(flops=flops, transcendentals=0, bytes_accessed=8 << 20),
    )(*scalars, *args)


def exchange(pieces, axis, groups=None):
    return lax.all_to_all(pieces, axis, 0, 0, tiled=True, axis_index_groups=groups)


def gather(piece, axis, count, groups=None):
    return exchange(jnp.broadcast_to(piece[None], (count,) + piece.shape), axis, groups)


def total_of(pieces):
    return jnp.sum(pieces.astype(F32), axis=0).astype(BF16)


def local(
    tokens,
    cotangent,
    lengths,
    dealing,
    ln1_gain,
    ln1_bias,
    w_query,
    b_query,
    w_key,
    w_value,
    b_value,
    w_out,
    b_out,
    ln2_gain,
    ln2_bias,
    w_up,
    b_up,
    w_down,
    b_down,
):
    seq_dev, length, width = tokens.shape
    dp = lax.axis_size("dp")
    nt = lax.axis_size("tensor")
    d = lax.axis_index("dp")
    t = lax.axis_index("tensor")
    rows = seq_dev * length // nt
    inner = 2
    outer = dp // inner
    pairs = [[inner * i + c for c in range(inner)] for i in range(outer)]
    planes = [[inner * i + c for i in range(outer)] for c in range(inner)]
    chunk = width // dp
    hid = w_up.shape[1]

    def own_rows(weight):
        return lax.dynamic_slice_in_dim(weight, d * chunk, chunk, axis=0)

    out_cols = lax.dynamic_slice_in_dim(w_out, d * chunk, chunk, axis=1).T
    attn_piece = jnp.concatenate(
        [own_rows(w_query), own_rows(w_key), own_rows(w_value), out_cols], axis=1
    )
    ffn_piece = jnp.stack([own_rows(w_up), own_rows(w_down)])
    bias_piece = jnp.concatenate([b_query, b_value, b_up]).reshape(-1, TILE)
    bias_piece = jnp.pad(bias_piece, ((0, -bias_piece.shape[0] % 8), (0, 0)))
    attn_w = gather(attn_piece, "tensor", nt)
    biases = gather(bias_piece, "tensor", nt)
    attn_w = gather(attn_w, "dp", outer, planes)
    ffn_w = gather(ffn_piece, "tensor", nt)
    attn_w = gather(attn_w, "dp", inner, pairs)
    ffn_w = gather(ffn_w, "dp", outer, planes)
    ffn_w = gather(ffn_w, "dp", inner, pairs)
    b_qv = biases[:, 0:2]
    b_ups = biases[:, 2 : 2 + hid // TILE].reshape(nt, 1, hid)

    halves = tokens.reshape(nt, rows, width)
    own = lax.dynamic_index_in_dim(halves, t, 0, keepdims=False)
    other = lax.dynamic_index_in_dim(halves, t ^ 1, 0, keepdims=False)
    dy = lax.dynamic_index_in_dim(cotangent.reshape(nt, rows, width), t, 0, keepdims=False)
    own_length = lengths[d * seq_dev + t // 2]
    own_base = (t % 2) * rows
    info = jnp.stack([own_length, own_base, rows - own_base]).astype(jnp.int32)
    row = lambda v: v.reshape(1, -1)
    top = rows >> level_shifts(rows)[-1]

    normed_one, pooled = call(
        norm_one_kernel,
        [((rows, width), BF16), ((4 * top, width), BF16)],
        [info],
        [own, other, row(ln1_gain), row(ln1_bias)],
        limit=16,
    )
    mixed, mixed_wide, total, q, k, v, prob = call(
        attend_kernel,
        [((nt, rows, TILE), BF16), ((nt, rows, TILE), F32), ((nt, rows, TILE), F32)]
        + [((nt, 2 * rows, TILE), BF16)] * 3
        + [((nt, 2 * rows // TILE, TILE, 2 * TILE), BF16)],
        [info],
        [normed_one, pooled, attn_w, b_qv],
        scratch=[
            pltpu.VMEM((rows, rows), BF16),
            pltpu.VMEM((rows, rows), BF16),
            pltpu.VMEM((2 * rows // TILE, 1, 2 * TILE), F32),
            pltpu.VMEM((2, TILE, 2 * TILE), F32),
            pltpu.VMEM((2 * rows, 2 * TILE), F32),
        ],
        flops=10**10,
    )
    out, hidden, normed_two, act, slope = call(
        feed_kernel,
        [((rows, width), BF16), ((rows, width), F32), ((rows, width), BF16)]
        + [((nt, rows, hid), BF16)] * 2,
        [],
        [own, mixed, attn_w, ffn_w, row(b_out), row(ln2_gain), row(ln2_bias), b_ups, row(b_down)],
        flops=10**10,
    )

    n_all = dp * nt
    piece = rows // n_all
    dealt = exchange(out.reshape(n_all, piece, width), ("dp", "tensor"))
    dealt = jnp.take(dealt.reshape(dp * seq_dev, -1, piece, width), dealing, axis=0)
    dealt = exchange(dealt.reshape(dp, seq_dev, -1, piece, width), "dp")
    dealt = gather(dealt, "tensor", nt)
    output = dealt.transpose(2, 3, 1, 0, 4, 5).reshape(seq_dev, length, width)

    grad_pre, grad_hidden, grad_hidden_low, numer, gtotal, sent, vec_two, vec_up = call(
        feed_back_kernel,
        [
            ((nt, rows, hid), BF16),
            ((rows, width), F32),
            ((rows, width), BF16),
            ((nt, rows, TILE), F32),
            ((nt, rows, TILE), F32),
            ((2 * top, width), F32),
            ((4, width), F32),
            ((nt, 1, hid), F32),
        ],
        [],
        [dy, ffn_w, attn_w, slope, hidden, row(ln2_gain), mixed_wide, total],
        flops=10**10,
    )
    swapped = lax.ppermute(sent, "tensor", [(i, i ^ 1) for i in range(nt)])
    swapped = swapped.reshape(2 * top, nt, TILE).transpose(1, 0, 2)
    (ffn_grads,) = call(
        feed_grads_kernel,
        [((inner, outer, nt, 2, chunk, hid), BF16)],
        [],
        [normed_two, act, grad_pre, dy],
        flops=10**10,
    )
    grad_low, qkv_grads, vec_one, vec_qv = call(
        attend_back_kernel,
        [
            ((rows, width), BF16),
            ((nt, rows, 3 * TILE), BF16),
            ((2, width), F32),
            ((nt, 2, TILE), F32),
        ],
        [info],
        [numer, gtotal, swapped, q, k, v, prob, attn_w, own, row(ln1_gain), grad_hidden],
        scratch=[
            pltpu.VMEM((rows, rows), BF16),
            pltpu.VMEM((rows, rows), BF16),
            pltpu.VMEM((2 * rows, TILE), BF16),
            pltpu.VMEM((2 * rows, TILE), F32),
            pltpu.VMEM((2 * rows, TILE), F32),
            pltpu.VMEM((2 * rows, TILE), F32),
            pltpu.VMEM((2 * rows, TILE), F32),
            pltpu.VMEM((rows, width), F32),
        ],
        flops=10**10,
    )
    grad_tokens = gather(grad_low, "tensor", nt).reshape(seq_dev, length, width)
    (attn_grads,) = call(
        attend_grads_kernel,
        [((inner, outer, nt, chunk, 4 * TILE), BF16)],
        [],
        [normed_one, qkv_grads, grad_hidden_low, mixed],
        flops=10**10,
    )

    def reduced(grads):
        grads = total_of(exchange(grads, "dp", pairs))
        grads = total_of(exchange(grads, "dp", planes))
        grads = total_of(exchange(grads, "tensor"))
        return gather(grads, "dp", dp)

    ffn_grads = reduced(ffn_grads).astype(F32)
    attn_grads = reduced(attn_grads).astype(F32)
    g_up = ffn_grads[:, 0].reshape(width, hid)
    g_down = ffn_grads[:, 1].reshape(hid, width)
    attn_grads = attn_grads.reshape(width, 4 * TILE)
    g_query = attn_grads[:, :TILE]
    g_key = attn_grads[:, TILE : 2 * TILE]
    g_value = attn_grads[:, 2 * TILE : 3 * TILE]
    g_out = attn_grads[:, 3 * TILE :].T

    vectors = jnp.concatenate(
        [vec_two, vec_up.reshape(nt, hid), vec_one, vec_qv.transpose(1, 0, 2).reshape(2, -1)]
    )
    vectors = gather(vectors.astype(BF16), ("dp", "tensor"), n_all)
    vectors = jnp.sum(vectors.astype(F32), axis=0)
    base = 4 + nt
    g_b_up = lax.dynamic_index_in_dim(vectors[4:base], t, 0, keepdims=False)
    g_b_q = lax.dynamic_index_in_dim(vectors[base + 2].reshape(nt, TILE), t, 0, keepdims=False)
    g_b_v = lax.dynamic_index_in_dim(vectors[base + 3].reshape(nt, TILE), t, 0, keepdims=False)
    return (
        output,
        grad_tokens,
        vectors[base],
        vectors[base + 1],
        g_query,
        g_b_q,
        g_key,
        g_value,
        g_b_v,
        g_out,
        vectors[3],
        vectors[0],
        vectors[1],
        g_up,
        g_b_up,
        g_down,
        vectors[2],
    )


def solution(mesh):
    placed = (
        P("dp", None, None),
        P("dp", None, None),
        P(),
        P(),
        P(),
        P(),
        P(None, "tensor"),
        P("tensor"),
        P(None, "tensor"),
        P(None, "tensor"),
        P("tensor"),
        P("tensor", None),
        P(),
        P(),
        P(),
        P(None, "tensor"),
        P("tensor"),
        P("tensor", None),
        P(),
    )
    return jax.shard_map(
        local,
        mesh=mesh,
        in_specs=placed,
        out_specs=(
            P("dp", None, None),
            P("dp", None, None),
            P(),
            P(),
            P(None, "tensor"),
            P("tensor"),
            P(None, "tensor"),
            P(None, "tensor"),
            P("tensor"),
            P("tensor", None),
            P(),
            P(),
            P(),
            P(None, "tensor"),
            P("tensor"),
            P("tensor", None),
            P(),
        ),
        check_vma=False,
    )
```

```python
import functools

import jax
import jax.numpy as jnp
from jax import lax
from jax.experimental import pallas as pl
from jax.experimental.pallas import tpu as pltpu
from jax.sharding import PartitionSpec as P

F32 = jnp.float32
BF16 = jnp.bfloat16
HEAD_SIZE = 64
BLOCK = 16
TILE = 128
EPS = 1e-05
INV_ROOT_TWO = 0.7071067811865476
INV_ROOT_TAU = 0.3989422804014327
SCALE = HEAD_SIZE ** (-0.5)


def mm(left, right):
    return lax.dot_general(left, right, (((1,), (0,)), ((), ())), preferred_element_type=F32)


def mm_nt(left, right):
    return lax.dot_general(left, right, (((1,), (1,)), ((), ())), preferred_element_type=F32)


def mm_tn(left, right):
    return lax.dot_general(left, right, (((0,), (0,)), ((), ())), preferred_element_type=F32)


def split_low(values):
    high = values.astype(BF16)
    return high, (values - high.astype(F32)).astype(BF16)


def mm_wide(left, values):
    high, low = split_low(values)
    return mm(left, high) + mm(left, low)


def iota(shape, axis):
    return lax.broadcasted_iota(jnp.int32, shape, axis)


def unit_rows(values):
    centred = values - jnp.mean(values, axis=-1, keepdims=True)
    inverse = lax.rsqrt(jnp.mean(centred * centred, axis=-1, keepdims=True) + EPS)
    return centred * inverse, inverse


def norm_back(grad, unit, inverse, gain):
    scaled = grad * gain
    return inverse * (
        scaled
        - jnp.mean(scaled, axis=-1, keepdims=True)
        - unit * jnp.mean(scaled * unit, axis=-1, keepdims=True)
    )


def level_shifts(rows):
    shifts = []
    shift = 1
    while (2 * rows) >> shift >= 2 * BLOCK:
        shifts.append(shift)
        shift += 1
    return shifts


def coarse_map(index, rows):
    shifts = level_shifts(rows)
    shift = jnp.zeros_like(index)
    start = jnp.zeros_like(index)
    offset = 0
    for s in shifts:
        here = index >= offset
        shift = jnp.where(here, s, shift)
        start = jnp.where(here, offset, start)
        offset += rows >> s
    other = index >= offset
    start = jnp.where(other, offset, start)
    return shift, index - start, other


def coarse_counts(index, rows, length, own, partner):
    shift, place, other = coarse_map(index, rows)
    base = jnp.where(other, partner, own)
    left = length - base - lax.shift_left(place, shift)
    return jnp.clip(left, 0, lax.shift_left(jnp.ones_like(shift), shift)).astype(F32), shift


def pool_matrix(rows):
    coarse = iota((rows, rows), 0)
    fine = iota((rows, rows), 1)
    shift, place, other = coarse_map(coarse, rows)
    hit = (lax.shift_right_logical(fine, shift) == place) & jnp.logical_not(other)
    return hit.astype(F32).astype(BF16)


def spread_matrix(rows):
    fine = iota((rows, rows), 0)
    coarse = iota((rows, rows), 1)
    shift, place, other = coarse_map(coarse, rows)
    hit = (lax.shift_right_logical(fine, shift) == place) & jnp.logical_not(other)
    return hit.astype(F32).astype(BF16)


def top_pool(rows):
    shift = level_shifts(rows)[-1]
    count = rows >> shift
    hit = lax.shift_right_logical(iota((count, rows), 1), shift) == iota((count, rows), 0)
    return hit.astype(F32).astype(BF16)


def head_masks(width=TILE):
    lane = iota((width, TILE), 1)
    first = (lane < HEAD_SIZE).astype(F32)
    return first.astype(BF16), (1.0 - first).astype(BF16)


def assemble(info, near_ref, far_ref, to_ref):
    core, plane, line = info[3], info[4], info[5]
    chunk = near_ref.shape[-2]
    for far, ref in enumerate((near_ref, far_ref)):
        for o in range(ref.shape[0]):
            at = ((o ^ plane) * 2 + (far ^ core)) * chunk
            at = pl.ds(pl.multiple_of(at, chunk), chunk)
            for z in range(ref.shape[1]):
                if len(ref.shape) == 5:
                    for part in range(ref.shape[2]):
                        to_ref[z ^ line, part, at, :] = ref[o, z, part]
                else:
                    to_ref[z ^ line, at, :] = ref[o, z]


def norm_one_kernel(info, own_ref, other_ref, gain_ref, bias_ref, normed_ref, pooled_ref):
    rows = own_ref.shape[0]
    length, partner = info[0], info[2]
    gain, bias = gain_ref[...], bias_ref[...]
    unit, _ = unit_rows(own_ref[...].astype(F32))
    normed_ref[...] = (unit * gain + bias).astype(BF16)
    unit, _ = unit_rows(other_ref[...].astype(F32))
    normed = (unit * gain + bias).astype(BF16)
    pool = top_pool(rows)
    count = pool.shape[0]
    live = (iota((1, rows), 1) + partner < length).astype(F32)
    pool_live = (pool.astype(F32) * live).astype(BF16)
    sums = mm(pool_live, normed)
    counts = jnp.sum(pool_live.astype(F32), axis=-1, keepdims=True)
    mean_live = sums / jnp.maximum(counts, 1.0)
    mean_all = mm(pool, normed) * (count / rows)
    high, low = split_low(mean_all)
    pooled_ref[0 * count : 1 * count, :] = high
    pooled_ref[1 * count : 2 * count, :] = low
    high, low = split_low(mean_live)
    pooled_ref[2 * count : 3 * count, :] = high
    pooled_ref[3 * count : 4 * count, :] = low


def attend_kernel(
    info,
    normed_ref,
    pooled_ref,
    near_ref,
    far_ref,
    bias_ref,
    mixed_ref,
    mixed_wide_ref,
    total_ref,
    q_ref,
    k_ref,
    v_ref,
    prob_ref,
    pool_s,
    spread_s,
    weight_s,
    mask_s,
    numer_s,
    full_s,
):
    rows = normed_ref.shape[0]
    pairs = q_ref.shape[0]
    tiles = 2 * rows // TILE
    half_tiles = rows // TILE
    length, own, partner = info[0], info[1], info[2]
    line = info[5]
    assemble(info, near_ref, far_ref, full_s)
    pool_s[...] = pool_matrix(rows)
    spread_s[...] = spread_matrix(rows)
    lane = iota((1, 2 * TILE), 1) & (TILE - 1)
    for i in range(half_tiles):
        weight_s[i] = (lane + (own + i * TILE) < length).astype(F32)
        counts, _ = coarse_counts(lane + i * TILE, rows, length, own, partner)
        weight_s[half_tiles + i] = counts
    row_at = iota((TILE, 2 * TILE), 0)
    key_at = iota((TILE, 2 * TILE), 1) & (TILE - 1)
    pair_same = (row_at >> 5) == (key_at >> 5)
    apart = (row_at >> 4) != (key_at >> 4)
    mask_s[0] = pair_same.astype(F32)
    mask_s[1] = (pair_same & apart).astype(F32)
    live = (iota((rows, 1), 0) + own < length).astype(F32)
    counts, shift = coarse_counts(iota((rows, 1), 0), rows, length, own, partner)
    key_scale = 1.0 / jnp.maximum(counts, 1.0)
    query_scale = 1.0 / lax.shift_left(jnp.ones_like(shift), shift).astype(F32)
    top = pooled_ref.shape[0] // 4
    counts_other = counts[rows - top :]
    filled = counts_other / jnp.maximum(counts_other, 1.0)
    head_lane = (iota((TILE, TILE), 1) >= HEAD_SIZE).astype(F32)
    ones_second = head_lane.astype(BF16)
    ones_first = (1.0 - head_lane).astype(BF16)

    def one_pair(p, carry):
        weight = full_s[p, :, : 3 * TILE]
        wide = mm(normed_ref[...], weight)
        bq = bias_ref[p ^ line, 0:1, :]
        bv = bias_ref[p ^ line, 1:2, :]
        query = (wide[:, :TILE] + bq).astype(BF16)
        key = (wide[:, TILE : 2 * TILE].astype(BF16).astype(F32) * live).astype(BF16)
        value = ((wide[:, 2 * TILE :] + bv).astype(BF16).astype(F32) * live).astype(BF16)
        extra = mm(pooled_ref[...], weight)
        q_other = extra[:top, :TILE] + extra[top : 2 * top, :TILE] + bq
        kv_other = extra[2 * top : 3 * top, TILE:] + extra[3 * top :, TILE:]
        k_other = kv_other[:, :TILE]
        v_other = kv_other[:, TILE:] + bv * filled
        q_ref[p, :rows, :] = query
        k_ref[p, :rows, :] = key
        v_ref[p, :rows, :] = value
        pool = pool_s[...]
        q_ref[p, rows:, :] = (mm(pool, query) * query_scale).astype(BF16)
        k_ref[p, rows:, :] = (mm(pool, key) * key_scale).astype(BF16)
        v_ref[p, rows:, :] = (mm(pool, value) * key_scale).astype(BF16)
        q_ref[p, 2 * rows - top :, :] = q_other.astype(BF16)
        k_ref[p, 2 * rows - top :, :] = k_other.astype(BF16)
        v_ref[p, 2 * rows - top :, :] = v_other.astype(BF16)

        def one_tile(i, inner):
            at = pl.ds(pl.multiple_of(i * TILE, TILE), TILE)
            q = q_ref[p, at, :]
            k = k_ref[p, at, :]
            v = v_ref[p, at, :]
            keys = jnp.concatenate([k * ones_first, k * ones_second], axis=0)
            score = mm_nt(q, keys) * SCALE
            mask = mask_s[jnp.where(i >= half_tiles, 1, 0)]
            prob = jnp.where(mask > 0.0, jnp.exp(score) * weight_s[i], 0.0).astype(BF16)
            prob_ref[p, i] = prob
            values = jnp.concatenate(
                [
                    jnp.concatenate([v * ones_first, ones_first], axis=1),
                    jnp.concatenate([v * ones_second, ones_second], axis=1),
                ],
                axis=0,
            )
            numer_s[at, :] = mm(prob, values)
            return inner

        lax.fori_loop(0, tiles, one_tile, 0, unroll=2)
        both = numer_s[:rows, :] + mm_wide(spread_s[...], numer_s[rows:, :])
        total = both[:, TILE:]
        mixed = both[:, :TILE] / total
        total_ref[p] = total
        mixed_wide_ref[p] = mixed
        mixed_ref[p] = mixed.astype(BF16)
        return carry

    lax.fori_loop(0, pairs, one_pair, 0)


def feed_kernel(
    info,
    own_ref,
    mixed_ref,
    near_ref,
    far_ref,
    ffn_near_ref,
    ffn_far_ref,
    b_out_ref,
    gain_ref,
    shift_ref,
    b_up_ref,
    b_down_ref,
    out_ref,
    hidden_ref,
    normed_ref,
    act_ref,
    slope_ref,
    full_s,
    ffn_s,
):
    pairs = mixed_ref.shape[0]
    line = info[5]
    assemble(info, near_ref, far_ref, full_s)
    assemble(info, ffn_near_ref, ffn_far_ref, ffn_s)
    hidden = own_ref[...].astype(F32) + b_out_ref[...]
    for p in range(pairs):
        hidden = hidden + mm_nt(mixed_ref[p], full_s[p, :, 3 * TILE :])
    hidden_ref[...] = hidden
    unit, _ = unit_rows(hidden)
    normed = (unit * gain_ref[...] + shift_ref[...]).astype(BF16)
    normed_ref[...] = normed
    result = hidden + b_down_ref[...]
    for z in range(pairs):
        pre = mm(normed, ffn_s[z, 0]) + b_up_ref[z ^ line]
        half_erf = 0.5 + 0.5 * lax.erf(pre * INV_ROOT_TWO)
        act = (pre * half_erf).astype(BF16)
        act_ref[z] = act
        slope_ref[z] = (half_erf + pre * jnp.exp(-0.5 * pre * pre) * INV_ROOT_TAU).astype(BF16)
        result = result + mm(act, ffn_s[z, 1])
    out_ref[...] = result.astype(BF16)


def feed_back_kernel(
    info,
    dy_ref,
    ffn_near_ref,
    ffn_far_ref,
    near_ref,
    far_ref,
    slope_ref,
    hidden_ref,
    gain_ref,
    mixed_wide_ref,
    total_ref,
    grad_pre_ref,
    grad_hidden_ref,
    grad_hidden_low_ref,
    numer_ref,
    gtotal_ref,
    exchange_ref,
    vector_ref,
    b_up_ref,
    full_s,
    ffn_s,
):
    rows = dy_ref.shape[0]
    assemble(info, ffn_near_ref, ffn_far_ref, ffn_s)
    assemble(info, near_ref, far_ref, full_s)
    pairs = slope_ref.shape[0]
    dy = dy_ref[...]
    grad_normed = jnp.zeros((rows, dy.shape[1]), F32)
    for z in range(pairs):
        grad_act = mm_nt(dy, ffn_s[z, 1])
        grad_pre = (grad_act * slope_ref[z].astype(F32)).astype(BF16)
        grad_pre_ref[z] = grad_pre
        b_up_ref[z] = jnp.sum(grad_pre.astype(F32), axis=0, keepdims=True)
        grad_normed = grad_normed + mm_nt(grad_pre, ffn_s[z, 0])
    unit, inverse = unit_rows(hidden_ref[...])
    dy_wide = dy.astype(F32)
    vector_ref[0:1, :] = jnp.sum(grad_normed * unit, axis=0, keepdims=True)
    vector_ref[1:2, :] = jnp.sum(grad_normed, axis=0, keepdims=True)
    vector_ref[2:3, :] = jnp.sum(dy_wide, axis=0, keepdims=True)
    grad_hidden = dy_wide + norm_back(grad_normed, unit, inverse, gain_ref[...])
    vector_ref[3:4, :] = jnp.sum(grad_hidden, axis=0, keepdims=True)
    grad_hidden_ref[...] = grad_hidden
    low = grad_hidden.astype(BF16)
    grad_hidden_low_ref[...] = low
    pool = top_pool(rows)
    top = pool.shape[0]
    same = ((iota((TILE, TILE), 0) // HEAD_SIZE) == (iota((TILE, TILE), 1) // HEAD_SIZE)).astype(F32).astype(BF16)
    for p in range(pairs):
        grad_mixed = mm(low, full_s[p, :, 3 * TILE :]).astype(BF16).astype(F32)
        inv = 1.0 / total_ref[p]
        numer = grad_mixed * inv
        high, rest = split_low(grad_mixed * mixed_wide_ref[p])
        gtotal = -(mm(high, same) + mm(rest, same)) * inv
        numer_ref[p] = numer
        gtotal_ref[p] = gtotal
        exchange_ref[:top, p * TILE : (p + 1) * TILE] = mm_wide(pool, numer)
        exchange_ref[top:, p * TILE : (p + 1) * TILE] = mm_wide(pool, gtotal)


def give_out(info, near_ref, far_ref, z, part, values_s):
    core, plane = info[3], info[4]
    chunk = near_ref.shape[-2]
    for far, ref in enumerate((near_ref, far_ref)):
        for o in range(ref.shape[0]):
            at = ((o ^ plane) * 2 + (far ^ core)) * chunk
            ref[o, z, part] = values_s[pl.ds(pl.multiple_of(at, chunk), chunk), :]


def feed_grads_kernel(
    info, normed_ref, act_ref, grad_pre_ref, dy_ref, near_ref, far_ref, up_s, down_s
):
    line = info[5]
    for z in range(act_ref.shape[0]):
        up_s[...] = mm_tn(normed_ref[...], grad_pre_ref[z ^ line]).astype(BF16)
        give_out(info, near_ref, far_ref, z, 0, up_s)
        down_s[...] = mm_tn(act_ref[z ^ line], dy_ref[...]).astype(BF16)
        give_out(info, near_ref, far_ref, z, 1, down_s)


def attend_back_kernel(
    info,
    numer_ref,
    gtotal_ref,
    exchange_ref,
    q_ref,
    k_ref,
    v_ref,
    prob_ref,
    near_ref,
    far_ref,
    own_ref,
    gain_ref,
    grad_hidden_ref,
    grad_tokens_ref,
    grads_ref,
    vector_ref,
    b_qv_ref,
    pool_s,
    spread_s,
    numer_s,
    gtotal_s,
    gq_s,
    gk_s,
    gv_s,
    acc_s,
    full_s,
):
    rows = own_ref.shape[0]
    pairs = q_ref.shape[0]
    tiles = 2 * rows // TILE
    length, own, partner = info[0], info[1], info[2]
    assemble(info, near_ref, far_ref, full_s)
    pool_s[...] = pool_matrix(rows)
    spread_s[...] = spread_matrix(rows)
    live = (iota((rows, 1), 0) + own < length).astype(F32)
    counts, shift = coarse_counts(iota((rows, 1), 0), rows, length, own, partner)
    key_scale = SCALE / jnp.maximum(counts, 1.0)
    value_scale = 1.0 / jnp.maximum(counts, 1.0)
    query_scale = SCALE / lax.shift_left(jnp.ones_like(shift), shift).astype(F32)
    lane = iota((TILE, TILE), 1)
    second = (lane >= HEAD_SIZE).astype(F32)
    ones_second = second.astype(BF16)
    ones_first = (1.0 - second).astype(BF16)
    at_lane = lane & (HEAD_SIZE - 1)
    pick = (at_lane < 2).astype(F32)
    pick_first = (pick * (1.0 - second)).astype(BF16)
    pick_second = (pick * second).astype(BF16)
    is_low = at_lane == 1
    top = exchange_ref.shape[1] // 2
    acc_s[...] = jnp.zeros_like(acc_s)

    def one_pair(p, carry):
        pool = pool_s[...]
        numer = numer_ref[p]
        gtotal = gtotal_ref[p]
        numer_s[:rows, :] = numer.astype(BF16)
        numer_s[rows:, :] = mm_wide(pool, numer).astype(BF16)
        gtotal_s[:rows, :] = gtotal
        gtotal_s[rows:, :] = mm_wide(pool, gtotal)
        numer_s[2 * rows - top :, :] = exchange_ref[p, :top, :].astype(BF16)
        gtotal_s[2 * rows - top :, :] = exchange_ref[p, top:, :]

        def one_tile(i, inner):
            at = pl.ds(pl.multiple_of(i * TILE, TILE), TILE)
            q = q_ref[p, at, :]
            k = k_ref[p, at, :]
            v = v_ref[p, at, :]
            prob = prob_ref[p, i]
            numer = numer_s[at, :]
            gtotal = gtotal_s[at, :]
            high = gtotal.astype(BF16).astype(F32)
            mixed_total = jnp.where(is_low, gtotal - high, high).astype(BF16)
            left = jnp.concatenate([numer, mixed_total], axis=1)
            right = jnp.concatenate(
                [
                    jnp.concatenate([v * ones_first, pick_first], axis=1),
                    jnp.concatenate([v * ones_second, pick_second], axis=1),
                ],
                axis=0,
            )
            grad_prob = mm_nt(left, right)
            grad_score = (grad_prob * prob.astype(F32)).astype(BF16)
            keys = jnp.concatenate([k * ones_first, k * ones_second], axis=0)
            gq_s[at, :] = mm(grad_score, keys)
            gk = mm_tn(grad_score, q)
            gk_s[at, :] = jnp.where(lane < HEAD_SIZE, gk[:TILE], gk[TILE:])
            gv = mm_tn(prob, numer)
            gv_s[at, :] = jnp.where(lane < HEAD_SIZE, gv[:TILE], gv[TILE:])
            return inner

        lax.fori_loop(0, tiles, one_tile, 0, unroll=2)
        spread = spread_s[...]
        gq = gq_s[:rows, :] * SCALE + mm_wide(spread, gq_s[rows:, :] * query_scale)
        gk = (gk_s[:rows, :] * SCALE + mm_wide(spread, gk_s[rows:, :] * key_scale)) * live
        gv = (gv_s[:rows, :] + mm_wide(spread, gv_s[rows:, :] * value_scale)) * live
        gq, gk, gv = gq.astype(BF16), gk.astype(BF16), gv.astype(BF16)
        b_qv_ref[p, 0:1, :] = jnp.sum(gq.astype(F32), axis=0, keepdims=True)
        b_qv_ref[p, 1:2, :] = jnp.sum(gv.astype(F32), axis=0, keepdims=True)
        grads = jnp.concatenate([gq, gk, gv], axis=1)
        grads_ref[p] = grads
        acc_s[...] += mm_nt(grads, full_s[p, :, : 3 * TILE])
        return carry

    lax.fori_loop(0, pairs, one_pair, 0)
    unit, inverse = unit_rows(own_ref[...].astype(F32))
    grad_normed = acc_s[...]
    vector_ref[0:1, :] = jnp.sum(grad_normed * unit, axis=0, keepdims=True)
    vector_ref[1:2, :] = jnp.sum(grad_normed, axis=0, keepdims=True)
    grad_tokens_ref[...] = (
        grad_hidden_ref[...] + norm_back(grad_normed, unit, inverse, gain_ref[...])
    ).astype(BF16)


def attend_grads_kernel(
    info, normed_ref, grads_ref, grad_hidden_ref, mixed_ref, near_ref, far_ref, both_s
):
    line = info[5]
    for z in range(grads_ref.shape[0]):
        both_s[:, : 3 * TILE] = mm_tn(normed_ref[...], grads_ref[z ^ line]).astype(BF16)
        both_s[:, 3 * TILE :] = mm_tn(grad_hidden_ref[...], mixed_ref[z ^ line]).astype(BF16)
        give_out(info, near_ref, far_ref, z, 0, both_s)


def place_grads_kernel(info, near_ref, far_ref, *outs):
    core, plane = info[3], info[4]
    chunk = near_ref.shape[-2]
    for far, ref in enumerate((near_ref, far_ref)):
        for o in range(ref.shape[0]):
            at = ((o ^ plane) * 2 + (far ^ core)) * chunk
            at = pl.ds(pl.multiple_of(at, chunk), chunk)
            for part in range(ref.shape[1]):
                piece = ref[o, part].astype(F32)
                width = piece.shape[1] * ref.shape[1] // len(outs)
                for n in range(piece.shape[1] // width):
                    outs[part + n][at, :] = piece[:, n * width : (n + 1) * width]


def place_line_kernel(info, *refs):
    line = info[5]
    out_ref = refs[-1]
    for z, ref in enumerate(refs[:-1]):
        out_ref[z ^ line] = ref[...]


def place_dealt_kernel(info, *refs):
    line = info[5]
    out_ref = refs[-1]
    for z, ref in enumerate(refs[:-1]):
        for i in range(ref.shape[0]):
            for a in range(ref.shape[1]):
                for b in range(ref.shape[2]):
                    out_ref[a, b, i, z ^ line] = ref[i, a, b]


VMEM_SPEC = pl.BlockSpec(memory_space=pltpu.VMEM)
SMEM_SPEC = pl.BlockSpec(memory_space=pltpu.SMEM)


def call(kernel, outs, scalars, args, scratch=(), limit=48, flops=0):
    return pl.pallas_call(
        kernel,
        out_shape=[jax.ShapeDtypeStruct(shape, dtype) for shape, dtype in outs],
        in_specs=[SMEM_SPEC] * len(scalars) + [VMEM_SPEC] * len(args),
        out_specs=[VMEM_SPEC] * len(outs),
        scratch_shapes=list(scratch),
        compiler_params=pltpu.CompilerParams(vmem_limit_bytes=limit << 20),
        cost_estimate=pl.CostEstimate(flops=flops, transcendentals=0, bytes_accessed=8 << 20),
    )(*scalars, *args)


def exchange(pieces, axis):
    return lax.all_to_all(pieces, axis, 0, 0, tiled=True)


def swap(piece, axis, distance):
    size = lax.axis_size(axis)
    return lax.ppermute(piece, axis, [(i, i ^ distance) for i in range(size)])


def total_of(pieces):
    return functools.reduce(jnp.add, [piece.astype(F32) for piece in pieces]).astype(BF16)


def local(
    tokens,
    cotangent,
    lengths,
    dealing,
    ln1_gain,
    ln1_bias,
    w_query,
    b_query,
    w_key,
    w_value,
    b_value,
    w_out,
    b_out,
    ln2_gain,
    ln2_bias,
    w_up,
    b_up,
    w_down,
    b_down,
):
    seq_dev, length, width = tokens.shape
    dp = lax.axis_size("dp")
    nt = lax.axis_size("tensor")
    d = lax.axis_index("dp")
    t = lax.axis_index("tensor")
    rows = seq_dev * length // nt
    outer = dp // 2
    chunk = width // dp
    hid = w_up.shape[1]

    def line_pieces(piece):
        return [piece] + [swap(piece, "tensor", z) for z in range(1, nt)]

    def plane_pieces(piece):
        return [piece] + [swap(piece, "dp", 2 * o) for o in range(1, outer)]

    def gathered(piece):
        near = jnp.stack(plane_pieces(jnp.stack(line_pieces(piece))))
        return near, swap(near, "dp", 1)

    def own_rows(weight):
        return lax.dynamic_slice_in_dim(weight, d * chunk, chunk, axis=0)

    out_cols = lax.dynamic_slice_in_dim(w_out, d * chunk, chunk, axis=1).T
    attn_piece = jnp.concatenate(
        [own_rows(w_query), own_rows(w_key), own_rows(w_value), out_cols], axis=1
    )
    ffn_piece = jnp.stack([own_rows(w_up), own_rows(w_down)])
    bias_piece = jnp.concatenate([b_query, b_value, b_up]).reshape(-1, TILE)
    bias_piece = jnp.pad(bias_piece, ((0, -bias_piece.shape[0] % 8), (0, 0)))
    attn_w = gathered(attn_piece)
    biases = jnp.stack(line_pieces(bias_piece))
    ffn_w = gathered(ffn_piece)
    b_qv = biases[:, 0:2]
    b_ups = biases[:, 2 : 2 + hid // TILE].reshape(nt, 1, hid)

    halves = tokens.reshape(nt, rows, width)
    own = lax.dynamic_index_in_dim(halves, t, 0, keepdims=False)
    other = lax.dynamic_index_in_dim(halves, t ^ 1, 0, keepdims=False)
    dy = lax.dynamic_index_in_dim(cotangent.reshape(nt, rows, width), t, 0, keepdims=False)
    own_length = lengths[d * seq_dev + t // 2]
    own_base = (t % 2) * rows
    info = jnp.stack([own_length, own_base, rows - own_base, d % 2, d // 2, t]).astype(jnp.int32)
    row = lambda v: v.reshape(1, -1)
    top = rows >> level_shifts(rows)[-1]

    attn_full = pltpu.VMEM((nt, width, 4 * TILE), BF16)
    ffn_full = pltpu.VMEM((nt, 2, width, hid), BF16)

    normed_one, pooled = call(
        norm_one_kernel,
        [((rows, width), BF16), ((4 * top, width), BF16)],
        [info],
        [own, other, row(ln1_gain), row(ln1_bias)],
        limit=16,
    )
    mixed, mixed_wide, total, q, k, v, prob = call(
        attend_kernel,
        [((nt, rows, TILE), BF16), ((nt, rows, TILE), F32), ((nt, rows, TILE), F32)]
        + [((nt, 2 * rows, TILE), BF16)] * 3
        + [((nt, 2 * rows // TILE, TILE, 2 * TILE), BF16)],
        [info],
        [normed_one, pooled, *attn_w, b_qv],
        scratch=[
            pltpu.VMEM((rows, rows), BF16),
            pltpu.VMEM((rows, rows), BF16),
            pltpu.VMEM((2 * rows // TILE, 1, 2 * TILE), F32),
            pltpu.VMEM((2, TILE, 2 * TILE), F32),
            pltpu.VMEM((2 * rows, 2 * TILE), F32),
            attn_full,
        ],
        flops=10**10,
    )
    out, hidden, normed_two, act, slope = call(
        feed_kernel,
        [((rows, width), BF16), ((rows, width), F32), ((rows, width), BF16)]
        + [((nt, rows, hid), BF16)] * 2,
        [info],
        [own, mixed, *attn_w, *ffn_w]
        + [row(b_out), row(ln2_gain), row(ln2_bias), b_ups, row(b_down)],
        scratch=[attn_full, ffn_full],
        flops=10**10,
    )

    n_all = dp * nt
    piece = rows // n_all
    dealt = exchange(out.reshape(n_all, piece, width), ("dp", "tensor"))
    dealt = jnp.take(dealt.reshape(dp * seq_dev, -1, piece, width), dealing, axis=0)
    dealt = exchange(dealt.reshape(dp, seq_dev, -1, piece, width), "dp")
    (output,) = call(
        place_dealt_kernel,
        [((seq_dev, dealt.shape[2], dp, nt, piece, width), BF16)],
        [info],
        line_pieces(dealt),
        limit=16,
    )
    output = output.reshape(seq_dev, length, width)

    grad_pre, grad_hidden, grad_hidden_low, numer, gtotal, sent, vec_two, vec_up = call(
        feed_back_kernel,
        [
            ((nt, rows, hid), BF16),
            ((rows, width), F32),
            ((rows, width), BF16),
            ((nt, rows, TILE), F32),
            ((nt, rows, TILE), F32),
            ((2 * top, width), F32),
            ((4, width), F32),
            ((nt, 1, hid), F32),
        ],
        [info],
        [dy, *ffn_w, *attn_w, slope, hidden, row(ln2_gain), mixed_wide, total],
        scratch=[attn_full, ffn_full],
        flops=10**10,
    )
    swapped = swap(sent, "tensor", 1)
    swapped = swapped.reshape(2 * top, nt, TILE).transpose(1, 0, 2)
    ffn_grads = call(
        feed_grads_kernel,
        [((outer, nt, 2, chunk, hid), BF16)] * 2,
        [info],
        [normed_two, act, grad_pre, dy],
        scratch=[pltpu.VMEM((width, hid), BF16)] * 2,
        flops=10**10,
    )
    grad_low, qkv_grads, vec_one, vec_qv = call(
        attend_back_kernel,
        [
            ((rows, width), BF16),
            ((nt, rows, 3 * TILE), BF16),
            ((2, width), F32),
            ((nt, 2, TILE), F32),
        ],
        [info],
        [numer, gtotal, swapped, q, k, v, prob, *attn_w, own, row(ln1_gain), grad_hidden],
        scratch=[
            pltpu.VMEM((rows, rows), BF16),
            pltpu.VMEM((rows, rows), BF16),
            pltpu.VMEM((2 * rows, TILE), BF16),
            pltpu.VMEM((2 * rows, TILE), F32),
            pltpu.VMEM((2 * rows, TILE), F32),
            pltpu.VMEM((2 * rows, TILE), F32),
            pltpu.VMEM((2 * rows, TILE), F32),
            pltpu.VMEM((rows, width), F32),
            attn_full,
        ],
        flops=10**10,
    )
    (grad_tokens,) = call(
        place_line_kernel,
        [((nt, rows, width), BF16)],
        [info],
        line_pieces(grad_low),
        limit=16,
    )
    grad_tokens = grad_tokens.reshape(seq_dev, length, width)
    attn_grads = call(
        attend_grads_kernel,
        [((outer, nt, 1, chunk, 4 * TILE), BF16)] * 2,
        [info],
        [normed_one, qkv_grads, grad_hidden_low, mixed],
        scratch=[pltpu.VMEM((width, 4 * TILE), BF16)],
        flops=10**10,
    )

    def reduced(grads):
        near, far = grads
        far = swap(far, "dp", 1)
        pieces = [total_of([near[o], far[o]]) for o in range(outer)]
        pieces = [pieces[0]] + [swap(pieces[o], "dp", 2 * o) for o in range(1, outer)]
        pieces = [total_of([piece[z] for piece in pieces]) for z in range(nt)]
        pieces = [pieces[0]] + [swap(pieces[z], "tensor", z) for z in range(1, nt)]
        near = jnp.stack(plane_pieces(total_of(pieces)))
        return near, swap(near, "dp", 1)

    g_up, g_down = call(
        place_grads_kernel,
        [((width, hid), F32), ((hid, width), F32)],
        [info],
        reduced(ffn_grads),
        limit=16,
    )
    g_query, g_key, g_value, g_out = call(
        place_grads_kernel,
        [((width, TILE), F32)] * 4,
        [info],
        reduced(attn_grads),
        limit=16,
    )
    g_out = g_out.T

    vectors = jnp.concatenate(
        [vec_two, vec_up.reshape(nt, hid), vec_one, vec_qv.transpose(1, 0, 2).reshape(2, -1)]
    )
    vectors = vectors.astype(BF16)
    vectors = exchange(
        jnp.broadcast_to(vectors[None], (n_all,) + vectors.shape), ("dp", "tensor")
    )
    vectors = jnp.sum(vectors.astype(F32), axis=0)
    base = 4 + nt
    g_b_up = lax.dynamic_index_in_dim(vectors[4:base], t, 0, keepdims=False)
    g_b_q = lax.dynamic_index_in_dim(vectors[base + 2].reshape(nt, TILE), t, 0, keepdims=False)
    g_b_v = lax.dynamic_index_in_dim(vectors[base + 3].reshape(nt, TILE), t, 0, keepdims=False)
    return (
        output,
        grad_tokens,
        vectors[base],
        vectors[base + 1],
        g_query,
        g_b_q,
        g_key,
        g_value,
        g_b_v,
        g_out,
        vectors[3],
        vectors[0],
        vectors[1],
        g_up,
        g_b_up,
        g_down,
        vectors[2],
    )


def solution(mesh):
    placed = (
        P("dp", None, None),
        P("dp", None, None),
        P(),
        P(),
        P(),
        P(),
        P(None, "tensor"),
        P("tensor"),
        P(None, "tensor"),
        P(None, "tensor"),
        P("tensor"),
        P("tensor", None),
        P(),
        P(),
        P(),
        P(None, "tensor"),
        P("tensor"),
        P("tensor", None),
        P(),
    )
    return jax.shard_map(
        local,
        mesh=mesh,
        in_specs=placed,
        out_specs=(
            P("dp", None, None),
            P("dp", None, None),
            P(),
            P(),
            P(None, "tensor"),
            P("tensor"),
            P(None, "tensor"),
            P(None, "tensor"),
            P("tensor"),
            P("tensor", None),
            P(),
            P(),
            P(),
            P(None, "tensor"),
            P("tensor"),
            P("tensor", None),
            P(),
        ),
        check_vma=False,
    )
```

```python
import functools

import jax
import jax.numpy as jnp
from jax import lax
from jax.experimental import pallas as pl
from jax.experimental.pallas import tpu as pltpu
from jax.sharding import PartitionSpec as P

F32 = jnp.float32
BF16 = jnp.bfloat16
HEAD_SIZE = 64
BLOCK = 16
TILE = 128
EPS = 1e-05
INV_ROOT_TWO = 0.7071067811865476
INV_ROOT_TAU = 0.3989422804014327
SCALE = HEAD_SIZE ** (-0.5)


def mm(left, right):
    return lax.dot_general(left, right, (((1,), (0,)), ((), ())), preferred_element_type=F32)


def mm_nt(left, right):
    return lax.dot_general(left, right, (((1,), (1,)), ((), ())), preferred_element_type=F32)


def mm_tn(left, right):
    return lax.dot_general(left, right, (((0,), (0,)), ((), ())), preferred_element_type=F32)


def split_low(values):
    high = values.astype(BF16)
    return high, (values - high.astype(F32)).astype(BF16)


def mm_wide(left, values):
    high, low = split_low(values)
    return mm(left, high) + mm(left, low)


def iota(shape, axis):
    return lax.broadcasted_iota(jnp.int32, shape, axis)


def unit_rows(values):
    centred = values - jnp.mean(values, axis=-1, keepdims=True)
    inverse = lax.rsqrt(jnp.mean(centred * centred, axis=-1, keepdims=True) + EPS)
    return centred * inverse, inverse


def norm_back(grad, unit, inverse, gain):
    scaled = grad * gain
    return inverse * (
        scaled
        - jnp.mean(scaled, axis=-1, keepdims=True)
        - unit * jnp.mean(scaled * unit, axis=-1, keepdims=True)
    )


def level_shifts(rows):
    shifts = []
    shift = 1
    while (2 * rows) >> shift >= 2 * BLOCK:
        shifts.append(shift)
        shift += 1
    return shifts


def coarse_map(index, rows):
    shifts = level_shifts(rows)
    shift = jnp.zeros_like(index)
    start = jnp.zeros_like(index)
    offset = 0
    for s in shifts:
        here = index >= offset
        shift = jnp.where(here, s, shift)
        start = jnp.where(here, offset, start)
        offset += rows >> s
    other = index >= offset
    start = jnp.where(other, offset, start)
    return shift, index - start, other


def coarse_counts(index, rows, length, own, partner):
    shift, place, other = coarse_map(index, rows)
    base = jnp.where(other, partner, own)
    left = length - base - lax.shift_left(place, shift)
    return jnp.clip(left, 0, lax.shift_left(jnp.ones_like(shift), shift)).astype(F32), shift


def tile_map(index):
    shift = jnp.zeros_like(index)
    start = jnp.zeros_like(index)
    offset = 0
    for s in range(1, 6):
        here = index >= offset
        shift = jnp.where(here, s, shift)
        start = jnp.where(here, offset, start)
        offset += TILE >> s
    return shift, index - start, index >= offset - (TILE >> 5)


def pool_tile(odd):
    shift, place, last = tile_map(iota((TILE, TILE), 0))
    place = jnp.where(last, place - odd * (TILE >> 5), place)
    hit = lax.shift_right_logical(iota((TILE, TILE), 1), shift) == place
    return hit.astype(F32).astype(BF16)


def spread_tile(odd):
    shift, place, last = tile_map(iota((TILE, TILE), 1))
    place = jnp.where(last, place - odd * (TILE >> 5), place)
    hit = lax.shift_right_logical(iota((TILE, TILE), 0), shift) == place
    return hit.astype(F32).astype(BF16)


def level_places(rows, tile):
    found = []
    local, offset = 0, 0
    for s in level_shifts(rows):
        count = TILE >> s
        found.append((local, count, offset + tile * count))
        local += count
        offset += rows >> s
    return found[:-1], found[-1]


def put_pooled(to_s, rows, tile, pooled):
    levels, (local, count, at) = level_places(rows, tile)
    for start, number, place in levels:
        to_s[place : place + number, :] = pooled[start : start + number]
    at -= (tile % 2) * count
    if tile % 2:
        to_s[at : at + 2 * count, :] += pooled[local : local + 2 * count]
    else:
        to_s[at : at + 2 * count, :] = pooled[local : local + 2 * count]


def take_local(from_s, base, rows, tile):
    levels, (local, count, at) = level_places(rows, tile)
    at -= (tile % 2) * count
    parts = [from_s[base + place : base + place + number, :] for _, number, place in levels]
    return jnp.concatenate(parts + [from_s[base + at : base + at + 2 * count, :]], axis=0)


def stacked_low(values):
    return jnp.concatenate(split_low(values), axis=0)


def top_pool(rows):
    shift = level_shifts(rows)[-1]
    count = rows >> shift
    hit = lax.shift_right_logical(iota((count, rows), 1), shift) == iota((count, rows), 0)
    return hit.astype(F32).astype(BF16)


def head_ones():
    second = (iota((TILE, TILE), 1) >= HEAD_SIZE).astype(F32)
    return (1.0 - second).astype(BF16), second.astype(BF16)


def two_heads(values, first, second):
    return jnp.concatenate([values * first, values * second], axis=0)


def stand(values):
    return jnp.concatenate([values[:, :TILE], values[:, TILE:]], axis=0)


def assemble(info, near_ref, far_ref, to_ref, by_line=True):
    core, plane = info[3], info[4]
    line = info[5] if by_line else 0
    chunk = near_ref.shape[-2]
    for far, ref in enumerate((near_ref, far_ref)):
        for o in range(ref.shape[0]):
            at = ((o ^ plane) * 2 + (far ^ core)) * chunk
            at = pl.ds(pl.multiple_of(at, chunk), chunk)
            for z in range(ref.shape[1]):
                if len(ref.shape) == 5:
                    for part in range(ref.shape[2]):
                        to_ref[z ^ line, part, at, :] = ref[o, z, part]
                else:
                    to_ref[z ^ line, at, :] = ref[o, z]


def pack_kernel(info, q_ref, k_ref, v_ref, o_ref, up_ref, down_ref, bq_ref, bv_ref, bu_ref, attn_ref, ffn_ref, turn_s):
    chunk = q_ref.shape[0]
    attn_ref[:chunk, 0 * TILE : 1 * TILE] = q_ref[...]
    attn_ref[:chunk, 1 * TILE : 2 * TILE] = k_ref[...]
    attn_ref[:chunk, 2 * TILE : 3 * TILE] = v_ref[...]
    turn_s[...] = o_ref[...].T
    at = pl.ds(pl.multiple_of((info[4] * 2 + info[3]) * chunk, chunk), chunk)
    attn_ref[:chunk, 3 * TILE :] = turn_s[at, :]
    ffn_ref[0] = up_ref[...]
    ffn_ref[1] = down_ref[...]
    lanes = bu_ref.shape[1]
    blank = jnp.zeros((1, lanes - 2 * TILE), F32)
    rest = jnp.concatenate(
        [bu_ref[...], jnp.concatenate([bq_ref[...], bv_ref[...], blank], axis=1)], axis=0
    )
    rows = []
    for _ in range(3):
        part = rest.astype(BF16).astype(F32)
        rows.append(part)
        rest = rest - part
    rows.append(jnp.zeros((10, lanes), F32))
    attn_ref[chunk:, :] = jnp.concatenate(rows, axis=0).astype(BF16)


def bias_row(bias_ref, z, row):
    total = bias_ref[z, row : row + 1, :].astype(F32)
    for part in range(1, 3):
        at = 2 * part + row
        total = total + bias_ref[z, at : at + 1, :].astype(F32)
    return total


def norm_one_kernel(info, lengths, own_ref, other_ref, gain_ref, bias_ref, normed_ref, pooled_ref):
    rows = own_ref.shape[0]
    length, partner = lengths[info[0]], info[2]
    gain, bias = gain_ref[...], bias_ref[...]
    unit, _ = unit_rows(own_ref[...].astype(F32))
    normed_ref[...] = (unit * gain + bias).astype(BF16)
    unit, _ = unit_rows(other_ref[...].astype(F32))
    normed = (unit * gain + bias).astype(BF16)
    pool = top_pool(rows)
    count = pool.shape[0]
    live = (iota((1, rows), 1) + partner < length).astype(F32)
    pool_live = (pool.astype(F32) * live).astype(BF16)
    sums = mm(pool_live, normed)
    counts = jnp.sum(pool_live.astype(F32), axis=-1, keepdims=True)
    mean_live = sums / jnp.maximum(counts, 1.0)
    mean_all = mm(pool, normed) * (count / rows)
    high, low = split_low(mean_all)
    pooled_ref[0 * count : 1 * count, :] = high
    pooled_ref[1 * count : 2 * count, :] = low
    high, low = split_low(mean_live)
    pooled_ref[2 * count : 3 * count, :] = high
    pooled_ref[3 * count : 4 * count, :] = low


def attend_kernel(
    info,
    lengths,
    normed_ref,
    pooled_ref,
    near_ref,
    far_ref,
    bias_ref,
    mixed_ref,
    mixed_wide_ref,
    total_ref,
    q_ref,
    k_ref,
    v_ref,
    prob_ref,
    weight_s,
    mask_s,
    coarse_s,
    numer_s,
    full_s,
):
    rows = normed_ref.shape[0]
    pairs = q_ref.shape[0]
    tiles = 2 * rows // TILE
    half_tiles = rows // TILE
    length, own, partner = lengths[info[0]], info[1], info[2]
    line = info[5]
    assemble(info, near_ref, far_ref, full_s)
    pools = [pool_tile(odd) for odd in range(2)]
    spreads = [jnp.concatenate([spread_tile(odd)] * 2, axis=1) for odd in range(2)]
    lane = iota((1, 2 * TILE), 1) & (TILE - 1)
    for i in range(half_tiles):
        weight_s[i] = (lane + (own + i * TILE) < length).astype(F32)
        counts, _ = coarse_counts(lane + i * TILE, rows, length, own, partner)
        weight_s[half_tiles + i] = counts
    row_at = iota((TILE, 2 * TILE), 0)
    key_at = iota((TILE, 2 * TILE), 1) & (TILE - 1)
    pair_same = (row_at >> 5) == (key_at >> 5)
    apart = (row_at >> 4) != (key_at >> 4)
    mask_s[0] = pair_same.astype(F32)
    mask_s[1] = (pair_same & apart).astype(F32)
    live = (iota((rows, 1), 0) + own < length).astype(F32)
    counts, shift = coarse_counts(iota((rows, 1), 0), rows, length, own, partner)
    key_scale = 1.0 / jnp.maximum(counts, 1.0)
    query_scale = 1.0 / lax.shift_left(jnp.ones_like(shift), shift).astype(F32)
    top = pooled_ref.shape[0] // 4
    counts_other = counts[rows - top :]
    filled = counts_other / jnp.maximum(counts_other, 1.0)
    first, second = head_ones()

    def one_pair(p, carry):
        weight = full_s[p, :, : 3 * TILE]
        wide = mm(normed_ref[...], weight)
        biases = bias_row(bias_ref, p ^ line, 1)
        bq, bv = biases[:, :TILE], biases[:, TILE : 2 * TILE]
        query = (wide[:, :TILE] + bq).astype(BF16)
        key = (wide[:, TILE : 2 * TILE].astype(BF16).astype(F32) * live).astype(BF16)
        value = ((wide[:, 2 * TILE :] + bv).astype(BF16).astype(F32) * live).astype(BF16)
        extra = mm(pooled_ref[...], weight)
        q_other = extra[:top, :TILE] + extra[top : 2 * top, :TILE] + bq
        kv_other = extra[2 * top : 3 * top, TILE:] + extra[3 * top :, TILE:]
        k_other = kv_other[:, :TILE]
        v_other = kv_other[:, TILE:] + bv * filled
        q_ref[p, :rows, :] = query
        k_ref[p, :rows, :] = key
        v_ref[p, :rows, :] = value
        rows_all = jnp.concatenate([query, key, value], axis=1)
        for t in range(half_tiles):
            put_pooled(coarse_s, rows, t, mm(pools[t % 2], rows_all[t * TILE : (t + 1) * TILE]))
        q_ref[p, rows:, :] = (coarse_s[:, :TILE] * query_scale).astype(BF16)
        k_ref[p, rows:, :] = (coarse_s[:, TILE : 2 * TILE] * key_scale).astype(BF16)
        v_ref[p, rows:, :] = (coarse_s[:, 2 * TILE :] * key_scale).astype(BF16)
        q_ref[p, 2 * rows - top :, :] = q_other.astype(BF16)
        k_ref[p, 2 * rows - top :, :] = k_other.astype(BF16)
        v_ref[p, 2 * rows - top :, :] = v_other.astype(BF16)

        def one_tile(i, inner):
            at = pl.ds(pl.multiple_of(i * TILE, TILE), TILE)
            v = v_ref[p, at, :]
            score = mm_nt(q_ref[p, at, :], two_heads(k_ref[p, at, :], first, second)) * SCALE
            mask = mask_s[jnp.where(i >= half_tiles, 1, 0)]
            prob = jnp.where(mask > 0.0, jnp.exp(score) * weight_s[i], 0.0).astype(BF16)
            prob_ref[p, i] = prob
            values = jnp.concatenate(
                [
                    jnp.concatenate([v * first, first], axis=1),
                    jnp.concatenate([v * second, second], axis=1),
                ],
                axis=0,
            )
            numer_s[at, :] = mm(prob, values)
            return inner

        lax.fori_loop(0, tiles, one_tile, 0, unroll=4)
        for t in range(half_tiles):
            at = slice(t * TILE, (t + 1) * TILE)
            both = numer_s[at, :] + mm(
                spreads[t % 2], stacked_low(take_local(numer_s, rows, rows, t))
            )
            total = both[:, TILE:]
            mixed = both[:, :TILE] / total
            total_ref[p, at, :] = total
            mixed_wide_ref[p, at, :] = mixed
            mixed_ref[p, at, :] = mixed.astype(BF16)
        return carry

    lax.fori_loop(0, pairs, one_pair, 0)


def feed_kernel(
    info,
    own_ref,
    mixed_ref,
    near_ref,
    far_ref,
    ffn_near_ref,
    ffn_far_ref,
    b_out_ref,
    gain_ref,
    shift_ref,
    bias_ref,
    b_down_ref,
    hidden_ref,
    normed_ref,
    act_ref,
    slope_ref,
    *refs,
):
    *out_refs, result_s, full_s, ffn_s = refs
    pairs = mixed_ref.shape[0]
    line = info[5]
    assemble(info, near_ref, far_ref, full_s)
    assemble(info, ffn_near_ref, ffn_far_ref, ffn_s, by_line=False)
    hidden = own_ref[...].astype(F32) + b_out_ref[...]
    for p in range(pairs):
        hidden = hidden + mm_nt(mixed_ref[p], full_s[p, :, 3 * TILE :])
    hidden_ref[...] = hidden
    unit, _ = unit_rows(hidden)
    normed = (unit * gain_ref[...] + shift_ref[...]).astype(BF16)
    normed_ref[...] = normed
    result = hidden + b_down_ref[...]
    for z in range(pairs):
        pre = mm(normed, ffn_s[z, 0]) + bias_row(bias_ref, z ^ line, 0)
        half_erf = 0.5 + 0.5 * lax.erf(pre * INV_ROOT_TWO)
        act = (pre * half_erf).astype(BF16)
        act_ref[z] = act
        slope_ref[z] = (half_erf + pre * jnp.exp(-0.5 * pre * pre) * INV_ROOT_TAU).astype(BF16)
        result = result + mm(act, ffn_s[z, 1])
    result_s[...] = result
    chunk = out_refs[0].shape[0]
    for k, out_ref in enumerate(out_refs):
        at = ((info[4] * 2 + info[3]) ^ k) * chunk
        out_ref[...] = result_s[pl.ds(pl.multiple_of(at, chunk), chunk), :].astype(BF16)


def feed_back_kernel(
    info,
    dy_ref,
    ffn_near_ref,
    ffn_far_ref,
    near_ref,
    far_ref,
    slope_ref,
    hidden_ref,
    gain_ref,
    mixed_wide_ref,
    total_ref,
    grad_pre_ref,
    grad_hidden_ref,
    grad_hidden_low_ref,
    numer_ref,
    gtotal_ref,
    exchange_ref,
    vector_ref,
    b_up_ref,
    full_s,
    ffn_s,
):
    rows = dy_ref.shape[0]
    assemble(info, ffn_near_ref, ffn_far_ref, ffn_s, by_line=False)
    assemble(info, near_ref, far_ref, full_s)
    pairs = slope_ref.shape[0]
    dy = dy_ref[...]
    grad_normed = jnp.zeros((rows, dy.shape[1]), F32)
    for z in range(pairs):
        grad_act = mm_nt(dy, ffn_s[z, 1])
        grad_pre = (grad_act * slope_ref[z].astype(F32)).astype(BF16)
        grad_pre_ref[z] = grad_pre
        b_up_ref[z] = jnp.sum(grad_pre.astype(F32), axis=0, keepdims=True)
        grad_normed = grad_normed + mm_nt(grad_pre, ffn_s[z, 0])
    unit, inverse = unit_rows(hidden_ref[...])
    dy_wide = dy.astype(F32)
    vector_ref[0:1, :] = jnp.sum(grad_normed * unit, axis=0, keepdims=True)
    vector_ref[1:2, :] = jnp.sum(grad_normed, axis=0, keepdims=True)
    vector_ref[2:3, :] = jnp.sum(dy_wide, axis=0, keepdims=True)
    grad_hidden = dy_wide + norm_back(grad_normed, unit, inverse, gain_ref[...])
    vector_ref[3:4, :] = jnp.sum(grad_hidden, axis=0, keepdims=True)
    grad_hidden_ref[...] = grad_hidden
    low = grad_hidden.astype(BF16)
    grad_hidden_low_ref[...] = low
    pool = top_pool(rows)
    top = pool.shape[0]
    same = ((iota((TILE, TILE), 0) // HEAD_SIZE) == (iota((TILE, TILE), 1) // HEAD_SIZE)).astype(F32).astype(BF16)
    for p in range(pairs):
        grad_mixed = mm(low, full_s[p, :, 3 * TILE :]).astype(BF16).astype(F32)
        inv = 1.0 / total_ref[p]
        numer = grad_mixed * inv
        high, rest = split_low(grad_mixed * mixed_wide_ref[p])
        gtotal = -(mm(high, same) + mm(rest, same)) * inv
        numer_ref[p] = numer
        gtotal_ref[p] = gtotal
        exchange_ref[p, :top, :] = mm_wide(pool, numer)
        exchange_ref[p, top:, :] = mm_wide(pool, gtotal)


def give_out(info, near_ref, far_ref, z, part, values_s):
    core, plane = info[3], info[4]
    chunk = near_ref.shape[-2]
    for far, ref in enumerate((near_ref, far_ref)):
        for o in range(ref.shape[0]):
            at = ((o ^ plane) * 2 + (far ^ core)) * chunk
            ref[o, z, part] = values_s[pl.ds(pl.multiple_of(at, chunk), chunk), :]


def feed_grads_kernel(
    info, normed_ref, act_ref, grad_pre_ref, dy_ref, near_ref, far_ref, up_s, down_s
):
    line = info[5]
    for z in range(act_ref.shape[0]):
        up_s[...] = mm_tn(normed_ref[...], grad_pre_ref[z]).astype(BF16)
        give_out(info, near_ref, far_ref, z ^ line, 0, up_s)
        down_s[...] = mm_tn(act_ref[z], dy_ref[...]).astype(BF16)
        give_out(info, near_ref, far_ref, z ^ line, 1, down_s)


def attend_back_kernel(first_pair, *refs):
    final = first_pair > 0
    info, lengths, numer_ref, gtotal_ref, exchange_ref = refs[:5]
    q_ref, k_ref, v_ref, prob_ref, near_ref, far_ref = refs[5:11]
    refs = refs[11:]
    if final:
        before_ref, own_ref, gain_ref, grad_hidden_ref, grads_ref, b_qv_ref, grad_tokens_ref, vector_ref = refs[:8]
        refs = refs[8:]
    else:
        grads_ref, b_qv_ref, acc_ref = refs[:3]
        refs = refs[3:]
    coarse_s, left_s, grad_s, full_s = refs[:4]
    acc_s = refs[4] if final else acc_ref
    pairs, rows = numer_ref.shape[0], numer_ref.shape[1]
    tiles = 2 * rows // TILE
    half_tiles = rows // TILE
    length, own, partner = lengths[info[0]], info[1], info[2]
    assemble(info, near_ref, far_ref, full_s)
    pools = [jnp.concatenate([pool_tile(odd)] * 2, axis=1) for odd in range(2)]
    spreads = [jnp.concatenate([spread_tile(odd)] * 2, axis=1) for odd in range(2)]
    live = (iota((rows, 1), 0) + own < length).astype(F32)
    counts, shift = coarse_counts(iota((rows, 1), 0), rows, length, own, partner)
    value_scale = 1.0 / jnp.maximum(counts, 1.0)
    query_scale = 1.0 / lax.shift_left(jnp.ones_like(shift), shift).astype(F32)
    first, second = head_ones()
    at_lane = iota((1, TILE), 1) & (HEAD_SIZE - 1)
    pick = (at_lane < 2).astype(F32)
    pick_first = (pick * first.astype(F32)).astype(BF16)
    pick_second = (pick * second.astype(F32)).astype(BF16)
    is_low = at_lane == 1
    top = exchange_ref.shape[1] // 2

    def two_parts(gtotal):
        high = gtotal.astype(BF16).astype(F32)
        return jnp.where(is_low, gtotal - high, high).astype(BF16)

    def one_pair(p, carry):
        for t in range(half_tiles):
            at = slice(t * TILE, (t + 1) * TILE)
            numer, gtotal = numer_ref[p, at, :], gtotal_ref[p, at, :]
            left_s[at, :TILE] = numer.astype(BF16)
            left_s[at, TILE:] = two_parts(gtotal)
            both = jnp.concatenate([numer, gtotal], axis=1)
            put_pooled(coarse_s, rows, t, mm(pools[t % 2], stacked_low(both)))
        coarse_s[rows - top :, :TILE] = exchange_ref[p, :top, :]
        coarse_s[rows - top :, TILE:] = exchange_ref[p, top:, :]
        left_s[rows:, :TILE] = coarse_s[:, :TILE].astype(BF16)
        left_s[rows:, TILE:] = two_parts(coarse_s[:, TILE:])

        def one_tile(i, inner):
            at = pl.ds(pl.multiple_of(i * TILE, TILE), TILE)
            v = v_ref[p, at, :]
            prob = prob_ref[p, i]
            left = left_s[at, :]
            right = jnp.concatenate(
                [
                    jnp.concatenate([v * first, pick_first], axis=1),
                    jnp.concatenate([v * second, pick_second], axis=1),
                ],
                axis=0,
            )
            grad_score = (mm_nt(left, right) * prob.astype(F32)).astype(BF16)
            grad_s[at, :TILE] = mm(grad_score, two_heads(k_ref[p, at, :], first, second))
            grad_s[at, TILE : 2 * TILE] = mm_tn(
                stand(grad_score), two_heads(q_ref[p, at, :], first, second)
            )
            grad_s[at, 2 * TILE :] = mm_tn(stand(prob), two_heads(left[:, :TILE], first, second))
            return inner

        lax.fori_loop(0, tiles, one_tile, 0, unroll=4)
        grad_s[rows:, :TILE] *= query_scale
        grad_s[rows:, TILE:] *= value_scale
        for t in range(half_tiles):
            at = slice(t * TILE, (t + 1) * TILE)
            fine = grad_s[at, :] + mm(
                spreads[t % 2], stacked_low(take_local(grad_s, rows, rows, t))
            )
            gq = (fine[:, :TILE] * SCALE).astype(BF16)
            gk = (fine[:, TILE : 2 * TILE] * (SCALE * live[at])).astype(BF16)
            gv = (fine[:, 2 * TILE :] * live[at]).astype(BF16)
            grads_ref[p, at, :] = jnp.concatenate([gq, gk, gv], axis=1)
        sums = jnp.sum(grads_ref[p].astype(F32), axis=0, keepdims=True)
        b_qv_ref[p, 0:1, :] = sums[:, :TILE]
        b_qv_ref[p, 1:2, :] = sums[:, 2 * TILE :]
        acc_s[...] += mm_nt(grads_ref[p], full_s[first_pair + p, :, : 3 * TILE])
        return carry

    acc_s[...] = before_ref[...] if final else jnp.zeros_like(acc_s)
    lax.fori_loop(0, pairs, one_pair, 0)
    if final:
        unit, inverse = unit_rows(own_ref[...].astype(F32))
        grad_normed = acc_s[...]
        vector_ref[0:1, :] = jnp.sum(grad_normed * unit, axis=0, keepdims=True)
        vector_ref[1:2, :] = jnp.sum(grad_normed, axis=0, keepdims=True)
        grad_tokens_ref[...] = (
            grad_hidden_ref[...] + norm_back(grad_normed, unit, inverse, gain_ref[...])
        ).astype(BF16)


def attend_grads_kernel(
    info,
    normed_ref,
    low_ref,
    high_ref,
    grad_hidden_ref,
    mixed_ref,
    vec_two_ref,
    vec_up_ref,
    vec_one_ref,
    qv_low_ref,
    qv_high_ref,
    near_ref,
    far_ref,
    both_s,
):
    core, plane, line = info[3], info[4], info[5]
    half, pairs = low_ref.shape[0], mixed_ref.shape[0]
    dp = 2 * near_ref.shape[0]
    chunk = both_s.shape[0] // dp
    for z in range(pairs):
        grads = low_ref[z] if z < half else high_ref[z - half]
        both_s[:, : 3 * TILE] = mm_tn(normed_ref[...], grads).astype(BF16)
        both_s[:, 3 * TILE :] = mm_tn(grad_hidden_ref[...], mixed_ref[z]).astype(BF16)
        for far, ref in enumerate((near_ref, far_ref)):
            for o in range(ref.shape[0]):
                at = ((o ^ plane) * 2 + (far ^ core)) * chunk
                at = pl.ds(pl.multiple_of(at, chunk), chunk)
                to = pl.ds(pl.multiple_of((z ^ line) * chunk, chunk), chunk)
                ref[o, to, :] = both_s[at, :]
    vectors = [vec_two_ref[...]] + [vec_up_ref[z] for z in range(pairs)] + [vec_one_ref[...]]
    for row in range(2):
        parts = [ref[p, row : row + 1, :] for ref in (qv_low_ref, qv_high_ref) for p in range(half)]
        vectors.append(jnp.concatenate(parts, axis=1))
    vectors = jnp.concatenate(vectors, axis=0)
    blank = jnp.zeros((near_ref.shape[1] - pairs * chunk - vectors.shape[0], vectors.shape[1]), F32)
    vectors = jnp.concatenate([vectors, blank], axis=0).astype(BF16)
    for ref in (near_ref, far_ref):
        for o in range(ref.shape[0]):
            ref[o, pairs * chunk :, :] = vectors


def place_grads_kernel(info, near_ref, far_ref, up_ref, down_ref, q_ref, k_ref, v_ref, o_ref, turn_s):
    core, plane = info[3], info[4]
    chunk = near_ref.shape[-2]
    for far, ref in enumerate((near_ref, far_ref)):
        for o in range(ref.shape[0]):
            at = ((o ^ plane) * 2 + (far ^ core)) * chunk
            at = pl.ds(pl.multiple_of(at, chunk), chunk)
            up_ref[at, :] = ref[o, 0].astype(F32)
            down_ref[at, :] = ref[o, 1].astype(F32)
            rest = ref[o, 2].astype(F32)
            q_ref[at, :] = rest[:, :TILE]
            k_ref[at, :] = rest[:, TILE : 2 * TILE]
            v_ref[at, :] = rest[:, 2 * TILE : 3 * TILE]
            turn_s[at, :] = rest[:, 3 * TILE :]
    o_ref[...] = turn_s[...].T


def gather_line(line, refs, to_ref):
    own, one, two, three, passed = refs
    middle = (line == 1) | (line == 2)
    to_ref[line] = own[...]
    to_ref[line ^ 1] = one[...]
    to_ref[line ^ 2] = two[...]

    @pl.when(middle)
    def _():
        to_ref[line ^ 3] = three[...]

    @pl.when(jnp.logical_not(middle))
    def _():
        to_ref[line ^ 3] = passed[...]


def place_rows_kernel(info, *refs):
    gather_line(info[5], refs[:-1], refs[-1])


def deal_kernel(info, dealing, *refs):
    *pieces, out_ref, all_s = refs
    gather_line(info[5], pieces, all_s)
    own = info[4] * 2 + info[3]
    for i in range(out_ref.shape[0]):
        for slot in range(out_ref.shape[1]):
            seq = dealing[i * out_ref.shape[1] + slot]
            for half in range(out_ref.shape[2]):
                out_ref[i, slot, half] = all_s[(seq & 1) * 2 + half, (seq >> 1) ^ own]


def settle_kernel(pieces_ref, out_ref):
    dps, slots, halves = pieces_ref.shape[:3]
    for i in range(dps):
        for slot in range(slots):
            for half in range(halves):
                out_ref[slot, half, i] = pieces_ref[i, slot, half]


VMEM_SPEC = pl.BlockSpec(memory_space=pltpu.VMEM)
SMEM_SPEC = pl.BlockSpec(memory_space=pltpu.SMEM)


def part_of(array, half):
    block = (array.shape[0] // 2,) + array.shape[1:]
    return array, pl.BlockSpec(
        block, lambda i: (half,) + (0,) * (len(block) - 1), pipeline_mode=pl.Buffered(1)
    )


def call(kernel, outs, scalars, args, scratch=(), limit=16, long=False):
    args = [arg if isinstance(arg, tuple) else (arg, VMEM_SPEC) for arg in args]
    grid = (1,) if any(spec is not VMEM_SPEC for _, spec in args) else ()
    return pl.pallas_call(
        kernel,
        out_shape=[jax.ShapeDtypeStruct(shape, dtype) for shape, dtype in outs],
        grid=grid,
        in_specs=[SMEM_SPEC] * len(scalars) + [spec for _, spec in args],
        out_specs=[VMEM_SPEC] * len(outs),
        scratch_shapes=list(scratch),
        compiler_params=pltpu.CompilerParams(vmem_limit_bytes=limit << 20),
        cost_estimate=pl.CostEstimate(
            flops=10**10 if long else 1, transcendentals=0, bytes_accessed=1
        ),
    )(*scalars, *[arg for arg, _ in args])


def exchange(pieces, axis, groups=None):
    return lax.all_to_all(pieces, axis, 0, 0, tiled=True, axis_index_groups=groups)


def gather(piece, axis, count):
    return exchange(jnp.broadcast_to(piece[None], (count,) + piece.shape), axis)


def swap(piece, axis, distance):
    size = lax.axis_size(axis)
    return lax.ppermute(piece, axis, [(i, i ^ distance) for i in range(size)])


def after(value, *others):
    return lax.optimization_barrier((value, *others))[0]


def total_of(pieces):
    return functools.reduce(jnp.add, [piece.astype(F32) for piece in pieces]).astype(BF16)


def local(
    tokens,
    cotangent,
    lengths,
    dealing,
    ln1_gain,
    ln1_bias,
    w_query,
    b_query,
    w_key,
    w_value,
    b_value,
    w_out,
    b_out,
    ln2_gain,
    ln2_bias,
    w_up,
    b_up,
    w_down,
    b_down,
):
    seq_dev, length, width = tokens.shape
    dp = lax.axis_size("dp")
    nt = lax.axis_size("tensor")
    d = lax.axis_index("dp")
    t = lax.axis_index("tensor")
    rows = seq_dev * length // nt
    outer = dp // 2
    planes = [[2 * o + c for o in range(outer)] for c in range(2)]
    chunk = width // dp
    hid = w_up.shape[1]

    def near_line(piece):
        return [piece] + [swap(piece, "tensor", z) for z in range(1, nt)]

    def line_first(piece):
        return [piece, swap(piece, "tensor", 1), swap(piece, "tensor", 2)]

    def line_second(pieces):
        piece, one, two = pieces
        three = lax.ppermute(after(piece, two), "tensor", [(1, 2), (2, 1)])
        passed = lax.ppermute(two, "tensor", [(1, 0), (2, 3)])
        return [piece, one, two, three, passed]

    def plane_pieces(piece):
        return [piece] + [swap(piece, "dp", 2 * o) for o in range(1, outer)]

    own_base = (t % 2) * rows
    info = jnp.stack([d * seq_dev + t // 2, own_base, rows - own_base, d % 2, d // 2, t])
    row = lambda v: v.reshape(1, -1)

    slice_spec = lambda lanes: pl.BlockSpec((chunk, lanes), lambda i, info: (info[4] * 2 + info[3], 0))
    whole_spec = lambda shape: pl.BlockSpec(shape, lambda i, info: (0,) * len(shape))
    attn_piece, ffn_piece = pl.pallas_call(
        pack_kernel,
        out_shape=[
            jax.ShapeDtypeStruct((chunk + 16, 4 * TILE), BF16),
            jax.ShapeDtypeStruct((2, chunk, hid), BF16),
        ],
        grid_spec=pltpu.PrefetchScalarGridSpec(
            num_scalar_prefetch=1,
            grid=(1,),
            in_specs=[slice_spec(TILE)] * 3
            + [whole_spec((TILE, width)), slice_spec(hid), slice_spec(width)]
            + [whole_spec((1, TILE)), whole_spec((1, TILE)), whole_spec((1, hid))],
            out_specs=[whole_spec((chunk + 16, 4 * TILE)), whole_spec((2, chunk, hid))],
            scratch_shapes=[pltpu.VMEM((width, TILE), BF16)],
        ),
    )(info, w_query, w_key, w_value, w_out, w_up, w_down, row(b_query), row(b_value), row(b_up))
    halves = tokens.reshape(nt, rows, width)
    own = lax.dynamic_index_in_dim(halves, t, 0, keepdims=False)
    other = lax.dynamic_index_in_dim(halves, t ^ 1, 0, keepdims=False)
    dy = lax.dynamic_index_in_dim(cotangent.reshape(nt, rows, width), t, 0, keepdims=False)
    top = rows >> level_shifts(rows)[-1]

    attn_full = pltpu.VMEM((nt, width, 4 * TILE), BF16)
    ffn_full = pltpu.VMEM((nt, 2, width, hid), BF16)

    normed_one, pooled = call(
        norm_one_kernel,
        [((rows, width), BF16), ((4 * top, width), BF16)],
        [info, lengths],
        [own, other, row(ln1_gain), row(ln1_bias)],
    )
    attn_line = near_line(attn_piece)
    normed_one, *attn_line = lax.optimization_barrier((normed_one, *attn_line))
    attn_near = jnp.stack(plane_pieces(jnp.stack([piece[:chunk] for piece in attn_line])))
    biases = jnp.stack([piece[chunk:] for piece in attn_line])
    ffn_line = gather(ffn_piece, "tensor", nt)
    attn_w = attn_near, swap(attn_near, "dp", 1)
    ffn_pieces = plane_pieces(after(ffn_line, attn_near))
    normed_one = after(normed_one, ffn_line)

    mixed, mixed_wide, total, q, k, v, prob = call(
        attend_kernel,
        [((nt, rows, TILE), BF16), ((nt, rows, TILE), F32), ((nt, rows, TILE), F32)]
        + [((nt, 2 * rows, TILE), BF16)] * 3
        + [((nt, 2 * rows // TILE, TILE, 2 * TILE), BF16)],
        [info, lengths],
        [normed_one, pooled, *attn_w, biases],
        scratch=[
            pltpu.VMEM((2 * rows // TILE, 1, 2 * TILE), F32),
            pltpu.VMEM((2, TILE, 2 * TILE), F32),
            pltpu.VMEM((rows, 3 * TILE), F32),
            pltpu.VMEM((2 * rows, 2 * TILE), F32),
            attn_full,
        ],
        limit=24,
        long=True,
    )
    ffn_near = jnp.stack([after(each, mixed) for each in ffn_pieces])
    ffn_w = ffn_near, swap(ffn_near, "dp", 1)
    piece = rows // dp
    hidden, normed_two, act, slope, *outs = call(
        feed_kernel,
        [((rows, width), F32), ((rows, width), BF16)]
        + [((nt, rows, hid), BF16)] * 2
        + [((piece, width), BF16)] * dp,
        [info],
        [own, mixed, *attn_w, *ffn_w]
        + [row(b_out), row(ln2_gain), row(ln2_bias), biases, row(b_down)],
        scratch=[pltpu.VMEM((rows, width), F32), attn_full, ffn_full],
        limit=28,
    )
    chunks = [outs[0]] + [swap(outs[k], "dp", k) for k in range(1, dp)]

    grad_pre, grad_hidden, grad_hidden_low, numer, gtotal, sent, vec_two, vec_up = call(
        feed_back_kernel,
        [
            ((nt, rows, hid), BF16),
            ((rows, width), F32),
            ((rows, width), BF16),
            ((nt, rows, TILE), F32),
            ((nt, rows, TILE), F32),
            ((nt, 2 * top, TILE), F32),
            ((4, width), F32),
            ((nt, 1, hid), F32),
        ],
        [info],
        [dy, *ffn_w, *attn_w, slope, hidden, row(ln2_gain), mixed_wide, total],
        scratch=[attn_full, ffn_full],
        limit=28,
    )
    swapped = swap(sent, "tensor", 1)
    ffn_grads = call(
        feed_grads_kernel,
        [((outer, nt, 2, chunk, hid), BF16)] * 2,
        [info],
        [normed_two, act, grad_pre, dy],
        scratch=[pltpu.VMEM((width, hid), BF16)] * 2,
    )
    ffn_far = swap(ffn_grads[1], "dp", 1)

    back_scratch = [
        pltpu.VMEM((rows, 2 * TILE), F32),
        pltpu.VMEM((2 * rows, 2 * TILE), BF16),
        pltpu.VMEM((2 * rows, 3 * TILE), F32),
        attn_full,
    ]

    def back_args(half):
        return [part_of(each, half) for each in (numer, gtotal, swapped, q, k, v, prob)] + [*attn_w]

    def core_sums(near, far):
        return [total_of([near[o], far[o]]) for o in range(outer)]

    def plane_parts(pieces):
        return [pieces[0]] + [swap(pieces[o], "dp", 2 * o) for o in range(1, outer)]

    chunks = line_first(jnp.stack(chunks))
    gtotal, chunks[0] = lax.optimization_barrier((gtotal, chunks[0]))
    grads_low, qv_low, acc = call(
        functools.partial(attend_back_kernel, 0),
        [((nt // 2, rows, 3 * TILE), BF16), ((nt // 2, 2, TILE), F32), ((rows, width), F32)],
        [info, lengths],
        back_args(0),
        scratch=back_scratch,
        limit=20,
        long=True,
    )
    ffn_parts = core_sums(after(ffn_grads[0], acc), ffn_far)
    acc, chunks[1], chunks[2], *ffn_parts = lax.optimization_barrier(
        (acc, chunks[1], chunks[2], *ffn_parts)
    )
    chunks = line_second(chunks)
    ffn_parts = plane_parts(ffn_parts)
    grads_high, qv_high, grad_low, vec_one = call(
        functools.partial(attend_back_kernel, nt // 2),
        [
            ((nt // 2, rows, 3 * TILE), BF16),
            ((nt // 2, 2, TILE), F32),
            ((rows, width), BF16),
            ((2, width), F32),
        ],
        [info, lengths],
        back_args(1) + [acc, own, row(ln1_gain), grad_hidden],
        scratch=back_scratch + [pltpu.VMEM((rows, width), F32)],
        limit=20,
        long=True,
    )
    grad_low, grad_hidden_low = lax.optimization_barrier((grad_low, grad_hidden_low))
    row_pieces = line_first(grad_low)
    attn_near, attn_far = call(
        attend_grads_kernel,
        [((outer, nt * chunk + 16, 4 * TILE), BF16)] * 2,
        [info],
        [normed_one, grads_low, grads_high, grad_hidden_low, mixed]
        + [vec_two, vec_up, vec_one, qv_low, qv_high],
        scratch=[pltpu.VMEM((width, 4 * TILE), BF16)],
    )
    chunks[3], chunks[4], attn_near = lax.optimization_barrier((chunks[3], chunks[4], attn_near))
    (dealt,) = call(
        deal_kernel,
        [((dp, seq_dev, nt // seq_dev, piece, width), BF16)],
        [info, dealing],
        chunks,
        scratch=[pltpu.VMEM((nt, dp, piece, width), BF16)],
    )
    dealt = exchange(dealt, "dp")
    attn_parts = core_sums(attn_near, swap(attn_far, "dp", 1))
    attn_parts = total_of(plane_parts(attn_parts))
    attn_parts, *row_pieces = lax.optimization_barrier((attn_parts, *row_pieces))
    ffn_parts = total_of(ffn_parts)
    grads = [
        jnp.concatenate(
            [ffn_parts[z].reshape(2 * chunk, hid), attn_parts[z * chunk : (z + 1) * chunk]]
            + [attn_parts[nt * chunk :]]
        )
        for z in range(nt)
    ]
    grads = total_of([grads[0]] + [swap(grads[z], "tensor", z) for z in range(1, nt)])
    vectors = grads[3 * chunk :].astype(F32)
    row_pieces = line_second(row_pieces)
    near = jnp.stack(plane_pieces(grads[: 3 * chunk].reshape(3, chunk, width)))
    grads = near, swap(near, "dp", 1)
    g_up, g_down, g_query, g_key, g_value, g_out = call(
        place_grads_kernel,
        [((width, hid), F32), ((hid, width), F32)]
        + [((width, TILE), F32)] * 3
        + [((TILE, width), F32)],
        [info],
        grads,
        scratch=[pltpu.VMEM((width, TILE), F32)],
    )
    (grad_tokens,) = call(
        place_rows_kernel, [((nt, rows, width), BF16)], [info], row_pieces
    )
    grad_tokens = grad_tokens.reshape(seq_dev, length, width)
    (output,) = call(
        settle_kernel, [((seq_dev, nt // seq_dev, dp, piece, width), BF16)], [], [dealt]
    )
    output = output.reshape(seq_dev, length, width)
    base = 4 + nt
    g_b_up = lax.dynamic_index_in_dim(vectors[4:base], t, 0, keepdims=False)
    g_b_q = lax.dynamic_index_in_dim(vectors[base + 2].reshape(nt, TILE), t, 0, keepdims=False)
    g_b_v = lax.dynamic_index_in_dim(vectors[base + 3].reshape(nt, TILE), t, 0, keepdims=False)
    return (
        output,
        grad_tokens,
        vectors[base],
        vectors[base + 1],
        g_query,
        g_b_q,
        g_key,
        g_value,
        g_b_v,
        g_out,
        vectors[3],
        vectors[0],
        vectors[1],
        g_up,
        g_b_up,
        g_down,
        vectors[2],
    )


def solution(mesh):
    placed = (
        P("dp", None, None),
        P("dp", None, None),
        P(),
        P(),
        P(),
        P(),
        P(None, "tensor"),
        P("tensor"),
        P(None, "tensor"),
        P(None, "tensor"),
        P("tensor"),
        P("tensor", None),
        P(),
        P(),
        P(),
        P(None, "tensor"),
        P("tensor"),
        P("tensor", None),
        P(),
    )
    return jax.shard_map(
        local,
        mesh=mesh,
        in_specs=placed,
        out_specs=(
            P("dp", None, None),
            P("dp", None, None),
            P(),
            P(),
            P(None, "tensor"),
            P("tensor"),
            P(None, "tensor"),
            P(None, "tensor"),
            P("tensor"),
            P("tensor", None),
            P(),
            P(),
            P(),
            P(None, "tensor"),
            P("tensor"),
            P("tensor", None),
            P(),
        ),
        check_vma=False,
    )
```

```python
import functools

import jax
import jax.numpy as jnp
from jax import lax
from jax.experimental import pallas as pl
from jax.experimental.pallas import tpu as pltpu
from jax.sharding import PartitionSpec as P

F32 = jnp.float32
BF16 = jnp.bfloat16
HEAD_SIZE = 64
BLOCK = 16
TILE = 128
EPS = 1e-05
INV_ROOT_TWO = 0.7071067811865476
INV_ROOT_TAU = 0.3989422804014327
SCALE = HEAD_SIZE ** (-0.5)


def mm(left, right):
    return lax.dot_general(left, right, (((1,), (0,)), ((), ())), preferred_element_type=F32)


def mm_nt(left, right):
    return lax.dot_general(left, right, (((1,), (1,)), ((), ())), preferred_element_type=F32)


def mm_tn(left, right):
    return lax.dot_general(left, right, (((0,), (0,)), ((), ())), preferred_element_type=F32)


def split_low(values):
    high = values.astype(BF16)
    return high, (values - high.astype(F32)).astype(BF16)


def mm_wide(left, values):
    high, low = split_low(values)
    return mm(left, high) + mm(left, low)


def iota(shape, axis):
    return lax.broadcasted_iota(jnp.int32, shape, axis)


def unit_rows(values):
    centred = values - jnp.mean(values, axis=-1, keepdims=True)
    inverse = lax.rsqrt(jnp.mean(centred * centred, axis=-1, keepdims=True) + EPS)
    return centred * inverse, inverse


def norm_back(grad, unit, inverse, gain):
    scaled = grad * gain
    return inverse * (
        scaled
        - jnp.mean(scaled, axis=-1, keepdims=True)
        - unit * jnp.mean(scaled * unit, axis=-1, keepdims=True)
    )


def level_shifts(rows):
    shifts = []
    shift = 1
    while (2 * rows) >> shift >= 2 * BLOCK:
        shifts.append(shift)
        shift += 1
    return shifts


def coarse_map(index, rows):
    shifts = level_shifts(rows)
    shift = jnp.zeros_like(index)
    start = jnp.zeros_like(index)
    offset = 0
    for s in shifts:
        here = index >= offset
        shift = jnp.where(here, s, shift)
        start = jnp.where(here, offset, start)
        offset += rows >> s
    other = index >= offset
    start = jnp.where(other, offset, start)
    return shift, index - start, other


def coarse_counts(index, rows, length, own, partner):
    shift, place, other = coarse_map(index, rows)
    base = jnp.where(other, partner, own)
    left = length - base - lax.shift_left(place, shift)
    return jnp.clip(left, 0, lax.shift_left(jnp.ones_like(shift), shift)).astype(F32), shift


def tile_map(index):
    shift = jnp.zeros_like(index)
    start = jnp.zeros_like(index)
    offset = 0
    for s in range(1, 6):
        here = index >= offset
        shift = jnp.where(here, s, shift)
        start = jnp.where(here, offset, start)
        offset += TILE >> s
    return shift, index - start, index >= offset - (TILE >> 5)


def pool_tile(odd):
    shift, place, last = tile_map(iota((TILE, TILE), 0))
    place = jnp.where(last, place - odd * (TILE >> 5), place)
    hit = lax.shift_right_logical(iota((TILE, TILE), 1), shift) == place
    return hit.astype(F32).astype(BF16)


def spread_tile(odd):
    shift, place, last = tile_map(iota((TILE, TILE), 1))
    place = jnp.where(last, place - odd * (TILE >> 5), place)
    hit = lax.shift_right_logical(iota((TILE, TILE), 0), shift) == place
    return hit.astype(F32).astype(BF16)


def level_places(rows, tile):
    found = []
    local, offset = 0, 0
    for s in level_shifts(rows):
        count = TILE >> s
        found.append((local, count, offset + tile * count))
        local += count
        offset += rows >> s
    return found[:-1], found[-1]


def put_pooled(to_s, rows, tile, pooled):
    levels, (local, count, at) = level_places(rows, tile)
    for start, number, place in levels:
        to_s[place : place + number, :] = pooled[start : start + number]
    at -= (tile % 2) * count
    if tile % 2:
        to_s[at : at + 2 * count, :] += pooled[local : local + 2 * count]
    else:
        to_s[at : at + 2 * count, :] = pooled[local : local + 2 * count]


def take_local(from_s, base, rows, tile):
    levels, (local, count, at) = level_places(rows, tile)
    at -= (tile % 2) * count
    parts = [from_s[base + place : base + place + number, :] for _, number, place in levels]
    return jnp.concatenate(parts + [from_s[base + at : base + at + 2 * count, :]], axis=0)


def stacked_low(values):
    return jnp.concatenate(split_low(values), axis=0)


def top_pool(rows):
    shift = level_shifts(rows)[-1]
    count = rows >> shift
    hit = lax.shift_right_logical(iota((count, rows), 1), shift) == iota((count, rows), 0)
    return hit.astype(F32).astype(BF16)


def head_ones():
    second = (iota((TILE, TILE), 1) >= HEAD_SIZE).astype(F32)
    return (1.0 - second).astype(BF16), second.astype(BF16)


def two_heads(values, first, second):
    return jnp.concatenate([values * first, values * second], axis=0)


def stand(values):
    return jnp.concatenate([values[:, :TILE], values[:, TILE:]], axis=0)


def assemble(info, near_ref, far_ref, to_ref, by_line=True):
    core, plane = info[3], info[4]
    line = info[5] if by_line else 0
    chunk = near_ref.shape[-2]
    for far, ref in enumerate((near_ref, far_ref)):
        for o in range(ref.shape[0]):
            at = ((o ^ plane) * 2 + (far ^ core)) * chunk
            at = pl.ds(pl.multiple_of(at, chunk), chunk)
            for z in range(ref.shape[1]):
                if len(ref.shape) == 5:
                    for part in range(ref.shape[2]):
                        to_ref[z ^ line, part, at, :] = ref[o, z, part]
                else:
                    to_ref[z ^ line, at, :] = ref[o, z]


def pack_kernel(info, q_ref, k_ref, v_ref, o_ref, up_ref, down_ref, bq_ref, bv_ref, bu_ref, attn_ref, ffn_ref, turn_s):
    chunk = q_ref.shape[0]
    attn_ref[:chunk, 0 * TILE : 1 * TILE] = q_ref[...]
    attn_ref[:chunk, 1 * TILE : 2 * TILE] = k_ref[...]
    attn_ref[:chunk, 2 * TILE : 3 * TILE] = v_ref[...]
    turn_s[...] = o_ref[...].T
    at = pl.ds(pl.multiple_of((info[4] * 2 + info[3]) * chunk, chunk), chunk)
    attn_ref[:chunk, 3 * TILE :] = turn_s[at, :]
    ffn_ref[0] = up_ref[...]
    ffn_ref[1] = down_ref[...]
    lanes = bu_ref.shape[1]
    blank = jnp.zeros((1, lanes - 2 * TILE), F32)
    rest = jnp.concatenate(
        [bu_ref[...], jnp.concatenate([bq_ref[...], bv_ref[...], blank], axis=1)], axis=0
    )
    rows = []
    for _ in range(3):
        part = rest.astype(BF16).astype(F32)
        rows.append(part)
        rest = rest - part
    rows.append(jnp.zeros((10, lanes), F32))
    attn_ref[chunk:, :] = jnp.concatenate(rows, axis=0).astype(BF16)


def bias_row(bias_ref, z, row):
    total = bias_ref[z, row : row + 1, :].astype(F32)
    for part in range(1, 3):
        at = 2 * part + row
        total = total + bias_ref[z, at : at + 1, :].astype(F32)
    return total


def norm_one_kernel(info, lengths, own_ref, other_ref, gain_ref, bias_ref, normed_ref, pooled_ref):
    rows = own_ref.shape[0]
    length, partner = lengths[info[0]], info[2]
    gain, bias = gain_ref[...], bias_ref[...]
    unit, _ = unit_rows(own_ref[...].astype(F32))
    normed_ref[...] = (unit * gain + bias).astype(BF16)
    unit, _ = unit_rows(other_ref[...].astype(F32))
    normed = (unit * gain + bias).astype(BF16)
    pool = top_pool(rows)
    count = pool.shape[0]
    live = (iota((1, rows), 1) + partner < length).astype(F32)
    pool_live = (pool.astype(F32) * live).astype(BF16)
    sums = mm(pool_live, normed)
    counts = jnp.sum(pool_live.astype(F32), axis=-1, keepdims=True)
    mean_live = sums / jnp.maximum(counts, 1.0)
    mean_all = mm(pool, normed) * (count / rows)
    high, low = split_low(mean_all)
    pooled_ref[0 * count : 1 * count, :] = high
    pooled_ref[1 * count : 2 * count, :] = low
    high, low = split_low(mean_live)
    pooled_ref[2 * count : 3 * count, :] = high
    pooled_ref[3 * count : 4 * count, :] = low


def attend_kernel(
    info,
    lengths,
    normed_ref,
    pooled_ref,
    near_ref,
    far_ref,
    bias_ref,
    mixed_ref,
    mixed_wide_ref,
    total_ref,
    q_ref,
    k_ref,
    v_ref,
    prob_ref,
    weight_s,
    mask_s,
    coarse_s,
    numer_s,
    full_s,
):
    rows = normed_ref.shape[0]
    pairs = q_ref.shape[0]
    tiles = 2 * rows // TILE
    half_tiles = rows // TILE
    length, own, partner = lengths[info[0]], info[1], info[2]
    line = info[5]
    assemble(info, near_ref, far_ref, full_s)
    pools = [pool_tile(odd) for odd in range(2)]
    spreads = [jnp.concatenate([spread_tile(odd)] * 2, axis=1) for odd in range(2)]
    lane = iota((1, 2 * TILE), 1) & (TILE - 1)
    for i in range(half_tiles):
        weight_s[i] = (lane + (own + i * TILE) < length).astype(F32)
        counts, _ = coarse_counts(lane + i * TILE, rows, length, own, partner)
        weight_s[half_tiles + i] = counts
    row_at = iota((TILE, 2 * TILE), 0)
    key_at = iota((TILE, 2 * TILE), 1) & (TILE - 1)
    pair_same = (row_at >> 5) == (key_at >> 5)
    apart = (row_at >> 4) != (key_at >> 4)
    mask_s[0] = pair_same.astype(F32)
    mask_s[1] = (pair_same & apart).astype(F32)
    live = (iota((rows, 1), 0) + own < length).astype(F32)
    counts, shift = coarse_counts(iota((rows, 1), 0), rows, length, own, partner)
    key_scale = 1.0 / jnp.maximum(counts, 1.0)
    query_scale = 1.0 / lax.shift_left(jnp.ones_like(shift), shift).astype(F32)
    top = pooled_ref.shape[0] // 4
    counts_other = counts[rows - top :]
    filled = counts_other / jnp.maximum(counts_other, 1.0)
    first, second = head_ones()

    def one_pair(p, carry):
        weight = full_s[p, :, : 3 * TILE]
        wide = mm(normed_ref[...], weight)
        biases = bias_row(bias_ref, p ^ line, 1)
        bq, bv = biases[:, :TILE], biases[:, TILE : 2 * TILE]
        query = (wide[:, :TILE] + bq).astype(BF16)
        key = (wide[:, TILE : 2 * TILE].astype(BF16).astype(F32) * live).astype(BF16)
        value = ((wide[:, 2 * TILE :] + bv).astype(BF16).astype(F32) * live).astype(BF16)
        extra = mm(pooled_ref[...], weight)
        q_other = extra[:top, :TILE] + extra[top : 2 * top, :TILE] + bq
        kv_other = extra[2 * top : 3 * top, TILE:] + extra[3 * top :, TILE:]
        k_other = kv_other[:, :TILE]
        v_other = kv_other[:, TILE:] + bv * filled
        q_ref[p, :rows, :] = query
        k_ref[p, :rows, :] = key
        v_ref[p, :rows, :] = value
        rows_all = jnp.concatenate([query, key, value], axis=1)
        for t in range(half_tiles):
            put_pooled(coarse_s, rows, t, mm(pools[t % 2], rows_all[t * TILE : (t + 1) * TILE]))
        q_ref[p, rows:, :] = (coarse_s[:, :TILE] * query_scale).astype(BF16)
        k_ref[p, rows:, :] = (coarse_s[:, TILE : 2 * TILE] * key_scale).astype(BF16)
        v_ref[p, rows:, :] = (coarse_s[:, 2 * TILE :] * key_scale).astype(BF16)
        q_ref[p, 2 * rows - top :, :] = q_other.astype(BF16)
        k_ref[p, 2 * rows - top :, :] = k_other.astype(BF16)
        v_ref[p, 2 * rows - top :, :] = v_other.astype(BF16)

        def one_tile(i, inner):
            at = pl.ds(pl.multiple_of(i * TILE, TILE), TILE)
            v = v_ref[p, at, :]
            score = mm_nt(q_ref[p, at, :], two_heads(k_ref[p, at, :], first, second)) * SCALE
            mask = mask_s[jnp.where(i >= half_tiles, 1, 0)]
            prob = jnp.where(mask > 0.0, jnp.exp(score) * weight_s[i], 0.0).astype(BF16)
            prob_ref[p, i] = prob
            values = jnp.concatenate(
                [
                    jnp.concatenate([v * first, first], axis=1),
                    jnp.concatenate([v * second, second], axis=1),
                ],
                axis=0,
            )
            numer_s[at, :] = mm(prob, values)
            return inner

        lax.fori_loop(0, tiles, one_tile, 0, unroll=4)
        for t in range(half_tiles):
            at = slice(t * TILE, (t + 1) * TILE)
            both = numer_s[at, :] + mm(
                spreads[t % 2], stacked_low(take_local(numer_s, rows, rows, t))
            )
            total = both[:, TILE:]
            mixed = both[:, :TILE] / total
            total_ref[p, at, :] = total
            mixed_wide_ref[p, at, :] = mixed
            mixed_ref[p, at, :] = mixed.astype(BF16)
        return carry

    lax.fori_loop(0, pairs, one_pair, 0)


def feed_kernel(
    info,
    own_ref,
    mixed_ref,
    near_ref,
    far_ref,
    ffn_near_ref,
    ffn_far_ref,
    b_out_ref,
    gain_ref,
    shift_ref,
    bias_ref,
    b_down_ref,
    hidden_ref,
    normed_ref,
    act_ref,
    slope_ref,
    *refs,
):
    *out_refs, result_s, full_s, ffn_s = refs
    pairs = mixed_ref.shape[0]
    line = info[5]
    assemble(info, near_ref, far_ref, full_s)
    assemble(info, ffn_near_ref, ffn_far_ref, ffn_s, by_line=False)
    hidden = own_ref[...].astype(F32) + b_out_ref[...]
    for p in range(pairs):
        hidden = hidden + mm_nt(mixed_ref[p], full_s[p, :, 3 * TILE :])
    hidden_ref[...] = hidden
    unit, _ = unit_rows(hidden)
    normed = (unit * gain_ref[...] + shift_ref[...]).astype(BF16)
    normed_ref[...] = normed
    result = hidden + b_down_ref[...]
    for z in range(pairs):
        pre = mm(normed, ffn_s[z, 0]) + bias_row(bias_ref, z ^ line, 0)
        half_erf = 0.5 + 0.5 * lax.erf(pre * INV_ROOT_TWO)
        act = (pre * half_erf).astype(BF16)
        act_ref[z] = act
        slope_ref[z] = (half_erf + pre * jnp.exp(-0.5 * pre * pre) * INV_ROOT_TAU).astype(BF16)
        result = result + mm(act, ffn_s[z, 1])
    result_s[...] = result
    chunk = out_refs[0].shape[0]
    for k, out_ref in enumerate(out_refs):
        at = ((info[4] * 2 + info[3]) ^ k) * chunk
        out_ref[...] = result_s[pl.ds(pl.multiple_of(at, chunk), chunk), :].astype(BF16)


def feed_back_kernel(
    info,
    dy_ref,
    ffn_near_ref,
    ffn_far_ref,
    near_ref,
    far_ref,
    slope_ref,
    hidden_ref,
    gain_ref,
    mixed_wide_ref,
    total_ref,
    grad_pre_ref,
    grad_hidden_ref,
    grad_hidden_low_ref,
    numer_ref,
    gtotal_ref,
    exchange_ref,
    vector_ref,
    b_up_ref,
    full_s,
    ffn_s,
):
    rows = dy_ref.shape[0]
    assemble(info, ffn_near_ref, ffn_far_ref, ffn_s, by_line=False)
    assemble(info, near_ref, far_ref, full_s)
    pairs = slope_ref.shape[0]
    dy = dy_ref[...]
    grad_normed = jnp.zeros((rows, dy.shape[1]), F32)
    for z in range(pairs):
        grad_act = mm_nt(dy, ffn_s[z, 1])
        grad_pre = (grad_act * slope_ref[z].astype(F32)).astype(BF16)
        grad_pre_ref[z] = grad_pre
        b_up_ref[z] = jnp.sum(grad_pre.astype(F32), axis=0, keepdims=True)
        grad_normed = grad_normed + mm_nt(grad_pre, ffn_s[z, 0])
    unit, inverse = unit_rows(hidden_ref[...])
    dy_wide = dy.astype(F32)
    vector_ref[0:1, :] = jnp.sum(grad_normed * unit, axis=0, keepdims=True)
    vector_ref[1:2, :] = jnp.sum(grad_normed, axis=0, keepdims=True)
    vector_ref[2:3, :] = jnp.sum(dy_wide, axis=0, keepdims=True)
    grad_hidden = dy_wide + norm_back(grad_normed, unit, inverse, gain_ref[...])
    vector_ref[3:4, :] = jnp.sum(grad_hidden, axis=0, keepdims=True)
    grad_hidden_ref[...] = grad_hidden
    low = grad_hidden.astype(BF16)
    grad_hidden_low_ref[...] = low
    pool = top_pool(rows)
    top = pool.shape[0]
    same = ((iota((TILE, TILE), 0) // HEAD_SIZE) == (iota((TILE, TILE), 1) // HEAD_SIZE)).astype(F32).astype(BF16)
    for p in range(pairs):
        grad_mixed = mm(low, full_s[p, :, 3 * TILE :]).astype(BF16).astype(F32)
        inv = 1.0 / total_ref[p]
        numer = grad_mixed * inv
        high, rest = split_low(grad_mixed * mixed_wide_ref[p])
        gtotal = -(mm(high, same) + mm(rest, same)) * inv
        numer_ref[p] = numer
        gtotal_ref[p] = gtotal
        exchange_ref[p, :top, :] = mm_wide(pool, numer)
        exchange_ref[p, top:, :] = mm_wide(pool, gtotal)


def give_out(info, near_ref, far_ref, z, part, values_s):
    core, plane = info[3], info[4]
    chunk = near_ref.shape[-2]
    for far, ref in enumerate((near_ref, far_ref)):
        for o in range(ref.shape[0]):
            at = ((o ^ plane) * 2 + (far ^ core)) * chunk
            ref[o, z, part] = values_s[pl.ds(pl.multiple_of(at, chunk), chunk), :]


def feed_grads_kernel(
    info, normed_ref, act_ref, grad_pre_ref, dy_ref, near_ref, far_ref, up_s, down_s
):
    line = info[5]
    for z in range(act_ref.shape[0]):
        up_s[...] = mm_tn(normed_ref[...], grad_pre_ref[z]).astype(BF16)
        give_out(info, near_ref, far_ref, z ^ line, 0, up_s)
        down_s[...] = mm_tn(act_ref[z], dy_ref[...]).astype(BF16)
        give_out(info, near_ref, far_ref, z ^ line, 1, down_s)


def attend_back_kernel(
    info,
    lengths,
    numer_ref,
    gtotal_ref,
    exchange_ref,
    q_ref,
    k_ref,
    v_ref,
    prob_ref,
    near_ref,
    far_ref,
    own_ref,
    gain_ref,
    grad_hidden_ref,
    grads_ref,
    b_qv_ref,
    grad_tokens_ref,
    vector_ref,
    coarse_s,
    left_s,
    grad_s,
    full_s,
    acc_s,
):
    pairs, rows = numer_ref.shape[0], numer_ref.shape[1]
    tiles = 2 * rows // TILE
    half_tiles = rows // TILE
    length, own, partner = lengths[info[0]], info[1], info[2]
    assemble(info, near_ref, far_ref, full_s)
    pools = [jnp.concatenate([pool_tile(odd)] * 2, axis=1) for odd in range(2)]
    spreads = [jnp.concatenate([spread_tile(odd)] * 2, axis=1) for odd in range(2)]
    live = (iota((rows, 1), 0) + own < length).astype(F32)
    counts, shift = coarse_counts(iota((rows, 1), 0), rows, length, own, partner)
    value_scale = 1.0 / jnp.maximum(counts, 1.0)
    query_scale = 1.0 / lax.shift_left(jnp.ones_like(shift), shift).astype(F32)
    first, second = head_ones()
    at_lane = iota((1, TILE), 1) & (HEAD_SIZE - 1)
    pick = (at_lane < 2).astype(F32)
    pick_first = (pick * first.astype(F32)).astype(BF16)
    pick_second = (pick * second.astype(F32)).astype(BF16)
    is_low = at_lane == 1
    top = exchange_ref.shape[1] // 2

    def two_parts(gtotal):
        high = gtotal.astype(BF16).astype(F32)
        return jnp.where(is_low, gtotal - high, high).astype(BF16)

    def one_pair(p, carry):
        for t in range(half_tiles):
            at = slice(t * TILE, (t + 1) * TILE)
            numer, gtotal = numer_ref[p, at, :], gtotal_ref[p, at, :]
            left_s[at, :TILE] = numer.astype(BF16)
            left_s[at, TILE:] = two_parts(gtotal)
            both = jnp.concatenate([numer, gtotal], axis=1)
            put_pooled(coarse_s, rows, t, mm(pools[t % 2], stacked_low(both)))
        coarse_s[rows - top :, :TILE] = exchange_ref[p, :top, :]
        coarse_s[rows - top :, TILE:] = exchange_ref[p, top:, :]
        left_s[rows:, :TILE] = coarse_s[:, :TILE].astype(BF16)
        left_s[rows:, TILE:] = two_parts(coarse_s[:, TILE:])

        def one_tile(i, inner):
            at = pl.ds(pl.multiple_of(i * TILE, TILE), TILE)
            v = v_ref[p, at, :]
            prob = prob_ref[p, i]
            left = left_s[at, :]
            right = jnp.concatenate(
                [
                    jnp.concatenate([v * first, pick_first], axis=1),
                    jnp.concatenate([v * second, pick_second], axis=1),
                ],
                axis=0,
            )
            grad_score = (mm_nt(left, right) * prob.astype(F32)).astype(BF16)
            grad_s[at, :TILE] = mm(grad_score, two_heads(k_ref[p, at, :], first, second))
            grad_s[at, TILE : 2 * TILE] = mm_tn(
                stand(grad_score), two_heads(q_ref[p, at, :], first, second)
            )
            grad_s[at, 2 * TILE :] = mm_tn(stand(prob), two_heads(left[:, :TILE], first, second))
            return inner

        lax.fori_loop(0, tiles, one_tile, 0, unroll=4)
        grad_s[rows:, :TILE] *= query_scale
        grad_s[rows:, TILE:] *= value_scale
        for t in range(half_tiles):
            at = slice(t * TILE, (t + 1) * TILE)
            fine = grad_s[at, :] + mm(
                spreads[t % 2], stacked_low(take_local(grad_s, rows, rows, t))
            )
            gq = (fine[:, :TILE] * SCALE).astype(BF16)
            gk = (fine[:, TILE : 2 * TILE] * (SCALE * live[at])).astype(BF16)
            gv = (fine[:, 2 * TILE :] * live[at]).astype(BF16)
            grads_ref[p, at, :] = jnp.concatenate([gq, gk, gv], axis=1)
        sums = jnp.sum(grads_ref[p].astype(F32), axis=0, keepdims=True)
        b_qv_ref[p, 0:1, :] = sums[:, :TILE]
        b_qv_ref[p, 1:2, :] = sums[:, 2 * TILE :]
        acc_s[...] += mm_nt(grads_ref[p], full_s[p, :, : 3 * TILE])
        return carry

    acc_s[...] = jnp.zeros_like(acc_s)
    lax.fori_loop(0, pairs, one_pair, 0)
    unit, inverse = unit_rows(own_ref[...].astype(F32))
    grad_normed = acc_s[...]
    vector_ref[0:1, :] = jnp.sum(grad_normed * unit, axis=0, keepdims=True)
    vector_ref[1:2, :] = jnp.sum(grad_normed, axis=0, keepdims=True)
    grad_tokens_ref[...] = (
        grad_hidden_ref[...] + norm_back(grad_normed, unit, inverse, gain_ref[...])
    ).astype(BF16)


def attend_grads_kernel(
    info,
    normed_ref,
    grads_ref,
    grad_hidden_ref,
    mixed_ref,
    vec_two_ref,
    vec_up_ref,
    vec_one_ref,
    b_qv_ref,
    near_ref,
    far_ref,
    both_s,
):
    core, line = info[3], info[5]
    pairs = mixed_ref.shape[0]
    dp = 2 * near_ref.shape[0]
    chunk = both_s.shape[0] // dp
    for z in range(pairs):
        grads = grads_ref[z]
        both_s[:, : 3 * TILE] = mm_tn(normed_ref[...], grads).astype(BF16)
        both_s[:, 3 * TILE :] = mm_tn(grad_hidden_ref[...], mixed_ref[z]).astype(BF16)
        for far, ref in enumerate((near_ref, far_ref)):
            for o in range(ref.shape[0]):
                at = (o * 2 + (far ^ core)) * chunk
                at = pl.ds(pl.multiple_of(at, chunk), chunk)
                to = pl.ds(pl.multiple_of((z ^ line) * chunk, chunk), chunk)
                ref[o, to, :] = both_s[at, :]
    vectors = [vec_two_ref[...]] + [vec_up_ref[z] for z in range(pairs)] + [vec_one_ref[...]]
    for row in range(2):
        parts = [b_qv_ref[p, row : row + 1, :] for p in range(pairs)]
        vectors.append(jnp.concatenate(parts, axis=1))
    vectors = jnp.concatenate(vectors, axis=0)
    blank = jnp.zeros((near_ref.shape[1] - pairs * chunk - vectors.shape[0], vectors.shape[1]), F32)
    vectors = jnp.concatenate([vectors, blank], axis=0).astype(BF16)
    for ref in (near_ref, far_ref):
        for o in range(ref.shape[0]):
            ref[o, pairs * chunk :, :] = vectors


def place_grads_kernel(info, near_ref, far_ref, up_ref, down_ref, q_ref, k_ref, v_ref, o_ref, turn_s):
    core, plane = info[3], info[4]
    chunk = near_ref.shape[-2]
    for far, ref in enumerate((near_ref, far_ref)):
        for o in range(ref.shape[0]):
            at = ((o ^ plane) * 2 + (far ^ core)) * chunk
            at = pl.ds(pl.multiple_of(at, chunk), chunk)
            up_ref[at, :] = ref[o, 0].astype(F32)
            down_ref[at, :] = ref[o, 1].astype(F32)
            rest = ref[o, 2].astype(F32)
            q_ref[at, :] = rest[:, :TILE]
            k_ref[at, :] = rest[:, TILE : 2 * TILE]
            v_ref[at, :] = rest[:, 2 * TILE : 3 * TILE]
            turn_s[at, :] = rest[:, 3 * TILE :]
    o_ref[...] = turn_s[...].T


def gather_line(line, refs, to_ref):
    own, one, two, three, passed = refs
    middle = (line == 1) | (line == 2)
    to_ref[line] = own[...]
    to_ref[line ^ 1] = one[...]
    to_ref[line ^ 2] = two[...]

    @pl.when(middle)
    def _():
        to_ref[line ^ 3] = three[...]

    @pl.when(jnp.logical_not(middle))
    def _():
        to_ref[line ^ 3] = passed[...]


def place_rows_kernel(info, *refs):
    gather_line(info[5], refs[:-1], refs[-1])


def deal_kernel(info, dealing, *refs):
    *pieces, out_ref, all_s = refs
    gather_line(info[5], pieces, all_s)
    own = info[4] * 2 + info[3]
    for i in range(out_ref.shape[0]):
        for slot in range(out_ref.shape[1]):
            seq = dealing[i * out_ref.shape[1] + slot]
            for half in range(out_ref.shape[2]):
                out_ref[i, slot, half] = all_s[(seq & 1) * 2 + half, (seq >> 1) ^ own]


def settle_kernel(pieces_ref, out_ref):
    dps, slots, halves = pieces_ref.shape[:3]
    for i in range(dps):
        for slot in range(slots):
            for half in range(halves):
                out_ref[slot, half, i] = pieces_ref[i, slot, half]


VMEM_SPEC = pl.BlockSpec(memory_space=pltpu.VMEM)
SMEM_SPEC = pl.BlockSpec(memory_space=pltpu.SMEM)


def call(kernel, outs, scalars, args, scratch=(), limit=16, long=False):
    return pl.pallas_call(
        kernel,
        out_shape=[jax.ShapeDtypeStruct(shape, dtype) for shape, dtype in outs],
        in_specs=[SMEM_SPEC] * len(scalars) + [VMEM_SPEC] * len(args),
        out_specs=[VMEM_SPEC] * len(outs),
        scratch_shapes=list(scratch),
        compiler_params=pltpu.CompilerParams(vmem_limit_bytes=limit << 20),
        cost_estimate=pl.CostEstimate(
            flops=10**10 if long else 1, transcendentals=0, bytes_accessed=1
        ),
    )(*scalars, *args)


def exchange(pieces, axis, groups=None):
    return lax.all_to_all(pieces, axis, 0, 0, tiled=True, axis_index_groups=groups)


def gather(piece, axis, count):
    return exchange(jnp.broadcast_to(piece[None], (count,) + piece.shape), axis)


def swap(piece, axis, distance):
    size = lax.axis_size(axis)
    return lax.ppermute(piece, axis, [(i, i ^ distance) for i in range(size)])


def after(value, *others):
    return lax.optimization_barrier((value, others))[0]


def total_of(pieces):
    return functools.reduce(jnp.add, [piece.astype(F32) for piece in pieces]).astype(BF16)


def local(
    tokens,
    cotangent,
    lengths,
    dealing,
    ln1_gain,
    ln1_bias,
    w_query,
    b_query,
    w_key,
    w_value,
    b_value,
    w_out,
    b_out,
    ln2_gain,
    ln2_bias,
    w_up,
    b_up,
    w_down,
    b_down,
):
    seq_dev, length, width = tokens.shape
    dp = lax.axis_size("dp")
    nt = lax.axis_size("tensor")
    d = lax.axis_index("dp")
    t = lax.axis_index("tensor")
    rows = seq_dev * length // nt
    outer = dp // 2
    planes = [[2 * o + c for o in range(outer)] for c in range(2)]
    chunk = width // dp
    hid = w_up.shape[1]

    def near_line(piece):
        return [piece] + [swap(piece, "tensor", z) for z in range(1, nt)]

    def line_first(piece):
        return [piece, swap(piece, "tensor", 1), swap(piece, "tensor", 2)]

    def line_second(pieces):
        piece, one, two = pieces
        three = lax.ppermute(after(piece, two), "tensor", [(1, 2), (2, 1)])
        passed = lax.ppermute(two, "tensor", [(1, 0), (2, 3)])
        return [piece, one, two, three, passed]

    def plane_pieces(piece):
        return [piece] + [swap(piece, "dp", 2 * o) for o in range(1, outer)]

    own_base = (t % 2) * rows
    info = jnp.stack([d * seq_dev + t // 2, own_base, rows - own_base, d % 2, d // 2, t])
    row = lambda v: v.reshape(1, -1)

    slice_spec = lambda lanes: pl.BlockSpec((chunk, lanes), lambda i, info: (info[4] * 2 + info[3], 0))
    whole_spec = lambda shape: pl.BlockSpec(shape, lambda i, info: (0,) * len(shape))
    attn_piece, ffn_piece = pl.pallas_call(
        pack_kernel,
        out_shape=[
            jax.ShapeDtypeStruct((chunk + 16, 4 * TILE), BF16),
            jax.ShapeDtypeStruct((2, chunk, hid), BF16),
        ],
        grid_spec=pltpu.PrefetchScalarGridSpec(
            num_scalar_prefetch=1,
            grid=(1,),
            in_specs=[slice_spec(TILE)] * 3
            + [whole_spec((TILE, width)), slice_spec(hid), slice_spec(width)]
            + [whole_spec((1, TILE)), whole_spec((1, TILE)), whole_spec((1, hid))],
            out_specs=[whole_spec((chunk + 16, 4 * TILE)), whole_spec((2, chunk, hid))],
            scratch_shapes=[pltpu.VMEM((width, TILE), BF16)],
        ),
    )(info, w_query, w_key, w_value, w_out, w_up, w_down, row(b_query), row(b_value), row(b_up))
    halves = tokens.reshape(nt, rows, width)
    own = lax.dynamic_index_in_dim(halves, t, 0, keepdims=False)
    other = lax.dynamic_index_in_dim(halves, t ^ 1, 0, keepdims=False)
    dy = lax.dynamic_index_in_dim(cotangent.reshape(nt, rows, width), t, 0, keepdims=False)
    top = rows >> level_shifts(rows)[-1]

    attn_full = pltpu.VMEM((nt, width, 4 * TILE), BF16)
    ffn_full = pltpu.VMEM((nt, 2, width, hid), BF16)

    normed_one, pooled = call(
        norm_one_kernel,
        [((rows, width), BF16), ((4 * top, width), BF16)],
        [info, lengths],
        [own, other, row(ln1_gain), row(ln1_bias)],
    )
    attn_line = near_line(attn_piece)
    normed_one, *attn_line = lax.optimization_barrier((normed_one, *attn_line))
    biases = jnp.stack([piece[chunk:] for piece in attn_line])
    ffn_line = gather(ffn_piece, "tensor", nt)
    attn_pieces = plane_pieces(jnp.stack([piece[:chunk] for piece in attn_line]))
    attn_near = jnp.stack(after(tuple(attn_pieces), ffn_line))
    attn_w = attn_near, swap(attn_near, "dp", 1)
    ffn_pieces = plane_pieces(after(ffn_line, attn_pieces[1]))
    normed_one = after(normed_one, ffn_line)

    mixed, mixed_wide, total, q, k, v, prob = call(
        attend_kernel,
        [((nt, rows, TILE), BF16), ((nt, rows, TILE), F32), ((nt, rows, TILE), F32)]
        + [((nt, 2 * rows, TILE), BF16)] * 3
        + [((nt, 2 * rows // TILE, TILE, 2 * TILE), BF16)],
        [info, lengths],
        [normed_one, pooled, *attn_w, biases],
        scratch=[
            pltpu.VMEM((2 * rows // TILE, 1, 2 * TILE), F32),
            pltpu.VMEM((2, TILE, 2 * TILE), F32),
            pltpu.VMEM((rows, 3 * TILE), F32),
            pltpu.VMEM((2 * rows, 2 * TILE), F32),
            attn_full,
        ],
        limit=24,
        long=True,
    )
    ffn_near = jnp.stack([after(each, mixed) for each in ffn_pieces])
    ffn_w = ffn_near, swap(ffn_near, "dp", 1)
    piece = rows // dp
    hidden, normed_two, act, slope, *outs = call(
        feed_kernel,
        [((rows, width), F32), ((rows, width), BF16)]
        + [((nt, rows, hid), BF16)] * 2
        + [((piece, width), BF16)] * dp,
        [info],
        [own, mixed, *attn_w, *ffn_w]
        + [row(b_out), row(ln2_gain), row(ln2_bias), biases, row(b_down)],
        scratch=[pltpu.VMEM((rows, width), F32), attn_full, ffn_full],
        limit=28,
    )
    chunks = [outs[0]] + [swap(outs[k], "dp", k) for k in range(1, dp)]

    grad_pre, grad_hidden, grad_hidden_low, numer, gtotal, sent, vec_two, vec_up = call(
        feed_back_kernel,
        [
            ((nt, rows, hid), BF16),
            ((rows, width), F32),
            ((rows, width), BF16),
            ((nt, rows, TILE), F32),
            ((nt, rows, TILE), F32),
            ((nt, 2 * top, TILE), F32),
            ((4, width), F32),
            ((nt, 1, hid), F32),
        ],
        [info],
        [dy, *ffn_w, *attn_w, slope, hidden, row(ln2_gain), mixed_wide, total],
        scratch=[attn_full, ffn_full],
        limit=28,
    )
    swapped = swap(sent, "tensor", 1)
    ffn_grads = call(
        feed_grads_kernel,
        [((outer, nt, 2, chunk, hid), BF16)] * 2,
        [info],
        [normed_two, act, grad_pre, dy],
        scratch=[pltpu.VMEM((width, hid), BF16)] * 2,
    )
    ffn_far = swap(ffn_grads[1], "dp", 1)

    def core_sums(near, far):
        return [total_of([near[o], far[o]]) for o in range(outer)]

    def plane_parts(pieces):
        return [pieces[0]] + [swap(pieces[o], "dp", 2 * o) for o in range(1, outer)]

    ffn_parts = core_sums(ffn_grads[0], ffn_far)
    gtotal, chunks, ffn_parts, swapped = lax.optimization_barrier(
        (gtotal, jnp.stack(chunks), ffn_parts, swapped)
    )
    chunks = line_first(chunks)
    ffn_parts = plane_parts(ffn_parts)
    qkv_grads, vec_qv, grad_low, vec_one = call(
        attend_back_kernel,
        [
            ((nt, rows, 3 * TILE), BF16),
            ((nt, 2, TILE), F32),
            ((rows, width), BF16),
            ((2, width), F32),
        ],
        [info, lengths],
        [numer, gtotal, swapped, q, k, v, prob, *attn_w]
        + [own, row(ln1_gain), grad_hidden],
        scratch=[
            pltpu.VMEM((rows, 2 * TILE), F32),
            pltpu.VMEM((2 * rows, 2 * TILE), BF16),
            pltpu.VMEM((2 * rows, 3 * TILE), F32),
            attn_full,
            pltpu.VMEM((rows, width), F32),
        ],
        limit=20,
        long=True,
    )
    row_pieces = line_first(grad_low)
    attn_near, attn_far = call(
        attend_grads_kernel,
        [((outer, nt * chunk + 16, 4 * TILE), BF16)] * 2,
        [info],
        [normed_one, qkv_grads, grad_hidden_low, mixed, vec_two, vec_up, vec_one, vec_qv],
        scratch=[pltpu.VMEM((width, 4 * TILE), BF16)],
    )
    attn_far, chunks, ffn_parts = lax.optimization_barrier((attn_far, chunks, ffn_parts))
    attn_far = swap(attn_far, "dp", 1)
    (dealt,) = call(
        deal_kernel,
        [((dp, seq_dev, nt // seq_dev, piece, width), BF16)],
        [info, dealing],
        line_second(chunks),
        scratch=[pltpu.VMEM((nt, dp, piece, width), BF16)],
    )
    dealt = exchange(dealt, "dp")
    attn_parts = exchange(total_of([attn_near, attn_far]), "dp", planes)
    attn_parts = total_of(list(attn_parts))
    attn_parts, row_pieces = lax.optimization_barrier((attn_parts, row_pieces))
    ffn_parts = total_of(ffn_parts)
    grads = [
        jnp.concatenate(
            [ffn_parts[z].reshape(2 * chunk, hid), attn_parts[z * chunk : (z + 1) * chunk]]
            + [attn_parts[nt * chunk :]]
        )
        for z in range(nt)
    ]
    grads = total_of([grads[0]] + [swap(grads[z], "tensor", z) for z in range(1, nt)])
    vectors = grads[3 * chunk :].astype(F32)
    row_pieces = line_second(row_pieces)
    near = jnp.stack(plane_pieces(grads[: 3 * chunk].reshape(3, chunk, width)))
    near = after(near, dealt)
    grads = near, swap(near, "dp", 1)
    g_up, g_down, g_query, g_key, g_value, g_out = call(
        place_grads_kernel,
        [((width, hid), F32), ((hid, width), F32)]
        + [((width, TILE), F32)] * 3
        + [((TILE, width), F32)],
        [info],
        grads,
        scratch=[pltpu.VMEM((width, TILE), F32)],
    )
    (grad_tokens,) = call(
        place_rows_kernel, [((nt, rows, width), BF16)], [info], row_pieces
    )
    grad_tokens = grad_tokens.reshape(seq_dev, length, width)
    (output,) = call(
        settle_kernel, [((seq_dev, nt // seq_dev, dp, piece, width), BF16)], [], [dealt]
    )
    output = output.reshape(seq_dev, length, width)
    base = 4 + nt
    g_b_up = lax.dynamic_index_in_dim(vectors[4:base], t, 0, keepdims=False)
    g_b_q = lax.dynamic_index_in_dim(vectors[base + 2].reshape(nt, TILE), t, 0, keepdims=False)
    g_b_v = lax.dynamic_index_in_dim(vectors[base + 3].reshape(nt, TILE), t, 0, keepdims=False)
    return (
        output,
        grad_tokens,
        vectors[base],
        vectors[base + 1],
        g_query,
        g_b_q,
        g_key,
        g_value,
        g_b_v,
        g_out,
        vectors[3],
        vectors[0],
        vectors[1],
        g_up,
        g_b_up,
        g_down,
        vectors[2],
    )


def solution(mesh):
    placed = (
        P("dp", None, None),
        P("dp", None, None),
        P(),
        P(),
        P(),
        P(),
        P(None, "tensor"),
        P("tensor"),
        P(None, "tensor"),
        P(None, "tensor"),
        P("tensor"),
        P("tensor", None),
        P(),
        P(),
        P(),
        P(None, "tensor"),
        P("tensor"),
        P("tensor", None),
        P(),
    )
    return jax.shard_map(
        local,
        mesh=mesh,
        in_specs=placed,
        out_specs=(
            P("dp", None, None),
            P("dp", None, None),
            P(),
            P(),
            P(None, "tensor"),
            P("tensor"),
            P(None, "tensor"),
            P(None, "tensor"),
            P("tensor"),
            P("tensor", None),
            P(),
            P(),
            P(),
            P(None, "tensor"),
            P("tensor"),
            P("tensor", None),
            P(),
        ),
        check_vma=False,
    )
```

```python
import functools

import jax
import jax.numpy as jnp
from jax import lax
from jax.experimental import pallas as pl
from jax.experimental.pallas import tpu as pltpu
from jax.sharding import PartitionSpec as P

F32 = jnp.float32
BF16 = jnp.bfloat16
HEAD_SIZE = 64
BLOCK = 16
TILE = 128
EPS = 1e-05
INV_ROOT_TWO = 0.7071067811865476
INV_ROOT_TAU = 0.3989422804014327
SCALE = HEAD_SIZE ** (-0.5)


def mm(left, right):
    return lax.dot_general(left, right, (((1,), (0,)), ((), ())), preferred_element_type=F32)


def mm_nt(left, right):
    return lax.dot_general(left, right, (((1,), (1,)), ((), ())), preferred_element_type=F32)


def mm_tn(left, right):
    return lax.dot_general(left, right, (((0,), (0,)), ((), ())), preferred_element_type=F32)


def split_low(values):
    high = values.astype(BF16)
    return high, (values - high.astype(F32)).astype(BF16)


def mm_wide(left, values):
    high, low = split_low(values)
    return mm(left, high) + mm(left, low)


def iota(shape, axis):
    return lax.broadcasted_iota(jnp.int32, shape, axis)


def unit_rows(values):
    centred = values - jnp.mean(values, axis=-1, keepdims=True)
    inverse = lax.rsqrt(jnp.mean(centred * centred, axis=-1, keepdims=True) + EPS)
    return centred * inverse, inverse


def norm_back(grad, unit, inverse, gain):
    scaled = grad * gain
    return inverse * (
        scaled
        - jnp.mean(scaled, axis=-1, keepdims=True)
        - unit * jnp.mean(scaled * unit, axis=-1, keepdims=True)
    )


def level_shifts(rows):
    shifts = []
    shift = 1
    while (2 * rows) >> shift >= 2 * BLOCK:
        shifts.append(shift)
        shift += 1
    return shifts


def coarse_map(index, rows):
    shifts = level_shifts(rows)
    shift = jnp.zeros_like(index)
    start = jnp.zeros_like(index)
    offset = 0
    for s in shifts:
        here = index >= offset
        shift = jnp.where(here, s, shift)
        start = jnp.where(here, offset, start)
        offset += rows >> s
    other = index >= offset
    start = jnp.where(other, offset, start)
    return shift, index - start, other


def coarse_counts(index, rows, length, own, partner):
    shift, place, other = coarse_map(index, rows)
    base = jnp.where(other, partner, own)
    left = length - base - lax.shift_left(place, shift)
    return jnp.clip(left, 0, lax.shift_left(jnp.ones_like(shift), shift)).astype(F32), shift


def tile_map(index):
    shift = jnp.zeros_like(index)
    start = jnp.zeros_like(index)
    offset = 0
    for s in range(1, 6):
        here = index >= offset
        shift = jnp.where(here, s, shift)
        start = jnp.where(here, offset, start)
        offset += TILE >> s
    return shift, index - start, index >= offset - (TILE >> 5)


def pool_tile(odd):
    shift, place, last = tile_map(iota((TILE, TILE), 0))
    place = jnp.where(last, place - odd * (TILE >> 5), place)
    hit = lax.shift_right_logical(iota((TILE, TILE), 1), shift) == place
    return hit.astype(F32).astype(BF16)


def spread_tile(odd):
    shift, place, last = tile_map(iota((TILE, TILE), 1))
    place = jnp.where(last, place - odd * (TILE >> 5), place)
    hit = lax.shift_right_logical(iota((TILE, TILE), 0), shift) == place
    return hit.astype(F32).astype(BF16)


def level_places(rows, tile):
    found = []
    local, offset = 0, 0
    for s in level_shifts(rows):
        count = TILE >> s
        found.append((local, count, offset + tile * count))
        local += count
        offset += rows >> s
    return found[:-1], found[-1]


def put_pooled(to_s, rows, tile, pooled):
    levels, (local, count, at) = level_places(rows, tile)
    for start, number, place in levels:
        to_s[place : place + number, :] = pooled[start : start + number]
    at -= (tile % 2) * count
    if tile % 2:
        to_s[at : at + 2 * count, :] += pooled[local : local + 2 * count]
    else:
        to_s[at : at + 2 * count, :] = pooled[local : local + 2 * count]


def take_local(from_s, base, rows, tile):
    levels, (local, count, at) = level_places(rows, tile)
    at -= (tile % 2) * count
    parts = [from_s[base + place : base + place + number, :] for _, number, place in levels]
    return jnp.concatenate(parts + [from_s[base + at : base + at + 2 * count, :]], axis=0)


def stacked_low(values):
    return jnp.concatenate(split_low(values), axis=0)


def top_pool(rows):
    shift = level_shifts(rows)[-1]
    count = rows >> shift
    hit = lax.shift_right_logical(iota((count, rows), 1), shift) == iota((count, rows), 0)
    return hit.astype(F32).astype(BF16)


def head_ones():
    second = (iota((TILE, TILE), 1) >= HEAD_SIZE).astype(F32)
    return (1.0 - second).astype(BF16), second.astype(BF16)


def two_heads(values, first, second):
    return jnp.concatenate([values * first, values * second], axis=0)


def stand(values):
    return jnp.concatenate([values[:, :TILE], values[:, TILE:]], axis=0)


def assemble(info, near_ref, far_ref, to_ref):
    core, plane, line = info[3], info[4], info[5]
    chunk = near_ref.shape[-2]
    for far, ref in enumerate((near_ref, far_ref)):
        for o in range(ref.shape[0]):
            at = ((o ^ plane) * 2 + (far ^ core)) * chunk
            at = pl.ds(pl.multiple_of(at, chunk), chunk)
            for z in range(ref.shape[1]):
                to_ref[z ^ line, at, :] = ref[o, z]


def assemble_feed(info, plan, refs, to_ref):
    core, plane = info[3], info[4]
    for (part, far, chips), ref in zip(plan, refs):
        chunk = ref.shape[-2]
        for i, o in enumerate(chips):
            at = ((o ^ plane) * 2 + (far ^ core)) * chunk
            at = pl.ds(pl.multiple_of(at, chunk), chunk)
            for z in range(ref.shape[1]):
                to_ref[z, part, at, :] = ref[i, z]


def pack_kernel(info, q_ref, k_ref, v_ref, o_ref, up_ref, down_ref, bq_ref, bv_ref, bu_ref, attn_ref, ffn_ref, turn_s):
    chunk = q_ref.shape[0]
    attn_ref[:chunk, 0 * TILE : 1 * TILE] = q_ref[...]
    attn_ref[:chunk, 1 * TILE : 2 * TILE] = k_ref[...]
    attn_ref[:chunk, 2 * TILE : 3 * TILE] = v_ref[...]
    turn_s[...] = o_ref[...].T
    at = pl.ds(pl.multiple_of((info[4] * 2 + info[3]) * chunk, chunk), chunk)
    attn_ref[:chunk, 3 * TILE :] = turn_s[at, :]
    ffn_ref[0] = up_ref[...]
    ffn_ref[1] = down_ref[...]
    lanes = bu_ref.shape[1]
    blank = jnp.zeros((1, lanes - 2 * TILE), F32)
    rest = jnp.concatenate(
        [bu_ref[...], jnp.concatenate([bq_ref[...], bv_ref[...], blank], axis=1)], axis=0
    )
    rows = []
    for _ in range(3):
        part = rest.astype(BF16).astype(F32)
        rows.append(part)
        rest = rest - part
    rows.append(jnp.zeros((10, lanes), F32))
    attn_ref[chunk:, :] = jnp.concatenate(rows, axis=0).astype(BF16)


def stack_kernel(*refs):
    *pieces, weight_ref, bias_ref = refs
    chunk = weight_ref.shape[1]
    for z, ref in enumerate(pieces):
        weight_ref[z] = ref[:chunk, :]
        bias_ref[z] = ref[chunk:, :]


def part_kernel(info, *refs):
    *pieces, up_ref, down_ref = refs
    for where, z, ref in line_sources(info[5], pieces):

        def put(z=z, ref=ref):
            up_ref[z] = ref[0]
            down_ref[z] = ref[1]

        put() if where is None else pl.when(where)(put)


def pair_kernel(near_ref, far_ref, *out_refs):
    for o, ref in enumerate(out_refs):
        ref[0] = near_ref[o]
        ref[1] = far_ref[o]


def bias_row(bias_ref, z, row):
    total = bias_ref[z, row : row + 1, :].astype(F32)
    for part in range(1, 3):
        at = 2 * part + row
        total = total + bias_ref[z, at : at + 1, :].astype(F32)
    return total


def norm_one_kernel(info, lengths, own_ref, other_ref, gain_ref, bias_ref, normed_ref, pooled_ref):
    rows = own_ref.shape[0]
    length, partner = lengths[info[0]], info[2]
    gain, bias = gain_ref[...], bias_ref[...]
    unit, _ = unit_rows(own_ref[...].astype(F32))
    normed_ref[...] = (unit * gain + bias).astype(BF16)
    unit, _ = unit_rows(other_ref[...].astype(F32))
    normed = (unit * gain + bias).astype(BF16)
    pool = top_pool(rows)
    count = pool.shape[0]
    live = (iota((1, rows), 1) + partner < length).astype(F32)
    pool_live = (pool.astype(F32) * live).astype(BF16)
    sums = mm(pool_live, normed)
    counts = jnp.sum(pool_live.astype(F32), axis=-1, keepdims=True)
    mean_live = sums / jnp.maximum(counts, 1.0)
    mean_all = mm(pool, normed) * (count / rows)
    high, low = split_low(mean_all)
    pooled_ref[0 * count : 1 * count, :] = high
    pooled_ref[1 * count : 2 * count, :] = low
    high, low = split_low(mean_live)
    pooled_ref[2 * count : 3 * count, :] = high
    pooled_ref[3 * count : 4 * count, :] = low


def attend_kernel(
    info,
    lengths,
    normed_ref,
    pooled_ref,
    near_ref,
    far_ref,
    bias_ref,
    mixed_ref,
    mixed_wide_ref,
    total_ref,
    q_ref,
    k_ref,
    v_ref,
    prob_ref,
    weight_s,
    mask_s,
    coarse_s,
    numer_s,
    full_s,
):
    rows = normed_ref.shape[0]
    pairs = q_ref.shape[0]
    tiles = 2 * rows // TILE
    half_tiles = rows // TILE
    length, own, partner = lengths[info[0]], info[1], info[2]
    line = info[5]
    assemble(info, near_ref, far_ref, full_s)
    pools = [pool_tile(odd) for odd in range(2)]
    spreads = [jnp.concatenate([spread_tile(odd)] * 2, axis=1) for odd in range(2)]
    lane = iota((1, 2 * TILE), 1) & (TILE - 1)
    for i in range(half_tiles):
        weight_s[i] = (lane + (own + i * TILE) < length).astype(F32)
        counts, _ = coarse_counts(lane + i * TILE, rows, length, own, partner)
        weight_s[half_tiles + i] = counts
    row_at = iota((TILE, 2 * TILE), 0)
    key_at = iota((TILE, 2 * TILE), 1) & (TILE - 1)
    pair_same = (row_at >> 5) == (key_at >> 5)
    apart = (row_at >> 4) != (key_at >> 4)
    mask_s[0] = pair_same.astype(F32)
    mask_s[1] = (pair_same & apart).astype(F32)
    live = (iota((rows, 1), 0) + own < length).astype(F32)
    counts, shift = coarse_counts(iota((rows, 1), 0), rows, length, own, partner)
    key_scale = 1.0 / jnp.maximum(counts, 1.0)
    query_scale = 1.0 / lax.shift_left(jnp.ones_like(shift), shift).astype(F32)
    top = pooled_ref.shape[0] // 4
    counts_other = counts[rows - top :]
    filled = counts_other / jnp.maximum(counts_other, 1.0)
    first, second = head_ones()

    def one_pair(p, carry):
        weight = full_s[p, :, : 3 * TILE]
        wide = mm(normed_ref[...], weight)
        biases = bias_row(bias_ref, p ^ line, 1)
        bq, bv = biases[:, :TILE], biases[:, TILE : 2 * TILE]
        query = (wide[:, :TILE] + bq).astype(BF16)
        key = (wide[:, TILE : 2 * TILE].astype(BF16).astype(F32) * live).astype(BF16)
        value = ((wide[:, 2 * TILE :] + bv).astype(BF16).astype(F32) * live).astype(BF16)
        extra = mm(pooled_ref[...], weight)
        q_other = extra[:top, :TILE] + extra[top : 2 * top, :TILE] + bq
        kv_other = extra[2 * top : 3 * top, TILE:] + extra[3 * top :, TILE:]
        k_other = kv_other[:, :TILE]
        v_other = kv_other[:, TILE:] + bv * filled
        q_ref[p, :rows, :] = query
        k_ref[p, :rows, :] = key
        v_ref[p, :rows, :] = value
        rows_all = jnp.concatenate([query, key, value], axis=1)
        for t in range(half_tiles):
            put_pooled(coarse_s, rows, t, mm(pools[t % 2], rows_all[t * TILE : (t + 1) * TILE]))
        q_ref[p, rows:, :] = (coarse_s[:, :TILE] * query_scale).astype(BF16)
        k_ref[p, rows:, :] = (coarse_s[:, TILE : 2 * TILE] * key_scale).astype(BF16)
        v_ref[p, rows:, :] = (coarse_s[:, 2 * TILE :] * key_scale).astype(BF16)
        q_ref[p, 2 * rows - top :, :] = q_other.astype(BF16)
        k_ref[p, 2 * rows - top :, :] = k_other.astype(BF16)
        v_ref[p, 2 * rows - top :, :] = v_other.astype(BF16)

        def one_tile(i, inner):
            at = pl.ds(pl.multiple_of(i * TILE, TILE), TILE)
            v = v_ref[p, at, :]
            score = mm_nt(q_ref[p, at, :], two_heads(k_ref[p, at, :], first, second)) * SCALE
            mask = mask_s[jnp.where(i >= half_tiles, 1, 0)]
            prob = jnp.where(mask > 0.0, jnp.exp(score) * weight_s[i], 0.0).astype(BF16)
            prob_ref[p, i] = prob
            values = jnp.concatenate(
                [
                    jnp.concatenate([v * first, first], axis=1),
                    jnp.concatenate([v * second, second], axis=1),
                ],
                axis=0,
            )
            numer_s[at, :] = mm(prob, values)
            return inner

        lax.fori_loop(0, tiles, one_tile, 0, unroll=4)
        for t in range(half_tiles):
            at = slice(t * TILE, (t + 1) * TILE)
            both = numer_s[at, :] + mm(
                spreads[t % 2], stacked_low(take_local(numer_s, rows, rows, t))
            )
            total = both[:, TILE:]
            mixed = both[:, :TILE] / total
            total_ref[p, at, :] = total
            mixed_wide_ref[p, at, :] = mixed
            mixed_ref[p, at, :] = mixed.astype(BF16)
        return carry

    lax.fori_loop(0, pairs, one_pair, 0)


def feed_kernel(plan, info, own_ref, mixed_ref, near_ref, far_ref, *refs):
    ffn_refs, refs = refs[: len(plan)], refs[len(plan) :]
    b_out_ref, gain_ref, shift_ref, bias_ref, b_down_ref, hidden_ref, normed_ref = refs[:7]
    act_ref, slope_ref, *out_refs, result_s, full_s, ffn_s = refs[7:]
    pairs = mixed_ref.shape[0]
    line = info[5]
    assemble(info, near_ref, far_ref, full_s)
    assemble_feed(info, plan, ffn_refs, ffn_s)
    hidden = own_ref[...].astype(F32) + b_out_ref[...]
    for p in range(pairs):
        hidden = hidden + mm_nt(mixed_ref[p], full_s[p, :, 3 * TILE :])
    hidden_ref[...] = hidden
    unit, _ = unit_rows(hidden)
    normed = (unit * gain_ref[...] + shift_ref[...]).astype(BF16)
    normed_ref[...] = normed
    result = hidden + b_down_ref[...]
    for z in range(pairs):
        pre = mm(normed, ffn_s[z, 0]) + bias_row(bias_ref, z ^ line, 0)
        half_erf = 0.5 + 0.5 * lax.erf(pre * INV_ROOT_TWO)
        act = (pre * half_erf).astype(BF16)
        act_ref[z] = act
        slope_ref[z] = (half_erf + pre * jnp.exp(-0.5 * pre * pre) * INV_ROOT_TAU).astype(BF16)
        result = result + mm(act, ffn_s[z, 1])
    result_s[...] = result
    chunk = out_refs[0].shape[1]
    for far, out_ref in enumerate(out_refs):
        for o in range(out_ref.shape[0]):
            at = ((o ^ info[4]) * 2 + (far ^ info[3])) * chunk
            out_ref[o] = result_s[pl.ds(pl.multiple_of(at, chunk), chunk), :].astype(BF16)


def feed_back_kernel(plan, info, dy_ref, near_ref, far_ref, *refs):
    ffn_refs, refs = refs[: len(plan)], refs[len(plan) :]
    slope_ref, hidden_ref, gain_ref, mixed_wide_ref, total_ref, grad_pre_ref, grad_hidden_ref = refs[:7]
    grad_hidden_low_ref, numer_ref, gtotal_ref, exchange_ref, vector_ref, b_up_ref = refs[7:13]
    full_s, ffn_s = refs[13:]
    rows = dy_ref.shape[0]
    assemble_feed(info, plan, ffn_refs, ffn_s)
    assemble(info, near_ref, far_ref, full_s)
    pairs = slope_ref.shape[0]
    dy = dy_ref[...]
    grad_normed = jnp.zeros((rows, dy.shape[1]), F32)
    for z in range(pairs):
        grad_act = mm_nt(dy, ffn_s[z, 1])
        grad_pre = (grad_act * slope_ref[z].astype(F32)).astype(BF16)
        grad_pre_ref[z] = grad_pre
        b_up_ref[z] = jnp.sum(grad_pre.astype(F32), axis=0, keepdims=True)
        grad_normed = grad_normed + mm_nt(grad_pre, ffn_s[z, 0])
    unit, inverse = unit_rows(hidden_ref[...])
    dy_wide = dy.astype(F32)
    vector_ref[0:1, :] = jnp.sum(grad_normed * unit, axis=0, keepdims=True)
    vector_ref[1:2, :] = jnp.sum(grad_normed, axis=0, keepdims=True)
    vector_ref[2:3, :] = jnp.sum(dy_wide, axis=0, keepdims=True)
    grad_hidden = dy_wide + norm_back(grad_normed, unit, inverse, gain_ref[...])
    vector_ref[3:4, :] = jnp.sum(grad_hidden, axis=0, keepdims=True)
    grad_hidden_ref[...] = grad_hidden
    low = grad_hidden.astype(BF16)
    grad_hidden_low_ref[...] = low
    pool = top_pool(rows)
    top = pool.shape[0]
    same = ((iota((TILE, TILE), 0) // HEAD_SIZE) == (iota((TILE, TILE), 1) // HEAD_SIZE)).astype(F32).astype(BF16)
    for p in range(pairs):
        grad_mixed = mm(low, full_s[p, :, 3 * TILE :]).astype(BF16).astype(F32)
        inv = 1.0 / total_ref[p]
        numer = grad_mixed * inv
        high, rest = split_low(grad_mixed * mixed_wide_ref[p])
        gtotal = -(mm(high, same) + mm(rest, same)) * inv
        numer_ref[p] = numer
        gtotal_ref[p] = gtotal
        exchange_ref[p, :top, :] = mm_wide(pool, numer)
        exchange_ref[p, top:, :] = mm_wide(pool, gtotal)


def give_out(info, near_ref, far_ref, z, part, values_s):
    core, plane = info[3], info[4]
    chunk = near_ref.shape[-2]
    for far, ref in enumerate((near_ref, far_ref)):
        for o in range(ref.shape[0]):
            at = ((o ^ plane) * 2 + (far ^ core)) * chunk
            ref[o, z, part] = values_s[pl.ds(pl.multiple_of(at, chunk), chunk), :]


def feed_grads_kernel(
    info, normed_ref, act_ref, grad_pre_ref, dy_ref, near_ref, far_ref, up_s, down_s
):
    line = info[5]
    for z in range(act_ref.shape[0]):
        up_s[...] = mm_tn(normed_ref[...], grad_pre_ref[z]).astype(BF16)
        give_out(info, near_ref, far_ref, z ^ line, 0, up_s)
        down_s[...] = mm_tn(act_ref[z], dy_ref[...]).astype(BF16)
        give_out(info, near_ref, far_ref, z ^ line, 1, down_s)


def attend_back_kernel(
    info,
    lengths,
    numer_ref,
    gtotal_ref,
    exchange_ref,
    q_ref,
    k_ref,
    v_ref,
    prob_ref,
    near_ref,
    far_ref,
    own_ref,
    gain_ref,
    grad_hidden_ref,
    grads_ref,
    b_qv_ref,
    grad_tokens_ref,
    vector_ref,
    coarse_s,
    left_s,
    grad_s,
    full_s,
    acc_s,
):
    pairs, rows = numer_ref.shape[0], numer_ref.shape[1]
    tiles = 2 * rows // TILE
    half_tiles = rows // TILE
    length, own, partner = lengths[info[0]], info[1], info[2]
    assemble(info, near_ref, far_ref, full_s)
    pools = [jnp.concatenate([pool_tile(odd)] * 2, axis=1) for odd in range(2)]
    spreads = [jnp.concatenate([spread_tile(odd)] * 2, axis=1) for odd in range(2)]
    live = (iota((rows, 1), 0) + own < length).astype(F32)
    counts, shift = coarse_counts(iota((rows, 1), 0), rows, length, own, partner)
    value_scale = 1.0 / jnp.maximum(counts, 1.0)
    query_scale = 1.0 / lax.shift_left(jnp.ones_like(shift), shift).astype(F32)
    first, second = head_ones()
    at_lane = iota((1, TILE), 1) & (HEAD_SIZE - 1)
    pick = (at_lane < 2).astype(F32)
    pick_first = (pick * first.astype(F32)).astype(BF16)
    pick_second = (pick * second.astype(F32)).astype(BF16)
    is_low = at_lane == 1
    top = exchange_ref.shape[1] // 2

    def two_parts(gtotal):
        high = gtotal.astype(BF16).astype(F32)
        return jnp.where(is_low, gtotal - high, high).astype(BF16)

    def one_pair(p, carry):
        for t in range(half_tiles):
            at = slice(t * TILE, (t + 1) * TILE)
            numer, gtotal = numer_ref[p, at, :], gtotal_ref[p, at, :]
            left_s[at, :TILE] = numer.astype(BF16)
            left_s[at, TILE:] = two_parts(gtotal)
            both = jnp.concatenate([numer, gtotal], axis=1)
            put_pooled(coarse_s, rows, t, mm(pools[t % 2], stacked_low(both)))
        coarse_s[rows - top :, :TILE] = exchange_ref[p, :top, :]
        coarse_s[rows - top :, TILE:] = exchange_ref[p, top:, :]
        left_s[rows:, :TILE] = coarse_s[:, :TILE].astype(BF16)
        left_s[rows:, TILE:] = two_parts(coarse_s[:, TILE:])

        def one_tile(i, inner):
            at = pl.ds(pl.multiple_of(i * TILE, TILE), TILE)
            v = v_ref[p, at, :]
            prob = prob_ref[p, i]
            left = left_s[at, :]
            right = jnp.concatenate(
                [
                    jnp.concatenate([v * first, pick_first], axis=1),
                    jnp.concatenate([v * second, pick_second], axis=1),
                ],
                axis=0,
            )
            grad_score = (mm_nt(left, right) * prob.astype(F32)).astype(BF16)
            grad_s[at, :TILE] = mm(grad_score, two_heads(k_ref[p, at, :], first, second))
            grad_s[at, TILE : 2 * TILE] = mm_tn(
                stand(grad_score), two_heads(q_ref[p, at, :], first, second)
            )
            grad_s[at, 2 * TILE :] = mm_tn(stand(prob), two_heads(left[:, :TILE], first, second))
            return inner

        lax.fori_loop(0, tiles, one_tile, 0, unroll=4)
        grad_s[rows:, :TILE] *= query_scale
        grad_s[rows:, TILE:] *= value_scale
        for t in range(half_tiles):
            at = slice(t * TILE, (t + 1) * TILE)
            fine = grad_s[at, :] + mm(
                spreads[t % 2], stacked_low(take_local(grad_s, rows, rows, t))
            )
            gq = (fine[:, :TILE] * SCALE).astype(BF16)
            gk = (fine[:, TILE : 2 * TILE] * (SCALE * live[at])).astype(BF16)
            gv = (fine[:, 2 * TILE :] * live[at]).astype(BF16)
            grads_ref[p, at, :] = jnp.concatenate([gq, gk, gv], axis=1)
        sums = jnp.sum(grads_ref[p].astype(F32), axis=0, keepdims=True)
        b_qv_ref[p, 0:1, :] = sums[:, :TILE]
        b_qv_ref[p, 1:2, :] = sums[:, 2 * TILE :]
        acc_s[...] += mm_nt(grads_ref[p], full_s[p, :, : 3 * TILE])
        return carry

    acc_s[...] = jnp.zeros_like(acc_s)
    lax.fori_loop(0, pairs, one_pair, 0)
    unit, inverse = unit_rows(own_ref[...].astype(F32))
    grad_normed = acc_s[...]
    vector_ref[0:1, :] = jnp.sum(grad_normed * unit, axis=0, keepdims=True)
    vector_ref[1:2, :] = jnp.sum(grad_normed, axis=0, keepdims=True)
    grad_tokens_ref[...] = (
        grad_hidden_ref[...] + norm_back(grad_normed, unit, inverse, gain_ref[...])
    ).astype(BF16)


def attend_grads_kernel(
    info,
    normed_ref,
    grads_ref,
    grad_hidden_ref,
    mixed_ref,
    vec_two_ref,
    vec_up_ref,
    vec_one_ref,
    b_qv_ref,
    near_ref,
    far_ref,
    both_s,
):
    core, plane, line = info[3], info[4], info[5]
    pairs = mixed_ref.shape[0]
    dp = 2 * near_ref.shape[0]
    chunk = both_s.shape[0] // dp
    for z in range(pairs):
        grads = grads_ref[z]
        both_s[:, : 3 * TILE] = mm_tn(normed_ref[...], grads).astype(BF16)
        both_s[:, 3 * TILE :] = mm_tn(grad_hidden_ref[...], mixed_ref[z]).astype(BF16)
        for far, ref in enumerate((near_ref, far_ref)):
            for o in range(ref.shape[0]):
                at = ((o ^ plane) * 2 + (far ^ core)) * chunk
                at = pl.ds(pl.multiple_of(at, chunk), chunk)
                to = pl.ds(pl.multiple_of((z ^ line) * chunk, chunk), chunk)
                ref[o, to, :] = both_s[at, :]
    vectors = [vec_two_ref[...]] + [vec_up_ref[z] for z in range(pairs)] + [vec_one_ref[...]]
    for row in range(2):
        parts = [b_qv_ref[p, row : row + 1, :] for p in range(pairs)]
        vectors.append(jnp.concatenate(parts, axis=1))
    vectors = jnp.concatenate(vectors, axis=0)
    blank = jnp.zeros((near_ref.shape[1] - pairs * chunk - vectors.shape[0], vectors.shape[1]), F32)
    vectors = jnp.concatenate([vectors, blank], axis=0).astype(BF16)
    for ref in (near_ref, far_ref):
        for o in range(ref.shape[0]):
            ref[o, pairs * chunk :, :] = vectors


def place_grads_kernel(info, near_ref, far_ref, up_ref, down_ref, q_ref, k_ref, v_ref, o_ref, turn_s):
    core, plane = info[3], info[4]
    chunk = near_ref.shape[-2]
    for far, ref in enumerate((near_ref, far_ref)):
        for o in range(ref.shape[0]):
            at = ((o ^ plane) * 2 + (far ^ core)) * chunk
            at = pl.ds(pl.multiple_of(at, chunk), chunk)
            up_ref[at, :] = ref[o, 0].astype(F32)
            down_ref[at, :] = ref[o, 1].astype(F32)
            rest = ref[o, 2].astype(F32)
            q_ref[at, :] = rest[:, :TILE]
            k_ref[at, :] = rest[:, TILE : 2 * TILE]
            v_ref[at, :] = rest[:, 2 * TILE : 3 * TILE]
            turn_s[at, :] = rest[:, 3 * TILE :]
    o_ref[...] = turn_s[...].T


def line_sources(line, refs):
    own, one, two, three, passed = refs
    middle = (line == 1) | (line == 2)
    return [
        (None, line, own),
        (None, line ^ 1, one),
        (None, line ^ 2, two),
        (middle, line ^ 3, three),
        (jnp.logical_not(middle), line ^ 3, passed),
    ]


def gather_line(line, refs, to_ref):
    for where, z, ref in line_sources(line, refs):

        def put(z=z, ref=ref):
            to_ref[z] = ref[...]

        put() if where is None else pl.when(where)(put)


def place_rows_kernel(info, *refs):
    gather_line(info[5], refs[:-1], refs[-1])


def deal_kernel(info, dealing, *refs):
    *pieces, out_ref, all_s = refs
    gather_line(info[5], pieces, all_s)
    own = info[4] * 2 + info[3]
    for i in range(out_ref.shape[0]):
        for slot in range(out_ref.shape[1]):
            seq = dealing[i * out_ref.shape[1] + slot]
            for half in range(out_ref.shape[2]):
                out_ref[i, slot, half] = all_s[(seq & 1) * 2 + half, (seq >> 1) ^ own]


def settle_kernel(pieces_ref, out_ref):
    dps, slots, halves = pieces_ref.shape[:3]
    for i in range(dps):
        for slot in range(slots):
            for half in range(halves):
                out_ref[slot, half, i] = pieces_ref[i, slot, half]


VMEM_SPEC = pl.BlockSpec(memory_space=pltpu.VMEM)
SMEM_SPEC = pl.BlockSpec(memory_space=pltpu.SMEM)


def call(kernel, outs, scalars, args, scratch=(), limit=16, long=False):
    return pl.pallas_call(
        kernel,
        out_shape=[jax.ShapeDtypeStruct(shape, dtype) for shape, dtype in outs],
        in_specs=[SMEM_SPEC] * len(scalars) + [VMEM_SPEC] * len(args),
        out_specs=[VMEM_SPEC] * len(outs),
        scratch_shapes=list(scratch),
        compiler_params=pltpu.CompilerParams(vmem_limit_bytes=limit << 20),
        cost_estimate=pl.CostEstimate(
            flops=10**10 if long else 1, transcendentals=0, bytes_accessed=1
        ),
    )(*scalars, *args)


def exchange(pieces, axis, groups=None):
    return lax.all_to_all(pieces, axis, 0, 0, tiled=True, axis_index_groups=groups)


def gather(piece, axis, count):
    return exchange(jnp.broadcast_to(piece[None], (count,) + piece.shape), axis)


def swap(piece, axis, distance):
    size = lax.axis_size(axis)
    return lax.ppermute(piece, axis, [(i, i ^ distance) for i in range(size)])


def after(value, *others):
    return lax.optimization_barrier((value, others))[0]


def total_of(pieces):
    return functools.reduce(jnp.add, [piece.astype(F32) for piece in pieces]).astype(BF16)


def local(
    tokens,
    cotangent,
    lengths,
    dealing,
    ln1_gain,
    ln1_bias,
    w_query,
    b_query,
    w_key,
    w_value,
    b_value,
    w_out,
    b_out,
    ln2_gain,
    ln2_bias,
    w_up,
    b_up,
    w_down,
    b_down,
):
    seq_dev, length, width = tokens.shape
    dp = lax.axis_size("dp")
    nt = lax.axis_size("tensor")
    d = lax.axis_index("dp")
    t = lax.axis_index("tensor")
    rows = seq_dev * length // nt
    outer = dp // 2
    planes = [[2 * o + c for o in range(outer)] for c in range(2)]
    chunk = width // dp
    hid = w_up.shape[1]

    def near_line(piece):
        return [piece] + [swap(piece, "tensor", z) for z in range(1, nt)]

    def line_first(piece):
        return [piece, swap(piece, "tensor", 1), swap(piece, "tensor", 2)]

    def line_second(pieces):
        piece, one, two = pieces
        three = lax.ppermute(after(piece, two), "tensor", [(1, 2), (2, 1)])
        passed = lax.ppermute(two, "tensor", [(1, 0), (2, 3)])
        return [piece, one, two, three, passed]

    def plane_pieces(piece, others=None):
        return [piece] + [swap(others[o] if others else piece, "dp", 2 * o) for o in range(1, outer)]

    own_base = (t % 2) * rows
    info = jnp.stack([d * seq_dev + t // 2, own_base, rows - own_base, d % 2, d // 2, t])
    row = lambda v: v.reshape(1, -1)

    slice_spec = lambda lanes: pl.BlockSpec((chunk, lanes), lambda i, info: (info[4] * 2 + info[3], 0))
    whole_spec = lambda shape: pl.BlockSpec(shape, lambda i, info: (0,) * len(shape))
    attn_piece, ffn_piece = pl.pallas_call(
        pack_kernel,
        out_shape=[
            jax.ShapeDtypeStruct((chunk + 16, 4 * TILE), BF16),
            jax.ShapeDtypeStruct((2, chunk, hid), BF16),
        ],
        grid_spec=pltpu.PrefetchScalarGridSpec(
            num_scalar_prefetch=1,
            grid=(1,),
            in_specs=[slice_spec(TILE)] * 3
            + [whole_spec((TILE, width)), slice_spec(hid), slice_spec(width)]
            + [whole_spec((1, TILE)), whole_spec((1, TILE)), whole_spec((1, hid))],
            out_specs=[whole_spec((chunk + 16, 4 * TILE)), whole_spec((2, chunk, hid))],
            scratch_shapes=[pltpu.VMEM((width, TILE), BF16)],
        ),
    )(info, w_query, w_key, w_value, w_out, w_up, w_down, row(b_query), row(b_value), row(b_up))
    halves = tokens.reshape(nt, rows, width)
    own = lax.dynamic_index_in_dim(halves, t, 0, keepdims=False)
    other = lax.dynamic_index_in_dim(halves, t ^ 1, 0, keepdims=False)
    dy = lax.dynamic_index_in_dim(cotangent.reshape(nt, rows, width), t, 0, keepdims=False)
    top = rows >> level_shifts(rows)[-1]

    attn_full = pltpu.VMEM((nt, width, 4 * TILE), BF16)
    ffn_full = pltpu.VMEM((nt, 2, width, hid), BF16)

    normed_one, pooled = call(
        norm_one_kernel,
        [((rows, width), BF16), ((4 * top, width), BF16)],
        [info, lengths],
        [own, other, row(ln1_gain), row(ln1_bias)],
    )
    attn_line = near_line(attn_piece)
    normed_one, *attn_line = lax.optimization_barrier((normed_one, *attn_line))
    biases = jnp.stack([piece[chunk:] for piece in attn_line])
    ffn_line = line_first(after(ffn_piece, attn_line[1]))
    attn_line, biases = call(
        stack_kernel,
        [((nt, chunk, 4 * TILE), BF16), ((nt, 16, 4 * TILE), BF16)],
        [],
        attn_line,
    )
    attn_pieces = plane_pieces(attn_line)
    up_line, down_line = call(
        part_kernel, [((nt, chunk, hid), BF16)] * 2, [info], line_second(ffn_line)
    )
    attn_pieces, up_line, down_line = lax.optimization_barrier((attn_pieces, up_line, down_line))
    attn_near = jnp.stack(attn_pieces)
    attn_w = attn_near, swap(attn_near, "dp", 1)
    ups = [jnp.stack([up_line, swap(up_line, "dp", 2)])]
    downs = [jnp.stack([down_line] + [swap(down_line, "dp", 4 * o) for o in range(1, outer // 2)])]
    ups += [swap(ups[0], "dp", 4 * o) for o in range(1, outer // 2)]
    downs += [swap(downs[0], "dp", 2)]
    plan = [(0, 0, (2 * o, 2 * o + 1)) for o in range(outer // 2)]
    plan += [(1, 0, tuple(range(first, outer, 2))) for first in range(2)]
    plan += [(part, 1, chips) for part, _, chips in plan]

    mixed, mixed_wide, total, q, k, v, prob = call(
        attend_kernel,
        [((nt, rows, TILE), BF16), ((nt, rows, TILE), F32), ((nt, rows, TILE), F32)]
        + [((nt, 2 * rows, TILE), BF16)] * 3
        + [((nt, 2 * rows // TILE, TILE, 2 * TILE), BF16)],
        [info, lengths],
        [normed_one, pooled, *attn_w, biases],
        scratch=[
            pltpu.VMEM((2 * rows // TILE, 1, 2 * TILE), F32),
            pltpu.VMEM((2, TILE, 2 * TILE), F32),
            pltpu.VMEM((rows, 3 * TILE), F32),
            pltpu.VMEM((2 * rows, 2 * TILE), F32),
            attn_full,
        ],
        limit=24,
        long=True,
    )
    ups, downs, mixed = lax.optimization_barrier((ups, downs, mixed))
    ffn_w = ups + downs
    ffn_w += [swap(each, "dp", 1) for each in ffn_w]
    piece = rows // dp
    hidden, normed_two, act, slope, out_near, out_far = call(
        functools.partial(feed_kernel, plan),
        [((rows, width), F32), ((rows, width), BF16)]
        + [((nt, rows, hid), BF16)] * 2
        + [((outer, piece, width), BF16)] * 2,
        [info],
        [own, mixed, *attn_w, *ffn_w]
        + [row(b_out), row(ln2_gain), row(ln2_bias), biases, row(b_down)],
        scratch=[pltpu.VMEM((rows, width), F32), attn_full, ffn_full],
        limit=28,
    )
    chunks = call(
        pair_kernel, [((2, piece, width), BF16)] * outer, [], [out_near, swap(out_far, "dp", 1)]
    )
    dy, chunks = lax.optimization_barrier((dy, chunks))

    grad_pre, grad_hidden, grad_hidden_low, numer, gtotal, sent, vec_two, vec_up = call(
        functools.partial(feed_back_kernel, plan),
        [
            ((nt, rows, hid), BF16),
            ((rows, width), F32),
            ((rows, width), BF16),
            ((nt, rows, TILE), F32),
            ((nt, rows, TILE), F32),
            ((nt, 2 * top, TILE), F32),
            ((4, width), F32),
            ((nt, 1, hid), F32),
        ],
        [info],
        [dy, *attn_w, *ffn_w, slope, hidden, row(ln2_gain), mixed_wide, total],
        scratch=[attn_full, ffn_full],
        limit=28,
    )
    swapped = swap(sent, "tensor", 1)
    chunks, grad_pre = lax.optimization_barrier(
        (jnp.concatenate(plane_pieces(chunks[0], chunks)), grad_pre)
    )
    chunks = line_first(chunks)
    ffn_grads = call(
        feed_grads_kernel,
        [((outer, nt, 2, chunk, hid), BF16)] * 2,
        [info],
        [normed_two, act, grad_pre, dy],
        scratch=[pltpu.VMEM((width, hid), BF16)] * 2,
    )
    ffn_far = swap(ffn_grads[1], "dp", 1)

    def core_sums(near, far):
        return [total_of([near[o], far[o]]) for o in range(outer)]

    def plane_parts(pieces):
        return [pieces[0]] + [swap(pieces[o], "dp", 2 * o) for o in range(1, outer)]

    ffn_parts = core_sums(ffn_grads[0], ffn_far)
    gtotal, ffn_parts, swapped = lax.optimization_barrier((gtotal, ffn_parts, swapped))
    ffn_parts = plane_parts(ffn_parts)
    qkv_grads, vec_qv, grad_low, vec_one = call(
        attend_back_kernel,
        [
            ((nt, rows, 3 * TILE), BF16),
            ((nt, 2, TILE), F32),
            ((rows, width), BF16),
            ((2, width), F32),
        ],
        [info, lengths],
        [numer, gtotal, swapped, q, k, v, prob, *attn_w]
        + [own, row(ln1_gain), grad_hidden],
        scratch=[
            pltpu.VMEM((rows, 2 * TILE), F32),
            pltpu.VMEM((2 * rows, 2 * TILE), BF16),
            pltpu.VMEM((2 * rows, 3 * TILE), F32),
            attn_full,
            pltpu.VMEM((rows, width), F32),
        ],
        limit=20,
        long=True,
    )
    chunks, grad_low, grad_hidden_low = lax.optimization_barrier(
        (chunks, grad_low, grad_hidden_low)
    )
    attn_near, attn_far = call(
        attend_grads_kernel,
        [((outer, nt * chunk + 16, 4 * TILE), BF16)] * 2,
        [info],
        [normed_one, qkv_grads, grad_hidden_low, mixed, vec_two, vec_up, vec_one, vec_qv],
        scratch=[pltpu.VMEM((width, 4 * TILE), BF16)],
    )
    row_pieces = line_first(grad_low)
    chunks = line_second(chunks)
    attn_far, ffn_parts = lax.optimization_barrier((attn_far, ffn_parts))
    attn_far = swap(attn_far, "dp", 1)
    attn_parts = plane_parts(core_sums(attn_near, attn_far))
    attn_parts, chunks, row_pieces[1] = lax.optimization_barrier(
        (attn_parts, chunks, row_pieces[1])
    )
    (dealt,) = call(
        deal_kernel,
        [((dp, seq_dev, nt // seq_dev, piece, width), BF16)],
        [info, dealing],
        chunks,
        scratch=[pltpu.VMEM((nt, dp, piece, width), BF16)],
    )
    dealt = exchange(dealt, "dp")
    attn_parts = total_of(attn_parts)
    attn_parts, row_pieces[2] = lax.optimization_barrier((attn_parts, row_pieces[2]))
    ffn_parts = total_of(ffn_parts)
    grads = [
        jnp.concatenate(
            [ffn_parts[z].reshape(2 * chunk, hid), attn_parts[z * chunk : (z + 1) * chunk]]
            + [attn_parts[nt * chunk :]]
        )
        for z in range(nt)
    ]
    grads = total_of([grads[0]] + [swap(grads[z], "tensor", z) for z in range(1, nt)])
    vectors = grads[3 * chunk :].astype(F32)
    grads, row_pieces = lax.optimization_barrier((grads, line_second(row_pieces)))
    near = jnp.stack(plane_pieces(grads[: 3 * chunk].reshape(3, chunk, width)))
    grads = near, swap(near, "dp", 1)
    g_up, g_down, g_query, g_key, g_value, g_out = call(
        place_grads_kernel,
        [((width, hid), F32), ((hid, width), F32)]
        + [((width, TILE), F32)] * 3
        + [((TILE, width), F32)],
        [info],
        grads,
        scratch=[pltpu.VMEM((width, TILE), F32)],
    )
    (grad_tokens,) = call(
        place_rows_kernel, [((nt, rows, width), BF16)], [info], row_pieces
    )
    grad_tokens = grad_tokens.reshape(seq_dev, length, width)
    (output,) = call(
        settle_kernel, [((seq_dev, nt // seq_dev, dp, piece, width), BF16)], [], [dealt]
    )
    output = output.reshape(seq_dev, length, width)
    base = 4 + nt
    g_b_up = lax.dynamic_index_in_dim(vectors[4:base], t, 0, keepdims=False)
    g_b_q = lax.dynamic_index_in_dim(vectors[base + 2].reshape(nt, TILE), t, 0, keepdims=False)
    g_b_v = lax.dynamic_index_in_dim(vectors[base + 3].reshape(nt, TILE), t, 0, keepdims=False)
    return (
        output,
        grad_tokens,
        vectors[base],
        vectors[base + 1],
        g_query,
        g_b_q,
        g_key,
        g_value,
        g_b_v,
        g_out,
        vectors[3],
        vectors[0],
        vectors[1],
        g_up,
        g_b_up,
        g_down,
        vectors[2],
    )


def solution(mesh):
    placed = (
        P("dp", None, None),
        P("dp", None, None),
        P(),
        P(),
        P(),
        P(),
        P(None, "tensor"),
        P("tensor"),
        P(None, "tensor"),
        P(None, "tensor"),
        P("tensor"),
        P("tensor", None),
        P(),
        P(),
        P(),
        P(None, "tensor"),
        P("tensor"),
        P("tensor", None),
        P(),
    )
    return jax.shard_map(
        local,
        mesh=mesh,
        in_specs=placed,
        out_specs=(
            P("dp", None, None),
            P("dp", None, None),
            P(),
            P(),
            P(None, "tensor"),
            P("tensor"),
            P(None, "tensor"),
            P(None, "tensor"),
            P("tensor"),
            P("tensor", None),
            P(),
            P(),
            P(),
            P(None, "tensor"),
            P("tensor"),
            P("tensor", None),
            P(),
        ),
        check_vma=False,
    )
```

```python
import functools

import jax
import jax.numpy as jnp
from jax import lax
from jax.experimental import pallas as pl
from jax.experimental.pallas import tpu as pltpu
from jax.sharding import PartitionSpec as P

F32 = jnp.float32
BF16 = jnp.bfloat16
HEAD_SIZE = 64
BLOCK = 16
TILE = 128
EPS = 1e-05
INV_ROOT_TWO = 0.7071067811865476
INV_ROOT_TAU = 0.3989422804014327
SCALE = HEAD_SIZE ** (-0.5)


def mm(left, right):
    return lax.dot_general(left, right, (((1,), (0,)), ((), ())), preferred_element_type=F32)


def mm_nt(left, right):
    return lax.dot_general(left, right, (((1,), (1,)), ((), ())), preferred_element_type=F32)


def mm_tn(left, right):
    return lax.dot_general(left, right, (((0,), (0,)), ((), ())), preferred_element_type=F32)


def split_low(values):
    high = values.astype(BF16)
    return high, (values - high.astype(F32)).astype(BF16)


def mm_wide(left, values):
    high, low = split_low(values)
    return mm(left, high) + mm(left, low)


def iota(shape, axis):
    return lax.broadcasted_iota(jnp.int32, shape, axis)


def unit_rows(values):
    centred = values - jnp.mean(values, axis=-1, keepdims=True)
    inverse = lax.rsqrt(jnp.mean(centred * centred, axis=-1, keepdims=True) + EPS)
    return centred * inverse, inverse


def norm_back(grad, unit, inverse, gain):
    scaled = grad * gain
    return inverse * (
        scaled
        - jnp.mean(scaled, axis=-1, keepdims=True)
        - unit * jnp.mean(scaled * unit, axis=-1, keepdims=True)
    )


def level_shifts(rows):
    shifts = []
    shift = 1
    while (2 * rows) >> shift >= 2 * BLOCK:
        shifts.append(shift)
        shift += 1
    return shifts


def coarse_map(index, rows):
    shifts = level_shifts(rows)
    shift = jnp.zeros_like(index)
    start = jnp.zeros_like(index)
    offset = 0
    for s in shifts:
        here = index >= offset
        shift = jnp.where(here, s, shift)
        start = jnp.where(here, offset, start)
        offset += rows >> s
    other = index >= offset
    start = jnp.where(other, offset, start)
    return shift, index - start, other


def coarse_counts(index, rows, length, own, partner):
    shift, place, other = coarse_map(index, rows)
    base = jnp.where(other, partner, own)
    left = length - base - lax.shift_left(place, shift)
    return jnp.clip(left, 0, lax.shift_left(jnp.ones_like(shift), shift)).astype(F32), shift


def tile_map(index):
    shift = jnp.zeros_like(index)
    start = jnp.zeros_like(index)
    offset = 0
    for s in range(1, 6):
        here = index >= offset
        shift = jnp.where(here, s, shift)
        start = jnp.where(here, offset, start)
        offset += TILE >> s
    return shift, index - start, index >= offset - (TILE >> 5)


def pool_tile(odd):
    shift, place, last = tile_map(iota((TILE, TILE), 0))
    place = jnp.where(last, place - odd * (TILE >> 5), place)
    hit = lax.shift_right_logical(iota((TILE, TILE), 1), shift) == place
    return hit.astype(F32).astype(BF16)


def spread_tile(odd):
    shift, place, last = tile_map(iota((TILE, TILE), 1))
    place = jnp.where(last, place - odd * (TILE >> 5), place)
    hit = lax.shift_right_logical(iota((TILE, TILE), 0), shift) == place
    return hit.astype(F32).astype(BF16)


def level_places(rows, tile):
    found = []
    local, offset = 0, 0
    for s in level_shifts(rows):
        count = TILE >> s
        found.append((local, count, offset + tile * count))
        local += count
        offset += rows >> s
    return found[:-1], found[-1]


def put_pooled(to_s, rows, tile, pooled):
    levels, (local, count, at) = level_places(rows, tile)
    for start, number, place in levels:
        to_s[place : place + number, :] = pooled[start : start + number]
    at -= (tile % 2) * count
    if tile % 2:
        to_s[at : at + 2 * count, :] += pooled[local : local + 2 * count]
    else:
        to_s[at : at + 2 * count, :] = pooled[local : local + 2 * count]


def take_local(from_s, base, rows, tile):
    levels, (local, count, at) = level_places(rows, tile)
    at -= (tile % 2) * count
    parts = [from_s[base + place : base + place + number, :] for _, number, place in levels]
    return jnp.concatenate(parts + [from_s[base + at : base + at + 2 * count, :]], axis=0)


def stacked_low(values):
    return jnp.concatenate(split_low(values), axis=0)


def top_pool(rows):
    shift = level_shifts(rows)[-1]
    count = rows >> shift
    hit = lax.shift_right_logical(iota((count, rows), 1), shift) == iota((count, rows), 0)
    return hit.astype(F32).astype(BF16)


def head_ones():
    second = (iota((TILE, TILE), 1) >= HEAD_SIZE).astype(F32)
    return (1.0 - second).astype(BF16), second.astype(BF16)


def two_heads(values, first, second):
    return jnp.concatenate([values * first, values * second], axis=0)


def stand(values):
    return jnp.concatenate([values[:, :TILE], values[:, TILE:]], axis=0)


def assemble(info, near_ref, far_ref, to_ref):
    core, plane, line = info[3], info[4], info[5]
    chunk = near_ref.shape[-2]
    for far, ref in enumerate((near_ref, far_ref)):
        for o in range(ref.shape[0]):
            at = ((o ^ plane) * 2 + (far ^ core)) * chunk
            at = pl.ds(pl.multiple_of(at, chunk), chunk)
            for z in range(ref.shape[1]):
                to_ref[z ^ line, at, :] = ref[o, z]


def assemble_feed(info, plan, refs, to_ref):
    core, plane = info[3], info[4]
    for (part, far, chips), ref in zip(plan, refs):
        chunk = ref.shape[-2]
        for i, o in enumerate(chips):
            at = ((o ^ plane) * 2 + (far ^ core)) * chunk
            at = pl.ds(pl.multiple_of(at, chunk), chunk)
            for z in range(ref.shape[1]):
                to_ref[z, part, at, :] = ref[i, z]


def pack_kernel(info, q_ref, k_ref, v_ref, o_ref, up_ref, down_ref, bq_ref, bv_ref, bu_ref, attn_ref, ffn_ref, turn_s):
    chunk = q_ref.shape[0]
    attn_ref[:chunk, 0 * TILE : 1 * TILE] = q_ref[...]
    attn_ref[:chunk, 1 * TILE : 2 * TILE] = k_ref[...]
    attn_ref[:chunk, 2 * TILE : 3 * TILE] = v_ref[...]
    turn_s[...] = o_ref[...].T
    at = pl.ds(pl.multiple_of((info[4] * 2 + info[3]) * chunk, chunk), chunk)
    attn_ref[:chunk, 3 * TILE :] = turn_s[at, :]
    ffn_ref[0] = up_ref[...]
    ffn_ref[1] = down_ref[...]
    lanes = bu_ref.shape[1]
    blank = jnp.zeros((1, lanes - 2 * TILE), F32)
    rest = jnp.concatenate(
        [bu_ref[...], jnp.concatenate([bq_ref[...], bv_ref[...], blank], axis=1)], axis=0
    )
    rows = []
    for _ in range(3):
        part = rest.astype(BF16).astype(F32)
        rows.append(part)
        rest = rest - part
    rows.append(jnp.zeros((10, lanes), F32))
    attn_ref[chunk:, :] = jnp.concatenate(rows, axis=0).astype(BF16)


def stack_kernel(*refs):
    *pieces, weight_ref, bias_ref = refs
    chunk = weight_ref.shape[1]
    for z, ref in enumerate(pieces):
        weight_ref[z] = ref[:chunk, :]
        bias_ref[z] = ref[chunk:, :]


def part_kernel(info, *refs):
    *pieces, up_ref, down_ref = refs
    for where, z, ref in line_sources(info[5], pieces):

        def put(z=z, ref=ref):
            up_ref[z] = ref[0]
            down_ref[z] = ref[1]

        put() if where is None else pl.when(where)(put)


def pair_kernel(near_ref, far_ref, *out_refs):
    for o, ref in enumerate(out_refs):
        ref[0] = near_ref[o]
        ref[1] = far_ref[o]


def bias_row(bias_ref, z, row):
    total = bias_ref[z, row : row + 1, :].astype(F32)
    for part in range(1, 3):
        at = 2 * part + row
        total = total + bias_ref[z, at : at + 1, :].astype(F32)
    return total


def norm_one_kernel(info, lengths, own_ref, other_ref, gain_ref, bias_ref, normed_ref, pooled_ref):
    rows = own_ref.shape[0]
    length, partner = lengths[info[0]], info[2]
    gain, bias = gain_ref[...], bias_ref[...]
    unit, _ = unit_rows(own_ref[...].astype(F32))
    normed_ref[...] = (unit * gain + bias).astype(BF16)
    unit, _ = unit_rows(other_ref[...].astype(F32))
    normed = (unit * gain + bias).astype(BF16)
    pool = top_pool(rows)
    count = pool.shape[0]
    live = (iota((1, rows), 1) + partner < length).astype(F32)
    pool_live = (pool.astype(F32) * live).astype(BF16)
    sums = mm(pool_live, normed)
    counts = jnp.sum(pool_live.astype(F32), axis=-1, keepdims=True)
    mean_live = sums / jnp.maximum(counts, 1.0)
    mean_all = mm(pool, normed) * (count / rows)
    high, low = split_low(mean_all)
    pooled_ref[0 * count : 1 * count, :] = high
    pooled_ref[1 * count : 2 * count, :] = low
    high, low = split_low(mean_live)
    pooled_ref[2 * count : 3 * count, :] = high
    pooled_ref[3 * count : 4 * count, :] = low


def attend_kernel(
    info,
    lengths,
    normed_ref,
    pooled_ref,
    near_ref,
    far_ref,
    bias_ref,
    mixed_ref,
    mixed_wide_ref,
    total_ref,
    q_ref,
    k_ref,
    v_ref,
    prob_ref,
    weight_s,
    mask_s,
    coarse_s,
    numer_s,
    full_s,
):
    rows = normed_ref.shape[0]
    pairs = q_ref.shape[0]
    tiles = 2 * rows // TILE
    half_tiles = rows // TILE
    length, own, partner = lengths[info[0]], info[1], info[2]
    line = info[5]
    assemble(info, near_ref, far_ref, full_s)
    pools = [pool_tile(odd) for odd in range(2)]
    spreads = [jnp.concatenate([spread_tile(odd)] * 2, axis=1) for odd in range(2)]
    lane = iota((1, 2 * TILE), 1) & (TILE - 1)
    for i in range(half_tiles):
        weight_s[i] = (lane + (own + i * TILE) < length).astype(F32)
        counts, _ = coarse_counts(lane + i * TILE, rows, length, own, partner)
        weight_s[half_tiles + i] = counts
    row_at = iota((TILE, 2 * TILE), 0)
    key_at = iota((TILE, 2 * TILE), 1) & (TILE - 1)
    pair_same = (row_at >> 5) == (key_at >> 5)
    apart = (row_at >> 4) != (key_at >> 4)
    mask_s[0] = pair_same.astype(F32)
    mask_s[1] = (pair_same & apart).astype(F32)
    live = (iota((rows, 1), 0) + own < length).astype(F32)
    counts, shift = coarse_counts(iota((rows, 1), 0), rows, length, own, partner)
    key_scale = 1.0 / jnp.maximum(counts, 1.0)
    query_scale = 1.0 / lax.shift_left(jnp.ones_like(shift), shift).astype(F32)
    top = pooled_ref.shape[0] // 4
    counts_other = counts[rows - top :]
    filled = counts_other / jnp.maximum(counts_other, 1.0)
    first, second = head_ones()

    def one_pair(p, carry):
        weight = full_s[p, :, : 3 * TILE]
        wide = mm(normed_ref[...], weight)
        biases = bias_row(bias_ref, p ^ line, 1)
        bq, bv = biases[:, :TILE], biases[:, TILE : 2 * TILE]
        query = (wide[:, :TILE] + bq).astype(BF16)
        key = (wide[:, TILE : 2 * TILE].astype(BF16).astype(F32) * live).astype(BF16)
        value = ((wide[:, 2 * TILE :] + bv).astype(BF16).astype(F32) * live).astype(BF16)
        extra = mm(pooled_ref[...], weight)
        q_other = extra[:top, :TILE] + extra[top : 2 * top, :TILE] + bq
        kv_other = extra[2 * top : 3 * top, TILE:] + extra[3 * top :, TILE:]
        k_other = kv_other[:, :TILE]
        v_other = kv_other[:, TILE:] + bv * filled
        q_ref[p, :rows, :] = query
        k_ref[p, :rows, :] = key
        v_ref[p, :rows, :] = value
        rows_all = jnp.concatenate([query, key, value], axis=1)
        for t in range(half_tiles):
            put_pooled(coarse_s, rows, t, mm(pools[t % 2], rows_all[t * TILE : (t + 1) * TILE]))
        q_ref[p, rows:, :] = (coarse_s[:, :TILE] * query_scale).astype(BF16)
        k_ref[p, rows:, :] = (coarse_s[:, TILE : 2 * TILE] * key_scale).astype(BF16)
        v_ref[p, rows:, :] = (coarse_s[:, 2 * TILE :] * key_scale).astype(BF16)
        q_ref[p, 2 * rows - top :, :] = q_other.astype(BF16)
        k_ref[p, 2 * rows - top :, :] = k_other.astype(BF16)
        v_ref[p, 2 * rows - top :, :] = v_other.astype(BF16)

        def one_tile(i, inner):
            at = pl.ds(pl.multiple_of(i * TILE, TILE), TILE)
            v = v_ref[p, at, :]
            score = mm_nt(q_ref[p, at, :], two_heads(k_ref[p, at, :], first, second)) * SCALE
            mask = mask_s[jnp.where(i >= half_tiles, 1, 0)]
            prob = jnp.where(mask > 0.0, jnp.exp(score) * weight_s[i], 0.0).astype(BF16)
            prob_ref[p, i] = prob
            values = jnp.concatenate(
                [
                    jnp.concatenate([v * first, first], axis=1),
                    jnp.concatenate([v * second, second], axis=1),
                ],
                axis=0,
            )
            numer_s[at, :] = mm(prob, values)
            return inner

        lax.fori_loop(0, tiles, one_tile, 0, unroll=4)
        for t in range(half_tiles):
            at = slice(t * TILE, (t + 1) * TILE)
            both = numer_s[at, :] + mm(
                spreads[t % 2], stacked_low(take_local(numer_s, rows, rows, t))
            )
            total = both[:, TILE:]
            mixed = both[:, :TILE] / total
            total_ref[p, at, :] = total
            mixed_wide_ref[p, at, :] = mixed
            mixed_ref[p, at, :] = mixed.astype(BF16)
        return carry

    lax.fori_loop(0, pairs, one_pair, 0)


def feed_kernel(plan, info, own_ref, mixed_ref, near_ref, far_ref, *refs):
    ffn_refs, refs = refs[: len(plan)], refs[len(plan) :]
    b_out_ref, gain_ref, shift_ref, bias_ref, b_down_ref, hidden_ref, normed_ref = refs[:7]
    act_ref, slope_ref, *out_refs, result_s, full_s, ffn_s = refs[7:]
    pairs = mixed_ref.shape[0]
    line = info[5]
    assemble(info, near_ref, far_ref, full_s)
    assemble_feed(info, plan, ffn_refs, ffn_s)
    hidden = own_ref[...].astype(F32) + b_out_ref[...]
    for p in range(pairs):
        hidden = hidden + mm_nt(mixed_ref[p], full_s[p, :, 3 * TILE :])
    hidden_ref[...] = hidden
    unit, _ = unit_rows(hidden)
    normed = (unit * gain_ref[...] + shift_ref[...]).astype(BF16)
    normed_ref[...] = normed
    result = hidden + b_down_ref[...]
    for z in range(pairs):
        pre = mm(normed, ffn_s[z, 0]) + bias_row(bias_ref, z ^ line, 0)
        half_erf = 0.5 + 0.5 * lax.erf(pre * INV_ROOT_TWO)
        act = (pre * half_erf).astype(BF16)
        act_ref[z] = act
        slope_ref[z] = (half_erf + pre * jnp.exp(-0.5 * pre * pre) * INV_ROOT_TAU).astype(BF16)
        result = result + mm(act, ffn_s[z, 1])
    result_s[...] = result
    chunk = out_refs[0].shape[1]
    for far, out_ref in enumerate(out_refs):
        for o in range(out_ref.shape[0]):
            at = ((o ^ info[4]) * 2 + (far ^ info[3])) * chunk
            out_ref[o] = result_s[pl.ds(pl.multiple_of(at, chunk), chunk), :].astype(BF16)


def feed_back_kernel(plan, info, dy_ref, near_ref, far_ref, *refs):
    ffn_refs, refs = refs[: len(plan)], refs[len(plan) :]
    slope_ref, hidden_ref, gain_ref, mixed_wide_ref, total_ref, grad_pre_ref, grad_hidden_ref = refs[:7]
    grad_hidden_low_ref, numer_ref, gtotal_ref, exchange_ref, vector_ref, b_up_ref = refs[7:13]
    full_s, ffn_s = refs[13:]
    rows = dy_ref.shape[0]
    assemble_feed(info, plan, ffn_refs, ffn_s)
    assemble(info, near_ref, far_ref, full_s)
    pairs = slope_ref.shape[0]
    dy = dy_ref[...]
    grad_normed = jnp.zeros((rows, dy.shape[1]), F32)
    for z in range(pairs):
        grad_act = mm_nt(dy, ffn_s[z, 1])
        grad_pre = (grad_act * slope_ref[z].astype(F32)).astype(BF16)
        grad_pre_ref[z] = grad_pre
        b_up_ref[z] = jnp.sum(grad_pre.astype(F32), axis=0, keepdims=True)
        grad_normed = grad_normed + mm_nt(grad_pre, ffn_s[z, 0])
    unit, inverse = unit_rows(hidden_ref[...])
    dy_wide = dy.astype(F32)
    vector_ref[0:1, :] = jnp.sum(grad_normed * unit, axis=0, keepdims=True)
    vector_ref[1:2, :] = jnp.sum(grad_normed, axis=0, keepdims=True)
    vector_ref[2:3, :] = jnp.sum(dy_wide, axis=0, keepdims=True)
    grad_hidden = dy_wide + norm_back(grad_normed, unit, inverse, gain_ref[...])
    vector_ref[3:4, :] = jnp.sum(grad_hidden, axis=0, keepdims=True)
    grad_hidden_ref[...] = grad_hidden
    low = grad_hidden.astype(BF16)
    grad_hidden_low_ref[...] = low
    pool = top_pool(rows)
    top = pool.shape[0]
    same = ((iota((TILE, TILE), 0) // HEAD_SIZE) == (iota((TILE, TILE), 1) // HEAD_SIZE)).astype(F32).astype(BF16)
    for p in range(pairs):
        grad_mixed = mm(low, full_s[p, :, 3 * TILE :]).astype(BF16).astype(F32)
        inv = 1.0 / total_ref[p]
        numer = grad_mixed * inv
        high, rest = split_low(grad_mixed * mixed_wide_ref[p])
        gtotal = -(mm(high, same) + mm(rest, same)) * inv
        numer_ref[p] = numer
        gtotal_ref[p] = gtotal
        exchange_ref[p, :top, :] = mm_wide(pool, numer)
        exchange_ref[p, top:, :] = mm_wide(pool, gtotal)


def give_out(info, near_ref, far_ref, z, part, values_s):
    core, plane = info[3], info[4]
    chunk = near_ref.shape[-2]
    for far, ref in enumerate((near_ref, far_ref)):
        for o in range(ref.shape[0]):
            at = ((o ^ plane) * 2 + (far ^ core)) * chunk
            ref[o, z, part] = values_s[pl.ds(pl.multiple_of(at, chunk), chunk), :]


def feed_grads_kernel(
    info, normed_ref, act_ref, grad_pre_ref, dy_ref, near_ref, far_ref, up_s, down_s
):
    line = info[5]
    for z in range(act_ref.shape[0]):
        up_s[...] = mm_tn(normed_ref[...], grad_pre_ref[z]).astype(BF16)
        give_out(info, near_ref, far_ref, z ^ line, 0, up_s)
        down_s[...] = mm_tn(act_ref[z], dy_ref[...]).astype(BF16)
        give_out(info, near_ref, far_ref, z ^ line, 1, down_s)


def attend_back_kernel(
    info,
    lengths,
    numer_ref,
    gtotal_ref,
    exchange_ref,
    q_ref,
    k_ref,
    v_ref,
    prob_ref,
    near_ref,
    far_ref,
    own_ref,
    gain_ref,
    grad_hidden_ref,
    grads_ref,
    b_qv_ref,
    grad_tokens_ref,
    vector_ref,
    coarse_s,
    left_s,
    grad_s,
    full_s,
    acc_s,
):
    pairs, rows = numer_ref.shape[0], numer_ref.shape[1]
    tiles = 2 * rows // TILE
    half_tiles = rows // TILE
    length, own, partner = lengths[info[0]], info[1], info[2]
    assemble(info, near_ref, far_ref, full_s)
    pools = [jnp.concatenate([pool_tile(odd)] * 2, axis=1) for odd in range(2)]
    spreads = [jnp.concatenate([spread_tile(odd)] * 2, axis=1) for odd in range(2)]
    live = (iota((rows, 1), 0) + own < length).astype(F32)
    counts, shift = coarse_counts(iota((rows, 1), 0), rows, length, own, partner)
    value_scale = 1.0 / jnp.maximum(counts, 1.0)
    query_scale = 1.0 / lax.shift_left(jnp.ones_like(shift), shift).astype(F32)
    first, second = head_ones()
    at_lane = iota((1, TILE), 1) & (HEAD_SIZE - 1)
    pick = (at_lane < 2).astype(F32)
    pick_first = (pick * first.astype(F32)).astype(BF16)
    pick_second = (pick * second.astype(F32)).astype(BF16)
    is_low = at_lane == 1
    top = exchange_ref.shape[1] // 2

    def two_parts(gtotal):
        high = gtotal.astype(BF16).astype(F32)
        return jnp.where(is_low, gtotal - high, high).astype(BF16)

    def one_pair(p, carry):
        for t in range(half_tiles):
            at = slice(t * TILE, (t + 1) * TILE)
            numer, gtotal = numer_ref[p, at, :], gtotal_ref[p, at, :]
            left_s[at, :TILE] = numer.astype(BF16)
            left_s[at, TILE:] = two_parts(gtotal)
            both = jnp.concatenate([numer, gtotal], axis=1)
            put_pooled(coarse_s, rows, t, mm(pools[t % 2], stacked_low(both)))
        coarse_s[rows - top :, :TILE] = exchange_ref[p, :top, :]
        coarse_s[rows - top :, TILE:] = exchange_ref[p, top:, :]
        left_s[rows:, :TILE] = coarse_s[:, :TILE].astype(BF16)
        left_s[rows:, TILE:] = two_parts(coarse_s[:, TILE:])

        def one_tile(i, inner):
            at = pl.ds(pl.multiple_of(i * TILE, TILE), TILE)
            v = v_ref[p, at, :]
            prob = prob_ref[p, i]
            left = left_s[at, :]
            right = jnp.concatenate(
                [
                    jnp.concatenate([v * first, pick_first], axis=1),
                    jnp.concatenate([v * second, pick_second], axis=1),
                ],
                axis=0,
            )
            grad_score = (mm_nt(left, right) * prob.astype(F32)).astype(BF16)
            grad_s[at, :TILE] = mm(grad_score, two_heads(k_ref[p, at, :], first, second))
            grad_s[at, TILE : 2 * TILE] = mm_tn(
                stand(grad_score), two_heads(q_ref[p, at, :], first, second)
            )
            grad_s[at, 2 * TILE :] = mm_tn(stand(prob), two_heads(left[:, :TILE], first, second))
            return inner

        lax.fori_loop(0, tiles, one_tile, 0, unroll=4)
        grad_s[rows:, :TILE] *= query_scale
        grad_s[rows:, TILE:] *= value_scale
        for t in range(half_tiles):
            at = slice(t * TILE, (t + 1) * TILE)
            fine = grad_s[at, :] + mm(
                spreads[t % 2], stacked_low(take_local(grad_s, rows, rows, t))
            )
            gq = (fine[:, :TILE] * SCALE).astype(BF16)
            gk = (fine[:, TILE : 2 * TILE] * (SCALE * live[at])).astype(BF16)
            gv = (fine[:, 2 * TILE :] * live[at]).astype(BF16)
            grads_ref[p, at, :] = jnp.concatenate([gq, gk, gv], axis=1)
        sums = jnp.sum(grads_ref[p].astype(F32), axis=0, keepdims=True)
        b_qv_ref[p, 0:1, :] = sums[:, :TILE]
        b_qv_ref[p, 1:2, :] = sums[:, 2 * TILE :]
        acc_s[...] += mm_nt(grads_ref[p], full_s[p, :, : 3 * TILE])
        return carry

    acc_s[...] = jnp.zeros_like(acc_s)
    lax.fori_loop(0, pairs, one_pair, 0)
    unit, inverse = unit_rows(own_ref[...].astype(F32))
    grad_normed = acc_s[...]
    vector_ref[0:1, :] = jnp.sum(grad_normed * unit, axis=0, keepdims=True)
    vector_ref[1:2, :] = jnp.sum(grad_normed, axis=0, keepdims=True)
    grad_tokens_ref[...] = (
        grad_hidden_ref[...] + norm_back(grad_normed, unit, inverse, gain_ref[...])
    ).astype(BF16)


def attend_grads_kernel(
    info,
    normed_ref,
    grads_ref,
    grad_hidden_ref,
    mixed_ref,
    vec_two_ref,
    vec_up_ref,
    vec_one_ref,
    b_qv_ref,
    near_ref,
    far_ref,
    both_s,
):
    core, plane, line = info[3], info[4], info[5]
    pairs = mixed_ref.shape[0]
    dp = 2 * near_ref.shape[0]
    chunk = both_s.shape[0] // dp
    for z in range(pairs):
        grads = grads_ref[z]
        both_s[:, : 3 * TILE] = mm_tn(normed_ref[...], grads).astype(BF16)
        both_s[:, 3 * TILE :] = mm_tn(grad_hidden_ref[...], mixed_ref[z]).astype(BF16)
        for far, ref in enumerate((near_ref, far_ref)):
            for o in range(ref.shape[0]):
                at = ((o ^ plane) * 2 + (far ^ core)) * chunk
                at = pl.ds(pl.multiple_of(at, chunk), chunk)
                to = pl.ds(pl.multiple_of((z ^ line) * chunk, chunk), chunk)
                ref[o, to, :] = both_s[at, :]
    vectors = [vec_two_ref[...]] + [vec_up_ref[z] for z in range(pairs)] + [vec_one_ref[...]]
    for row in range(2):
        parts = [b_qv_ref[p, row : row + 1, :] for p in range(pairs)]
        vectors.append(jnp.concatenate(parts, axis=1))
    vectors = jnp.concatenate(vectors, axis=0)
    blank = jnp.zeros((near_ref.shape[1] - pairs * chunk - vectors.shape[0], vectors.shape[1]), F32)
    vectors = jnp.concatenate([vectors, blank], axis=0).astype(BF16)
    for ref in (near_ref, far_ref):
        for o in range(ref.shape[0]):
            ref[o, pairs * chunk :, :] = vectors


def place_grads_kernel(info, near_ref, far_ref, up_ref, down_ref, q_ref, k_ref, v_ref, o_ref, turn_s):
    core, plane = info[3], info[4]
    chunk = near_ref.shape[-2]
    for far, ref in enumerate((near_ref, far_ref)):
        for o in range(ref.shape[0]):
            at = ((o ^ plane) * 2 + (far ^ core)) * chunk
            at = pl.ds(pl.multiple_of(at, chunk), chunk)
            up_ref[at, :] = ref[o, 0].astype(F32)
            down_ref[at, :] = ref[o, 1].astype(F32)
            rest = ref[o, 2].astype(F32)
            q_ref[at, :] = rest[:, :TILE]
            k_ref[at, :] = rest[:, TILE : 2 * TILE]
            v_ref[at, :] = rest[:, 2 * TILE : 3 * TILE]
            turn_s[at, :] = rest[:, 3 * TILE :]
    o_ref[...] = turn_s[...].T


def line_sources(line, refs):
    own, one, two, three, passed = refs
    middle = (line == 1) | (line == 2)
    return [
        (None, line, own),
        (None, line ^ 1, one),
        (None, line ^ 2, two),
        (middle, line ^ 3, three),
        (jnp.logical_not(middle), line ^ 3, passed),
    ]


def gather_line(line, refs, to_ref):
    for where, z, ref in line_sources(line, refs):

        def put(z=z, ref=ref):
            to_ref[z] = ref[...]

        put() if where is None else pl.when(where)(put)


def place_rows_kernel(info, *refs):
    gather_line(info[5], refs[:-1], refs[-1])


def deal_kernel(info, dealing, *refs):
    *pieces, out_ref, all_s = refs
    gather_line(info[5], pieces, all_s)
    own = info[4] * 2 + info[3]
    for i in range(out_ref.shape[0]):
        for slot in range(out_ref.shape[1]):
            seq = dealing[i * out_ref.shape[1] + slot]
            for half in range(out_ref.shape[2]):
                out_ref[i, slot, half] = all_s[(seq & 1) * 2 + half, (seq >> 1) ^ own]


def settle_kernel(pieces_ref, out_ref):
    dps, slots, halves = pieces_ref.shape[:3]
    for i in range(dps):
        for slot in range(slots):
            for half in range(halves):
                out_ref[slot, half, i] = pieces_ref[i, slot, half]


VMEM_SPEC = pl.BlockSpec(memory_space=pltpu.VMEM)
SMEM_SPEC = pl.BlockSpec(memory_space=pltpu.SMEM)


def call(kernel, outs, scalars, args, scratch=(), limit=16, long=False):
    return pl.pallas_call(
        kernel,
        out_shape=[jax.ShapeDtypeStruct(shape, dtype) for shape, dtype in outs],
        in_specs=[SMEM_SPEC] * len(scalars) + [VMEM_SPEC] * len(args),
        out_specs=[VMEM_SPEC] * len(outs),
        scratch_shapes=list(scratch),
        compiler_params=pltpu.CompilerParams(vmem_limit_bytes=limit << 20),
        cost_estimate=pl.CostEstimate(
            flops=10**10 if long else 1, transcendentals=0, bytes_accessed=1
        ),
    )(*scalars, *args)


def exchange(pieces, axis, groups=None):
    return lax.all_to_all(pieces, axis, 0, 0, tiled=True, axis_index_groups=groups)


def gather(piece, axis, count):
    return exchange(jnp.broadcast_to(piece[None], (count,) + piece.shape), axis)


def swap(piece, axis, distance):
    size = lax.axis_size(axis)
    return lax.ppermute(piece, axis, [(i, i ^ distance) for i in range(size)])


def after(value, *others):
    return lax.optimization_barrier((value, others))[0]


def total_of(pieces):
    return functools.reduce(jnp.add, [piece.astype(F32) for piece in pieces]).astype(BF16)


def local(
    tokens,
    cotangent,
    lengths,
    dealing,
    ln1_gain,
    ln1_bias,
    w_query,
    b_query,
    w_key,
    w_value,
    b_value,
    w_out,
    b_out,
    ln2_gain,
    ln2_bias,
    w_up,
    b_up,
    w_down,
    b_down,
):
    seq_dev, length, width = tokens.shape
    dp = lax.axis_size("dp")
    nt = lax.axis_size("tensor")
    d = lax.axis_index("dp")
    t = lax.axis_index("tensor")
    rows = seq_dev * length // nt
    outer = dp // 2
    planes = [[2 * o + c for o in range(outer)] for c in range(2)]
    chunk = width // dp
    hid = w_up.shape[1]

    def near_line(piece):
        return [piece] + [swap(piece, "tensor", z) for z in range(1, nt)]

    def line_first(piece):
        return [piece, swap(piece, "tensor", 1), swap(piece, "tensor", 2)]

    def line_second(pieces):
        piece, one, two = pieces
        three = lax.ppermute(after(piece, two), "tensor", [(1, 2), (2, 1)])
        passed = lax.ppermute(two, "tensor", [(1, 0), (2, 3)])
        return [piece, one, two, three, passed]

    def plane_pieces(piece, others=None):
        return [piece] + [swap(others[o] if others else piece, "dp", 2 * o) for o in range(1, outer)]

    own_base = (t % 2) * rows
    info = jnp.stack([d * seq_dev + t // 2, own_base, rows - own_base, d % 2, d // 2, t])
    row = lambda v: v.reshape(1, -1)

    slice_spec = lambda lanes: pl.BlockSpec((chunk, lanes), lambda i, info: (info[4] * 2 + info[3], 0))
    whole_spec = lambda shape: pl.BlockSpec(shape, lambda i, info: (0,) * len(shape))
    attn_piece, ffn_piece = pl.pallas_call(
        pack_kernel,
        out_shape=[
            jax.ShapeDtypeStruct((chunk + 16, 4 * TILE), BF16),
            jax.ShapeDtypeStruct((2, chunk, hid), BF16),
        ],
        grid_spec=pltpu.PrefetchScalarGridSpec(
            num_scalar_prefetch=1,
            grid=(1,),
            in_specs=[slice_spec(TILE)] * 3
            + [whole_spec((TILE, width)), slice_spec(hid), slice_spec(width)]
            + [whole_spec((1, TILE)), whole_spec((1, TILE)), whole_spec((1, hid))],
            out_specs=[whole_spec((chunk + 16, 4 * TILE)), whole_spec((2, chunk, hid))],
            scratch_shapes=[pltpu.VMEM((width, TILE), BF16)],
        ),
    )(info, w_query, w_key, w_value, w_out, w_up, w_down, row(b_query), row(b_value), row(b_up))
    halves = tokens.reshape(nt, rows, width)
    own = lax.dynamic_index_in_dim(halves, t, 0, keepdims=False)
    other = lax.dynamic_index_in_dim(halves, t ^ 1, 0, keepdims=False)
    dy = lax.dynamic_index_in_dim(cotangent.reshape(nt, rows, width), t, 0, keepdims=False)
    top = rows >> level_shifts(rows)[-1]

    attn_full = pltpu.VMEM((nt, width, 4 * TILE), BF16)
    ffn_full = pltpu.VMEM((nt, 2, width, hid), BF16)

    normed_one, pooled = call(
        norm_one_kernel,
        [((rows, width), BF16), ((4 * top, width), BF16)],
        [info, lengths],
        [own, other, row(ln1_gain), row(ln1_bias)],
    )
    attn_line = near_line(attn_piece)
    normed_one, *attn_line = lax.optimization_barrier((normed_one, *attn_line))
    biases = jnp.stack([piece[chunk:] for piece in attn_line])
    ffn_line = line_first(after(ffn_piece, attn_line[1]))
    attn_line, biases = call(
        stack_kernel,
        [((nt, chunk, 4 * TILE), BF16), ((nt, 16, 4 * TILE), BF16)],
        [],
        attn_line,
    )
    attn_pieces = plane_pieces(attn_line)
    up_line, down_line = call(
        part_kernel, [((nt, chunk, hid), BF16)] * 2, [info], line_second(ffn_line)
    )
    attn_pieces, up_line, down_line = lax.optimization_barrier((attn_pieces, up_line, down_line))
    attn_near = jnp.stack(attn_pieces)
    attn_w = attn_near, swap(attn_near, "dp", 1)
    ups = [jnp.stack([up_line, swap(up_line, "dp", 2)])]
    downs = [jnp.stack([down_line] + [swap(down_line, "dp", 4 * o) for o in range(1, outer // 2)])]
    ups += [swap(ups[0], "dp", 4 * o) for o in range(1, outer // 2)]
    downs += [swap(downs[0], "dp", 2)]
    plan = [(0, 0, (2 * o, 2 * o + 1)) for o in range(outer // 2)]
    plan += [(1, 0, tuple(range(first, outer, 2))) for first in range(2)]
    plan += [(part, 1, chips) for part, _, chips in plan]

    mixed, mixed_wide, total, q, k, v, prob = call(
        attend_kernel,
        [((nt, rows, TILE), BF16), ((nt, rows, TILE), F32), ((nt, rows, TILE), F32)]
        + [((nt, 2 * rows, TILE), BF16)] * 3
        + [((nt, 2 * rows // TILE, TILE, 2 * TILE), BF16)],
        [info, lengths],
        [normed_one, pooled, *attn_w, biases],
        scratch=[
            pltpu.VMEM((2 * rows // TILE, 1, 2 * TILE), F32),
            pltpu.VMEM((2, TILE, 2 * TILE), F32),
            pltpu.VMEM((rows, 3 * TILE), F32),
            pltpu.VMEM((2 * rows, 2 * TILE), F32),
            attn_full,
        ],
        limit=24,
        long=True,
    )
    ups, downs, mixed = lax.optimization_barrier((ups, downs, mixed))
    ffn_w = ups + downs
    ffn_w += [swap(each, "dp", 1) for each in ffn_w]
    piece = rows // dp
    hidden, normed_two, act, slope, out_near, out_far = call(
        functools.partial(feed_kernel, plan),
        [((rows, width), F32), ((rows, width), BF16)]
        + [((nt, rows, hid), BF16)] * 2
        + [((outer, piece, width), BF16)] * 2,
        [info],
        [own, mixed, *attn_w, *ffn_w]
        + [row(b_out), row(ln2_gain), row(ln2_bias), biases, row(b_down)],
        scratch=[pltpu.VMEM((rows, width), F32), attn_full, ffn_full],
        limit=28,
    )
    chunks = call(
        pair_kernel, [((2, piece, width), BF16)] * outer, [], [out_near, swap(out_far, "dp", 1)]
    )
    dy, chunks = lax.optimization_barrier((dy, chunks))

    grad_pre, grad_hidden, grad_hidden_low, numer, gtotal, sent, vec_two, vec_up = call(
        functools.partial(feed_back_kernel, plan),
        [
            ((nt, rows, hid), BF16),
            ((rows, width), F32),
            ((rows, width), BF16),
            ((nt, rows, TILE), F32),
            ((nt, rows, TILE), F32),
            ((nt, 2 * top, TILE), F32),
            ((4, width), F32),
            ((nt, 1, hid), F32),
        ],
        [info],
        [dy, *attn_w, *ffn_w, slope, hidden, row(ln2_gain), mixed_wide, total],
        scratch=[attn_full, ffn_full],
        limit=28,
    )
    swapped = swap(sent, "tensor", 1)
    chunks, grad_pre = lax.optimization_barrier(
        (jnp.concatenate(plane_pieces(chunks[0], chunks)), grad_pre)
    )
    chunks = line_first(chunks)
    ffn_grads = call(
        feed_grads_kernel,
        [((outer, nt, 2, chunk, hid), BF16)] * 2,
        [info],
        [normed_two, act, grad_pre, dy],
        scratch=[pltpu.VMEM((width, hid), BF16)] * 2,
    )
    ffn_far = swap(ffn_grads[1], "dp", 1)

    def core_sums(near, far):
        return [total_of([near[o], far[o]]) for o in range(outer)]

    def plane_parts(pieces):
        return [pieces[0]] + [swap(pieces[o], "dp", 2 * o) for o in range(1, outer)]

    ffn_parts = core_sums(ffn_grads[0], ffn_far)
    gtotal, ffn_parts, swapped = lax.optimization_barrier((gtotal, ffn_parts, swapped))
    ffn_parts = plane_parts(ffn_parts)
    qkv_grads, vec_qv, grad_low, vec_one = call(
        attend_back_kernel,
        [
            ((nt, rows, 3 * TILE), BF16),
            ((nt, 2, TILE), F32),
            ((rows, width), BF16),
            ((2, width), F32),
        ],
        [info, lengths],
        [numer, gtotal, swapped, q, k, v, prob, *attn_w]
        + [own, row(ln1_gain), grad_hidden],
        scratch=[
            pltpu.VMEM((rows, 2 * TILE), F32),
            pltpu.VMEM((2 * rows, 2 * TILE), BF16),
            pltpu.VMEM((2 * rows, 3 * TILE), F32),
            attn_full,
            pltpu.VMEM((rows, width), F32),
        ],
        limit=20,
        long=True,
    )
    chunks, grad_low, grad_hidden_low = lax.optimization_barrier(
        (chunks, grad_low, grad_hidden_low)
    )
    attn_near, attn_far = call(
        attend_grads_kernel,
        [((outer, nt * chunk + 16, 4 * TILE), BF16)] * 2,
        [info],
        [normed_one, qkv_grads, grad_hidden_low, mixed, vec_two, vec_up, vec_one, vec_qv],
        scratch=[pltpu.VMEM((width, 4 * TILE), BF16)],
    )
    row_pieces = line_first(grad_low)
    chunks = line_second(chunks)
    attn_far, ffn_parts = lax.optimization_barrier((attn_far, ffn_parts))
    attn_far = swap(attn_far, "dp", 1)
    attn_parts = plane_parts(core_sums(attn_near, attn_far))
    attn_parts, chunks, row_pieces[1] = lax.optimization_barrier(
        (attn_parts, chunks, row_pieces[1])
    )
    (dealt,) = call(
        deal_kernel,
        [((dp, seq_dev, nt // seq_dev, piece, width), BF16)],
        [info, dealing],
        chunks,
        scratch=[pltpu.VMEM((nt, dp, piece, width), BF16)],
    )
    dealt = exchange(dealt, "dp")
    attn_parts = total_of(attn_parts)
    attn_parts, row_pieces[2] = lax.optimization_barrier((attn_parts, row_pieces[2]))
    ffn_parts = total_of(ffn_parts)
    grads = [
        jnp.concatenate(
            [ffn_parts[z].reshape(2 * chunk, hid), attn_parts[z * chunk : (z + 1) * chunk]]
            + [attn_parts[nt * chunk :]]
        )
        for z in range(nt)
    ]
    grads = total_of([grads[0]] + [swap(grads[z], "tensor", z) for z in range(1, nt)])
    vectors = grads[3 * chunk :].astype(F32)
    row_pieces = line_second(row_pieces)
    near = jnp.stack(plane_pieces(grads[: 3 * chunk].reshape(3, chunk, width)))
    (grad_tokens,) = call(
        place_rows_kernel, [((nt, rows, width), BF16)], [info], row_pieces
    )
    grad_tokens = grad_tokens.reshape(seq_dev, length, width)
    (output,) = call(
        settle_kernel, [((seq_dev, nt // seq_dev, dp, piece, width), BF16)], [], [dealt]
    )
    output = output.reshape(seq_dev, length, width)
    near, output, grad_tokens, vectors = lax.optimization_barrier(
        (near, output, grad_tokens, vectors)
    )
    grads = near, swap(near, "dp", 1)
    g_up, g_down, g_query, g_key, g_value, g_out = call(
        place_grads_kernel,
        [((width, hid), F32), ((hid, width), F32)]
        + [((width, TILE), F32)] * 3
        + [((TILE, width), F32)],
        [info],
        grads,
        scratch=[pltpu.VMEM((width, TILE), F32)],
    )
    base = 4 + nt
    g_b_up = lax.dynamic_index_in_dim(vectors[4:base], t, 0, keepdims=False)
    g_b_q = lax.dynamic_index_in_dim(vectors[base + 2].reshape(nt, TILE), t, 0, keepdims=False)
    g_b_v = lax.dynamic_index_in_dim(vectors[base + 3].reshape(nt, TILE), t, 0, keepdims=False)
    return (
        output,
        grad_tokens,
        vectors[base],
        vectors[base + 1],
        g_query,
        g_b_q,
        g_key,
        g_value,
        g_b_v,
        g_out,
        vectors[3],
        vectors[0],
        vectors[1],
        g_up,
        g_b_up,
        g_down,
        vectors[2],
    )


def solution(mesh):
    placed = (
        P("dp", None, None),
        P("dp", None, None),
        P(),
        P(),
        P(),
        P(),
        P(None, "tensor"),
        P("tensor"),
        P(None, "tensor"),
        P(None, "tensor"),
        P("tensor"),
        P("tensor", None),
        P(),
        P(),
        P(),
        P(None, "tensor"),
        P("tensor"),
        P("tensor", None),
        P(),
    )
    return jax.shard_map(
        local,
        mesh=mesh,
        in_specs=placed,
        out_specs=(
            P("dp", None, None),
            P("dp", None, None),
            P(),
            P(),
            P(None, "tensor"),
            P("tensor"),
            P(None, "tensor"),
            P(None, "tensor"),
            P("tensor"),
            P("tensor", None),
            P(),
            P(),
            P(),
            P(None, "tensor"),
            P("tensor"),
            P("tensor", None),
            P(),
        ),
        check_vma=False,
    )
```

```python
import functools

import jax
import jax.numpy as jnp
from jax import lax
from jax.experimental import pallas as pl
from jax.experimental.pallas import tpu as pltpu
from jax.sharding import PartitionSpec as P

F32 = jnp.float32
BF16 = jnp.bfloat16
HEAD_SIZE = 64
BLOCK = 16
TILE = 128
EPS = 1e-05
INV_ROOT_TWO = 0.7071067811865476
INV_ROOT_TAU = 0.3989422804014327
SCALE = HEAD_SIZE ** (-0.5)


def mm(left, right):
    return lax.dot_general(left, right, (((1,), (0,)), ((), ())), preferred_element_type=F32)


def mm_nt(left, right):
    return lax.dot_general(left, right, (((1,), (1,)), ((), ())), preferred_element_type=F32)


def mm_tn(left, right):
    return lax.dot_general(left, right, (((0,), (0,)), ((), ())), preferred_element_type=F32)


def split_low(values):
    high = values.astype(BF16)
    return high, (values - high.astype(F32)).astype(BF16)


def mm_wide(left, values):
    high, low = split_low(values)
    return mm(left, high) + mm(left, low)


def iota(shape, axis):
    return lax.broadcasted_iota(jnp.int32, shape, axis)


def unit_rows(values):
    centred = values - jnp.mean(values, axis=-1, keepdims=True)
    inverse = lax.rsqrt(jnp.mean(centred * centred, axis=-1, keepdims=True) + EPS)
    return centred * inverse, inverse


def norm_back(grad, unit, inverse, gain):
    scaled = grad * gain
    return inverse * (
        scaled
        - jnp.mean(scaled, axis=-1, keepdims=True)
        - unit * jnp.mean(scaled * unit, axis=-1, keepdims=True)
    )


def level_shifts(rows):
    shifts = []
    shift = 1
    while (2 * rows) >> shift >= 2 * BLOCK:
        shifts.append(shift)
        shift += 1
    return shifts


def coarse_map(index, rows):
    shifts = level_shifts(rows)
    shift = jnp.zeros_like(index)
    start = jnp.zeros_like(index)
    offset = 0
    for s in shifts:
        here = index >= offset
        shift = jnp.where(here, s, shift)
        start = jnp.where(here, offset, start)
        offset += rows >> s
    other = index >= offset
    start = jnp.where(other, offset, start)
    return shift, index - start, other


def coarse_counts(index, rows, length, own, partner):
    shift, place, other = coarse_map(index, rows)
    base = jnp.where(other, partner, own)
    left = length - base - lax.shift_left(place, shift)
    return jnp.clip(left, 0, lax.shift_left(jnp.ones_like(shift), shift)).astype(F32), shift


def tile_map(index):
    shift = jnp.zeros_like(index)
    start = jnp.zeros_like(index)
    offset = 0
    for s in range(1, 6):
        here = index >= offset
        shift = jnp.where(here, s, shift)
        start = jnp.where(here, offset, start)
        offset += TILE >> s
    return shift, index - start, index >= offset - (TILE >> 5)


def pool_tile(odd):
    shift, place, last = tile_map(iota((TILE, TILE), 0))
    place = jnp.where(last, place - odd * (TILE >> 5), place)
    hit = lax.shift_right_logical(iota((TILE, TILE), 1), shift) == place
    return hit.astype(F32).astype(BF16)


def spread_tile(odd):
    shift, place, last = tile_map(iota((TILE, TILE), 1))
    place = jnp.where(last, place - odd * (TILE >> 5), place)
    hit = lax.shift_right_logical(iota((TILE, TILE), 0), shift) == place
    return hit.astype(F32).astype(BF16)


def level_places(rows, tile):
    found = []
    local, offset = 0, 0
    for s in level_shifts(rows):
        count = TILE >> s
        found.append((local, count, offset + tile * count))
        local += count
        offset += rows >> s
    return found[:-1], found[-1]


def put_pooled(to_s, rows, tile, pooled):
    levels, (local, count, at) = level_places(rows, tile)
    for start, number, place in levels:
        to_s[place : place + number, :] = pooled[start : start + number]
    at -= (tile % 2) * count
    if tile % 2:
        to_s[at : at + 2 * count, :] += pooled[local : local + 2 * count]
    else:
        to_s[at : at + 2 * count, :] = pooled[local : local + 2 * count]


def take_local(from_s, base, rows, tile):
    levels, (local, count, at) = level_places(rows, tile)
    at -= (tile % 2) * count
    parts = [from_s[base + place : base + place + number, :] for _, number, place in levels]
    return jnp.concatenate(parts + [from_s[base + at : base + at + 2 * count, :]], axis=0)


def stacked_low(values):
    return jnp.concatenate(split_low(values), axis=0)


def top_pool(rows):
    shift = level_shifts(rows)[-1]
    count = rows >> shift
    hit = lax.shift_right_logical(iota((count, rows), 1), shift) == iota((count, rows), 0)
    return hit.astype(F32).astype(BF16)


def head_ones():
    second = (iota((TILE, TILE), 1) >= HEAD_SIZE).astype(F32)
    return (1.0 - second).astype(BF16), second.astype(BF16)


def two_heads(values, first, second):
    return jnp.concatenate([values * first, values * second], axis=0)


def stand(values):
    return jnp.concatenate([values[:, :TILE], values[:, TILE:]], axis=0)


def assemble(info, near_ref, far_ref, to_ref):
    core, plane, line = info[3], info[4], info[5]
    chunk = near_ref.shape[-2]
    for far, ref in enumerate((near_ref, far_ref)):
        for o in range(ref.shape[0]):
            at = ((o ^ plane) * 2 + (far ^ core)) * chunk
            at = pl.ds(pl.multiple_of(at, chunk), chunk)
            for z in range(ref.shape[1]):
                to_ref[z ^ line, at, :] = ref[o, z]


def assemble_feed(info, plan, refs, to_ref):
    core, plane = info[3], info[4]
    for (part, far, chips), ref in zip(plan, refs):
        chunk = ref.shape[-2]
        for i, o in enumerate(chips):
            at = ((o ^ plane) * 2 + (far ^ core)) * chunk
            at = pl.ds(pl.multiple_of(at, chunk), chunk)
            for z in range(ref.shape[1]):
                to_ref[z, part, at, :] = ref[i, z]


def pack_kernel(info, q_ref, k_ref, v_ref, o_ref, up_ref, down_ref, bq_ref, bv_ref, bu_ref, attn_ref, ffn_ref, turn_s):
    chunk = q_ref.shape[0]
    attn_ref[:chunk, 0 * TILE : 1 * TILE] = q_ref[...]
    attn_ref[:chunk, 1 * TILE : 2 * TILE] = k_ref[...]
    attn_ref[:chunk, 2 * TILE : 3 * TILE] = v_ref[...]
    turn_s[...] = o_ref[...].T
    at = pl.ds(pl.multiple_of((info[4] * 2 + info[3]) * chunk, chunk), chunk)
    attn_ref[:chunk, 3 * TILE :] = turn_s[at, :]
    ffn_ref[0] = up_ref[...]
    ffn_ref[1] = down_ref[...]
    lanes = bu_ref.shape[1]
    blank = jnp.zeros((1, lanes - 2 * TILE), F32)
    rest = jnp.concatenate(
        [bu_ref[...], jnp.concatenate([bq_ref[...], bv_ref[...], blank], axis=1)], axis=0
    )
    rows = []
    for _ in range(3):
        part = rest.astype(BF16).astype(F32)
        rows.append(part)
        rest = rest - part
    rows.append(jnp.zeros((10, lanes), F32))
    attn_ref[chunk:, :] = jnp.concatenate(rows, axis=0).astype(BF16)


def stack_kernel(*refs):
    *pieces, weight_ref, bias_ref = refs
    chunk = weight_ref.shape[1]
    for z, ref in enumerate(pieces):
        weight_ref[z] = ref[:chunk, :]
        bias_ref[z] = ref[chunk:, :]


def part_kernel(info, *refs):
    *pieces, up_ref, down_ref = refs
    for where, z, ref in line_sources(info[5], pieces):

        def put(z=z, ref=ref):
            up_ref[z] = ref[0]
            down_ref[z] = ref[1]

        put() if where is None else pl.when(where)(put)


def pair_kernel(near_ref, far_ref, *out_refs):
    for o, ref in enumerate(out_refs):
        ref[0] = near_ref[o]
        ref[1] = far_ref[o]


def bias_row(bias_ref, z, row):
    total = bias_ref[z, row : row + 1, :].astype(F32)
    for part in range(1, 3):
        at = 2 * part + row
        total = total + bias_ref[z, at : at + 1, :].astype(F32)
    return total


def norm_one_kernel(info, lengths, own_ref, other_ref, gain_ref, bias_ref, normed_ref, pooled_ref):
    rows = own_ref.shape[0]
    length, partner = lengths[info[0]], info[2]
    gain, bias = gain_ref[...], bias_ref[...]
    unit, _ = unit_rows(own_ref[...].astype(F32))
    normed_ref[...] = (unit * gain + bias).astype(BF16)
    unit, _ = unit_rows(other_ref[...].astype(F32))
    normed = (unit * gain + bias).astype(BF16)
    pool = top_pool(rows)
    count = pool.shape[0]
    live = (iota((1, rows), 1) + partner < length).astype(F32)
    pool_live = (pool.astype(F32) * live).astype(BF16)
    sums = mm(pool_live, normed)
    counts = jnp.sum(pool_live.astype(F32), axis=-1, keepdims=True)
    mean_live = sums / jnp.maximum(counts, 1.0)
    mean_all = mm(pool, normed) * (count / rows)
    high, low = split_low(mean_all)
    pooled_ref[0 * count : 1 * count, :] = high
    pooled_ref[1 * count : 2 * count, :] = low
    high, low = split_low(mean_live)
    pooled_ref[2 * count : 3 * count, :] = high
    pooled_ref[3 * count : 4 * count, :] = low


def attend_kernel(
    info,
    lengths,
    normed_ref,
    pooled_ref,
    near_ref,
    far_ref,
    bias_ref,
    mixed_ref,
    mixed_wide_ref,
    total_ref,
    q_ref,
    k_ref,
    v_ref,
    prob_ref,
    full_s,
    weight_s,
    mask_s,
    coarse_s,
    numer_s,
):
    rows = normed_ref.shape[0]
    pairs = q_ref.shape[0]
    tiles = 2 * rows // TILE
    half_tiles = rows // TILE
    length, own, partner = lengths[info[0]], info[1], info[2]
    line = info[5]
    assemble(info, near_ref, far_ref, full_s)
    pools = [pool_tile(odd) for odd in range(2)]
    spreads = [jnp.concatenate([spread_tile(odd)] * 2, axis=1) for odd in range(2)]
    lane = iota((1, 2 * TILE), 1) & (TILE - 1)
    for i in range(half_tiles):
        weight_s[i] = (lane + (own + i * TILE) < length).astype(F32)
        counts, _ = coarse_counts(lane + i * TILE, rows, length, own, partner)
        weight_s[half_tiles + i] = counts
    row_at = iota((TILE, 2 * TILE), 0)
    key_at = iota((TILE, 2 * TILE), 1) & (TILE - 1)
    pair_same = (row_at >> 5) == (key_at >> 5)
    apart = (row_at >> 4) != (key_at >> 4)
    mask_s[0] = pair_same.astype(F32)
    mask_s[1] = (pair_same & apart).astype(F32)
    live = (iota((rows, 1), 0) + own < length).astype(F32)
    counts, shift = coarse_counts(iota((rows, 1), 0), rows, length, own, partner)
    key_scale = 1.0 / jnp.maximum(counts, 1.0)
    query_scale = 1.0 / lax.shift_left(jnp.ones_like(shift), shift).astype(F32)
    top = pooled_ref.shape[0] // 4
    counts_other = counts[rows - top :]
    filled = counts_other / jnp.maximum(counts_other, 1.0)
    first, second = head_ones()

    def one_pair(p, carry):
        weight = full_s[p, :, : 3 * TILE]
        wide = mm(normed_ref[...], weight)
        biases = bias_row(bias_ref, p ^ line, 1)
        bq, bv = biases[:, :TILE], biases[:, TILE : 2 * TILE]
        query = (wide[:, :TILE] + bq).astype(BF16)
        key = (wide[:, TILE : 2 * TILE].astype(BF16).astype(F32) * live).astype(BF16)
        value = ((wide[:, 2 * TILE :] + bv).astype(BF16).astype(F32) * live).astype(BF16)
        extra = mm(pooled_ref[...], weight)
        q_other = extra[:top, :TILE] + extra[top : 2 * top, :TILE] + bq
        kv_other = extra[2 * top : 3 * top, TILE:] + extra[3 * top :, TILE:]
        k_other = kv_other[:, :TILE]
        v_other = kv_other[:, TILE:] + bv * filled
        q_ref[p, :rows, :] = query
        k_ref[p, :rows, :] = key
        v_ref[p, :rows, :] = value
        rows_all = jnp.concatenate([query, key, value], axis=1)
        for t in range(half_tiles):
            put_pooled(coarse_s, rows, t, mm(pools[t % 2], rows_all[t * TILE : (t + 1) * TILE]))
        q_ref[p, rows:, :] = (coarse_s[:, :TILE] * query_scale).astype(BF16)
        k_ref[p, rows:, :] = (coarse_s[:, TILE : 2 * TILE] * key_scale).astype(BF16)
        v_ref[p, rows:, :] = (coarse_s[:, 2 * TILE :] * key_scale).astype(BF16)
        q_ref[p, 2 * rows - top :, :] = q_other.astype(BF16)
        k_ref[p, 2 * rows - top :, :] = k_other.astype(BF16)
        v_ref[p, 2 * rows - top :, :] = v_other.astype(BF16)

        def one_tile(i, inner):
            at = pl.ds(pl.multiple_of(i * TILE, TILE), TILE)
            v = v_ref[p, at, :]
            score = mm_nt(q_ref[p, at, :], two_heads(k_ref[p, at, :], first, second)) * SCALE
            mask = mask_s[jnp.where(i >= half_tiles, 1, 0)]
            prob = jnp.where(mask > 0.0, jnp.exp(score) * weight_s[i], 0.0).astype(BF16)
            prob_ref[p, i] = prob
            values = jnp.concatenate(
                [
                    jnp.concatenate([v * first, first], axis=1),
                    jnp.concatenate([v * second, second], axis=1),
                ],
                axis=0,
            )
            numer_s[at, :] = mm(prob, values)
            return inner

        lax.fori_loop(0, tiles, one_tile, 0, unroll=4)
        for t in range(half_tiles):
            at = slice(t * TILE, (t + 1) * TILE)
            both = numer_s[at, :] + mm(
                spreads[t % 2], stacked_low(take_local(numer_s, rows, rows, t))
            )
            total = both[:, TILE:]
            mixed = both[:, :TILE] / total
            total_ref[p, at, :] = total
            mixed_wide_ref[p, at, :] = mixed
            mixed_ref[p, at, :] = mixed.astype(BF16)
        return carry

    lax.fori_loop(0, pairs, one_pair, 0)


def feed_kernel(plan, info, own_ref, mixed_ref, full_s, *refs):
    ffn_refs, refs = refs[: len(plan)], refs[len(plan) :]
    b_out_ref, gain_ref, shift_ref, bias_ref, b_down_ref, hidden_ref, normed_ref = refs[:7]
    act_ref, slope_ref, ffn_s, *out_refs, result_s = refs[7:]
    pairs = mixed_ref.shape[0]
    line = info[5]
    assemble_feed(info, plan, ffn_refs, ffn_s)
    hidden = own_ref[...].astype(F32) + b_out_ref[...]
    for p in range(pairs):
        hidden = hidden + mm_nt(mixed_ref[p], full_s[p, :, 3 * TILE :])
    hidden_ref[...] = hidden
    unit, _ = unit_rows(hidden)
    normed = (unit * gain_ref[...] + shift_ref[...]).astype(BF16)
    normed_ref[...] = normed
    result = hidden + b_down_ref[...]
    for z in range(pairs):
        pre = mm(normed, ffn_s[z, 0]) + bias_row(bias_ref, z ^ line, 0)
        half_erf = 0.5 + 0.5 * lax.erf(pre * INV_ROOT_TWO)
        act = (pre * half_erf).astype(BF16)
        act_ref[z] = act
        slope_ref[z] = (half_erf + pre * jnp.exp(-0.5 * pre * pre) * INV_ROOT_TAU).astype(BF16)
        result = result + mm(act, ffn_s[z, 1])
    result_s[...] = result
    chunk = out_refs[0].shape[1]
    for far, out_ref in enumerate(out_refs):
        for o in range(out_ref.shape[0]):
            at = ((o ^ info[4]) * 2 + (far ^ info[3])) * chunk
            out_ref[o] = result_s[pl.ds(pl.multiple_of(at, chunk), chunk), :].astype(BF16)


def feed_back_kernel(dy_ref, full_s, ffn_s, *refs):
    slope_ref, hidden_ref, gain_ref, mixed_wide_ref, total_ref, grad_pre_ref, grad_hidden_ref = refs[:7]
    grad_hidden_low_ref, numer_ref, gtotal_ref, exchange_ref, vector_ref, b_up_ref = refs[7:13]
    rows = dy_ref.shape[0]
    pairs = slope_ref.shape[0]
    dy = dy_ref[...]
    grad_normed = jnp.zeros((rows, dy.shape[1]), F32)
    for z in range(pairs):
        grad_act = mm_nt(dy, ffn_s[z, 1])
        grad_pre = (grad_act * slope_ref[z].astype(F32)).astype(BF16)
        grad_pre_ref[z] = grad_pre
        b_up_ref[z] = jnp.sum(grad_pre.astype(F32), axis=0, keepdims=True)
        grad_normed = grad_normed + mm_nt(grad_pre, ffn_s[z, 0])
    unit, inverse = unit_rows(hidden_ref[...])
    dy_wide = dy.astype(F32)
    vector_ref[0:1, :] = jnp.sum(grad_normed * unit, axis=0, keepdims=True)
    vector_ref[1:2, :] = jnp.sum(grad_normed, axis=0, keepdims=True)
    vector_ref[2:3, :] = jnp.sum(dy_wide, axis=0, keepdims=True)
    grad_hidden = dy_wide + norm_back(grad_normed, unit, inverse, gain_ref[...])
    vector_ref[3:4, :] = jnp.sum(grad_hidden, axis=0, keepdims=True)
    grad_hidden_ref[...] = grad_hidden
    low = grad_hidden.astype(BF16)
    grad_hidden_low_ref[...] = low
    pool = top_pool(rows)
    top = pool.shape[0]
    same = ((iota((TILE, TILE), 0) // HEAD_SIZE) == (iota((TILE, TILE), 1) // HEAD_SIZE)).astype(F32).astype(BF16)
    for p in range(pairs):
        grad_mixed = mm(low, full_s[p, :, 3 * TILE :]).astype(BF16).astype(F32)
        inv = 1.0 / total_ref[p]
        numer = grad_mixed * inv
        high, rest = split_low(grad_mixed * mixed_wide_ref[p])
        gtotal = -(mm(high, same) + mm(rest, same)) * inv
        numer_ref[p] = numer
        gtotal_ref[p] = gtotal
        exchange_ref[p, :top, :] = mm_wide(pool, numer)
        exchange_ref[p, top:, :] = mm_wide(pool, gtotal)


def give_out(info, near_ref, far_ref, z, part, values_s):
    core, plane = info[3], info[4]
    chunk = near_ref.shape[-2]
    for far, ref in enumerate((near_ref, far_ref)):
        for o in range(ref.shape[0]):
            at = ((o ^ plane) * 2 + (far ^ core)) * chunk
            ref[o, z, part] = values_s[pl.ds(pl.multiple_of(at, chunk), chunk), :]


def feed_grads_kernel(
    info, normed_ref, act_ref, grad_pre_ref, dy_ref, near_ref, far_ref, up_s, down_s
):
    line = info[5]
    for z in range(act_ref.shape[0]):
        up_s[...] = mm_tn(normed_ref[...], grad_pre_ref[z]).astype(BF16)
        give_out(info, near_ref, far_ref, z ^ line, 0, up_s)
        down_s[...] = mm_tn(act_ref[z], dy_ref[...]).astype(BF16)
        give_out(info, near_ref, far_ref, z ^ line, 1, down_s)


def attend_back_kernel(
    info,
    lengths,
    numer_ref,
    gtotal_ref,
    exchange_ref,
    q_ref,
    k_ref,
    v_ref,
    prob_ref,
    full_s,
    own_ref,
    gain_ref,
    grad_hidden_ref,
    grads_ref,
    b_qv_ref,
    grad_tokens_ref,
    vector_ref,
    coarse_s,
    left_s,
    grad_s,
    acc_s,
):
    pairs, rows = numer_ref.shape[0], numer_ref.shape[1]
    tiles = 2 * rows // TILE
    half_tiles = rows // TILE
    length, own, partner = lengths[info[0]], info[1], info[2]
    pools = [jnp.concatenate([pool_tile(odd)] * 2, axis=1) for odd in range(2)]
    spreads = [jnp.concatenate([spread_tile(odd)] * 2, axis=1) for odd in range(2)]
    live = (iota((rows, 1), 0) + own < length).astype(F32)
    counts, shift = coarse_counts(iota((rows, 1), 0), rows, length, own, partner)
    value_scale = 1.0 / jnp.maximum(counts, 1.0)
    query_scale = 1.0 / lax.shift_left(jnp.ones_like(shift), shift).astype(F32)
    first, second = head_ones()
    at_lane = iota((1, TILE), 1) & (HEAD_SIZE - 1)
    pick = (at_lane < 2).astype(F32)
    pick_first = (pick * first.astype(F32)).astype(BF16)
    pick_second = (pick * second.astype(F32)).astype(BF16)
    is_low = at_lane == 1
    top = exchange_ref.shape[1] // 2

    def two_parts(gtotal):
        high = gtotal.astype(BF16).astype(F32)
        return jnp.where(is_low, gtotal - high, high).astype(BF16)

    def one_pair(p, carry):
        for t in range(half_tiles):
            at = slice(t * TILE, (t + 1) * TILE)
            numer, gtotal = numer_ref[p, at, :], gtotal_ref[p, at, :]
            left_s[at, :TILE] = numer.astype(BF16)
            left_s[at, TILE:] = two_parts(gtotal)
            both = jnp.concatenate([numer, gtotal], axis=1)
            put_pooled(coarse_s, rows, t, mm(pools[t % 2], stacked_low(both)))
        coarse_s[rows - top :, :TILE] = exchange_ref[p, :top, :]
        coarse_s[rows - top :, TILE:] = exchange_ref[p, top:, :]
        left_s[rows:, :TILE] = coarse_s[:, :TILE].astype(BF16)
        left_s[rows:, TILE:] = two_parts(coarse_s[:, TILE:])

        def one_tile(i, inner):
            at = pl.ds(pl.multiple_of(i * TILE, TILE), TILE)
            v = v_ref[p, at, :]
            prob = prob_ref[p, i]
            left = left_s[at, :]
            right = jnp.concatenate(
                [
                    jnp.concatenate([v * first, pick_first], axis=1),
                    jnp.concatenate([v * second, pick_second], axis=1),
                ],
                axis=0,
            )
            grad_score = (mm_nt(left, right) * prob.astype(F32)).astype(BF16)
            grad_s[at, :TILE] = mm(grad_score, two_heads(k_ref[p, at, :], first, second))
            grad_s[at, TILE : 2 * TILE] = mm_tn(
                stand(grad_score), two_heads(q_ref[p, at, :], first, second)
            )
            grad_s[at, 2 * TILE :] = mm_tn(stand(prob), two_heads(left[:, :TILE], first, second))
            return inner

        lax.fori_loop(0, tiles, one_tile, 0, unroll=4)
        grad_s[rows:, :TILE] *= query_scale
        grad_s[rows:, TILE:] *= value_scale
        for t in range(half_tiles):
            at = slice(t * TILE, (t + 1) * TILE)
            fine = grad_s[at, :] + mm(
                spreads[t % 2], stacked_low(take_local(grad_s, rows, rows, t))
            )
            gq = (fine[:, :TILE] * SCALE).astype(BF16)
            gk = (fine[:, TILE : 2 * TILE] * (SCALE * live[at])).astype(BF16)
            gv = (fine[:, 2 * TILE :] * live[at]).astype(BF16)
            grads_ref[p, at, :] = jnp.concatenate([gq, gk, gv], axis=1)
        sums = jnp.sum(grads_ref[p].astype(F32), axis=0, keepdims=True)
        b_qv_ref[p, 0:1, :] = sums[:, :TILE]
        b_qv_ref[p, 1:2, :] = sums[:, 2 * TILE :]
        acc_s[...] += mm_nt(grads_ref[p], full_s[p, :, : 3 * TILE])
        return carry

    acc_s[...] = jnp.zeros_like(acc_s)
    lax.fori_loop(0, pairs, one_pair, 0)
    unit, inverse = unit_rows(own_ref[...].astype(F32))
    grad_normed = acc_s[...]
    vector_ref[0:1, :] = jnp.sum(grad_normed * unit, axis=0, keepdims=True)
    vector_ref[1:2, :] = jnp.sum(grad_normed, axis=0, keepdims=True)
    grad_tokens_ref[...] = (
        grad_hidden_ref[...] + norm_back(grad_normed, unit, inverse, gain_ref[...])
    ).astype(BF16)


def attend_grads_kernel(
    info,
    normed_ref,
    grads_ref,
    grad_hidden_ref,
    mixed_ref,
    vec_two_ref,
    vec_up_ref,
    vec_one_ref,
    b_qv_ref,
    near_ref,
    far_ref,
    both_s,
):
    core, plane, line = info[3], info[4], info[5]
    pairs = mixed_ref.shape[0]
    dp = 2 * near_ref.shape[0]
    chunk = both_s.shape[0] // dp
    for z in range(pairs):
        grads = grads_ref[z]
        both_s[:, : 3 * TILE] = mm_tn(normed_ref[...], grads).astype(BF16)
        both_s[:, 3 * TILE :] = mm_tn(grad_hidden_ref[...], mixed_ref[z]).astype(BF16)
        for far, ref in enumerate((near_ref, far_ref)):
            for o in range(ref.shape[0]):
                at = ((o ^ plane) * 2 + (far ^ core)) * chunk
                at = pl.ds(pl.multiple_of(at, chunk), chunk)
                to = pl.ds(pl.multiple_of((z ^ line) * chunk, chunk), chunk)
                ref[o, to, :] = both_s[at, :]
    vectors = [vec_two_ref[...]] + [vec_up_ref[z] for z in range(pairs)] + [vec_one_ref[...]]
    for row in range(2):
        parts = [b_qv_ref[p, row : row + 1, :] for p in range(pairs)]
        vectors.append(jnp.concatenate(parts, axis=1))
    vectors = jnp.concatenate(vectors, axis=0)
    blank = jnp.zeros((near_ref.shape[1] - pairs * chunk - vectors.shape[0], vectors.shape[1]), F32)
    vectors = jnp.concatenate([vectors, blank], axis=0).astype(BF16)
    for ref in (near_ref, far_ref):
        for o in range(ref.shape[0]):
            ref[o, pairs * chunk :, :] = vectors


def place_grads_kernel(info, near_ref, far_ref, up_ref, down_ref, q_ref, k_ref, v_ref, o_ref, turn_s):
    core, plane = info[3], info[4]
    chunk = near_ref.shape[-2]
    for far, ref in enumerate((near_ref, far_ref)):
        for o in range(ref.shape[0]):
            at = ((o ^ plane) * 2 + (far ^ core)) * chunk
            at = pl.ds(pl.multiple_of(at, chunk), chunk)
            up_ref[at, :] = ref[o, 0].astype(F32)
            down_ref[at, :] = ref[o, 1].astype(F32)
            rest = ref[o, 2].astype(F32)
            q_ref[at, :] = rest[:, :TILE]
            k_ref[at, :] = rest[:, TILE : 2 * TILE]
            v_ref[at, :] = rest[:, 2 * TILE : 3 * TILE]
            turn_s[at, :] = rest[:, 3 * TILE :]
    o_ref[...] = turn_s[...].T


def line_sources(line, refs):
    own, one, two, three, passed = refs
    middle = (line == 1) | (line == 2)
    return [
        (None, line, own),
        (None, line ^ 1, one),
        (None, line ^ 2, two),
        (middle, line ^ 3, three),
        (jnp.logical_not(middle), line ^ 3, passed),
    ]


def gather_line(line, refs, to_ref):
    for where, z, ref in line_sources(line, refs):

        def put(z=z, ref=ref):
            to_ref[z] = ref[...]

        put() if where is None else pl.when(where)(put)


def place_rows_kernel(info, *refs):
    *pieces, out_ref, sems = refs
    for step in range(2):
        for n, (where, z, ref) in enumerate(line_sources(info[5], pieces)):

            def move(n=n, z=z, ref=ref):
                copy = pltpu.make_async_copy(ref, out_ref.at[z], sems.at[n])
                copy.wait() if step else copy.start()

            move() if where is None else pl.when(where)(move)


def deal_kernel(info, dealing, *refs):
    *pieces, out_ref, all_s = refs
    gather_line(info[5], pieces, all_s)
    own = info[4] * 2 + info[3]
    for i in range(out_ref.shape[0]):
        for slot in range(out_ref.shape[1]):
            seq = dealing[i * out_ref.shape[1] + slot]
            for half in range(out_ref.shape[2]):
                out_ref[i, slot, half] = all_s[(seq & 1) * 2 + half, (seq >> 1) ^ own]


def settle_kernel(pieces_ref, out_ref):
    dps, slots, halves = pieces_ref.shape[:3]
    for i in range(dps):
        for slot in range(slots):
            for half in range(halves):
                out_ref[slot, half, i] = pieces_ref[i, slot, half]


VMEM_SPEC = pl.BlockSpec(memory_space=pltpu.VMEM)
SMEM_SPEC = pl.BlockSpec(memory_space=pltpu.SMEM)


def call(kernel, outs, scalars, args, scratch=(), limit=16, long=False, flops=1, off_chip=False):
    spec = VMEM_SPEC
    if off_chip:
        spec = pl.BlockSpec(memory_space=pl.ANY)
    return pl.pallas_call(
        kernel,
        out_shape=[jax.ShapeDtypeStruct(shape, dtype) for shape, dtype in outs],
        in_specs=[SMEM_SPEC] * len(scalars) + [spec] * len(args),
        out_specs=[spec] * len(outs),
        scratch_shapes=list(scratch),
        compiler_params=pltpu.CompilerParams(vmem_limit_bytes=limit << 20),
        cost_estimate=pl.CostEstimate(
            flops=10**10 if long else flops, transcendentals=0, bytes_accessed=1
        ),
    )(*scalars, *args)


def exchange(pieces, axis, groups=None):
    return lax.all_to_all(pieces, axis, 0, 0, tiled=True, axis_index_groups=groups)


def gather(piece, axis, count):
    return exchange(jnp.broadcast_to(piece[None], (count,) + piece.shape), axis)


def swap(piece, axis, distance):
    size = lax.axis_size(axis)
    return lax.ppermute(piece, axis, [(i, i ^ distance) for i in range(size)])


def after(value, *others):
    return lax.optimization_barrier((value, others))[0]


def total_of(pieces):
    return functools.reduce(jnp.add, [piece.astype(F32) for piece in pieces]).astype(BF16)


def local(
    tokens,
    cotangent,
    lengths,
    dealing,
    ln1_gain,
    ln1_bias,
    w_query,
    b_query,
    w_key,
    w_value,
    b_value,
    w_out,
    b_out,
    ln2_gain,
    ln2_bias,
    w_up,
    b_up,
    w_down,
    b_down,
):
    seq_dev, length, width = tokens.shape
    dp = lax.axis_size("dp")
    nt = lax.axis_size("tensor")
    d = lax.axis_index("dp")
    t = lax.axis_index("tensor")
    rows = seq_dev * length // nt
    outer = dp // 2
    planes = [[2 * o + c for o in range(outer)] for c in range(2)]
    chunk = width // dp
    hid = w_up.shape[1]

    def near_line(piece):
        return [piece] + [swap(piece, "tensor", z) for z in range(1, nt)]

    def line_first(piece):
        return [piece, swap(piece, "tensor", 1), swap(piece, "tensor", 2)]

    def line_second(pieces):
        piece, one, two = pieces
        three = lax.ppermute(after(piece, two), "tensor", [(1, 2), (2, 1)])
        passed = lax.ppermute(two, "tensor", [(1, 0), (2, 3)])
        return [piece, one, two, three, passed]

    def plane_pieces(piece, others=None):
        return [piece] + [swap(others[o] if others else piece, "dp", 2 * o) for o in range(1, outer)]

    own_base = (t % 2) * rows
    info = jnp.stack([d * seq_dev + t // 2, own_base, rows - own_base, d % 2, d // 2, t])
    row = lambda v: v.reshape(1, -1)

    slice_spec = lambda lanes: pl.BlockSpec((chunk, lanes), lambda i, info: (info[4] * 2 + info[3], 0))
    whole_spec = lambda shape: pl.BlockSpec(shape, lambda i, info: (0,) * len(shape))
    attn_piece, ffn_piece = pl.pallas_call(
        pack_kernel,
        out_shape=[
            jax.ShapeDtypeStruct((chunk + 16, 4 * TILE), BF16),
            jax.ShapeDtypeStruct((2, chunk, hid), BF16),
        ],
        grid_spec=pltpu.PrefetchScalarGridSpec(
            num_scalar_prefetch=1,
            grid=(1,),
            in_specs=[slice_spec(TILE)] * 3
            + [whole_spec((TILE, width)), slice_spec(hid), slice_spec(width)]
            + [whole_spec((1, TILE)), whole_spec((1, TILE)), whole_spec((1, hid))],
            out_specs=[whole_spec((chunk + 16, 4 * TILE)), whole_spec((2, chunk, hid))],
            scratch_shapes=[pltpu.VMEM((width, TILE), BF16)],
        ),
    )(info, w_query, w_key, w_value, w_out, w_up, w_down, row(b_query), row(b_value), row(b_up))
    halves = tokens.reshape(nt, rows, width)
    own = lax.dynamic_index_in_dim(halves, t, 0, keepdims=False)
    other = lax.dynamic_index_in_dim(halves, t ^ 1, 0, keepdims=False)
    dy = lax.dynamic_index_in_dim(cotangent.reshape(nt, rows, width), t, 0, keepdims=False)
    top = rows >> level_shifts(rows)[-1]


    normed_one, pooled = call(
        norm_one_kernel,
        [((rows, width), BF16), ((4 * top, width), BF16)],
        [info, lengths],
        [own, other, row(ln1_gain), row(ln1_bias)],
    )
    attn_line = near_line(attn_piece)
    normed_one, *attn_line = lax.optimization_barrier((normed_one, *attn_line))
    biases = jnp.stack([piece[chunk:] for piece in attn_line])
    ffn_line = line_first(ffn_piece)
    attn_line, biases = call(
        stack_kernel,
        [((nt, chunk, 4 * TILE), BF16), ((nt, 16, 4 * TILE), BF16)],
        [],
        attn_line,
    )
    attn_pieces = plane_pieces(attn_line)
    up_line, down_line = call(
        part_kernel, [((nt, chunk, hid), BF16)] * 2, [info], line_second(ffn_line)
    )
    attn_pieces, up_line, down_line = lax.optimization_barrier((attn_pieces, up_line, down_line))
    attn_near = jnp.stack(attn_pieces)
    attn_w = attn_near, swap(attn_near, "dp", 1)
    ups = [jnp.stack([up_line, swap(up_line, "dp", 2)])]
    downs = [jnp.stack([down_line] + [swap(down_line, "dp", 4 * o) for o in range(1, outer // 2)])]
    ups += [swap(ups[0], "dp", 4 * o) for o in range(1, outer // 2)]
    downs += [swap(downs[0], "dp", 2)]
    plan = [(0, 0, (2 * o, 2 * o + 1)) for o in range(outer // 2)]
    plan += [(1, 0, tuple(range(first, outer, 2))) for first in range(2)]
    plan += [(part, 1, chips) for part, _, chips in plan]

    mixed, mixed_wide, total, q, k, v, prob, attn_full = call(
        attend_kernel,
        [((nt, rows, TILE), BF16), ((nt, rows, TILE), F32), ((nt, rows, TILE), F32)]
        + [((nt, 2 * rows, TILE), BF16)] * 3
        + [((nt, 2 * rows // TILE, TILE, 2 * TILE), BF16)]
        + [((nt, width, 4 * TILE), BF16)],
        [info, lengths],
        [normed_one, pooled, *attn_w, biases],
        scratch=[
            pltpu.VMEM((2 * rows // TILE, 1, 2 * TILE), F32),
            pltpu.VMEM((2, TILE, 2 * TILE), F32),
            pltpu.VMEM((rows, 3 * TILE), F32),
            pltpu.VMEM((2 * rows, 2 * TILE), F32),
        ],
        limit=24,
        long=True,
    )
    ups, downs, mixed = lax.optimization_barrier((ups, downs, mixed))
    ffn_w = ups + downs
    ffn_w += [swap(each, "dp", 1) for each in ffn_w]
    piece = rows // dp
    hidden, normed_two, act, slope, ffn_full, out_near, out_far = call(
        functools.partial(feed_kernel, plan),
        [((rows, width), F32), ((rows, width), BF16)]
        + [((nt, rows, hid), BF16)] * 2
        + [((nt, 2, width, hid), BF16)]
        + [((outer, piece, width), BF16)] * 2,
        [info],
        [own, mixed, attn_full, *ffn_w]
        + [row(b_out), row(ln2_gain), row(ln2_bias), biases, row(b_down)],
        scratch=[pltpu.VMEM((rows, width), F32)],
        limit=28,
    )
    chunks = call(
        pair_kernel, [((2, piece, width), BF16)] * outer, [], [out_near, swap(out_far, "dp", 1)]
    )
    dy, chunks = lax.optimization_barrier((dy, chunks))

    grad_pre, grad_hidden, grad_hidden_low, numer, gtotal, sent, vec_two, vec_up = call(
        feed_back_kernel,
        [
            ((nt, rows, hid), BF16),
            ((rows, width), F32),
            ((rows, width), BF16),
            ((nt, rows, TILE), F32),
            ((nt, rows, TILE), F32),
            ((nt, 2 * top, TILE), F32),
            ((4, width), F32),
            ((nt, 1, hid), F32),
        ],
        [],
        [dy, attn_full, ffn_full, slope, hidden, row(ln2_gain), mixed_wide, total],
        limit=28,
    )
    swapped = swap(sent, "tensor", 1)
    chunks, grad_pre = lax.optimization_barrier(
        (jnp.concatenate(plane_pieces(chunks[0], chunks)), grad_pre)
    )
    chunks = line_first(chunks)
    ffn_grads = call(
        feed_grads_kernel,
        [((outer, nt, 2, chunk, hid), BF16)] * 2,
        [info],
        [normed_two, act, grad_pre, dy],
        scratch=[pltpu.VMEM((width, hid), BF16)] * 2,
    )
    ffn_far = swap(ffn_grads[1], "dp", 1)

    def core_sums(near, far):
        return [total_of([near[o], far[o]]) for o in range(outer)]

    def plane_parts(pieces):
        return [pieces[0]] + [swap(pieces[o], "dp", 2 * o) for o in range(1, outer)]

    ffn_parts = core_sums(ffn_grads[0], ffn_far)
    gtotal, ffn_parts, swapped = lax.optimization_barrier((gtotal, ffn_parts, swapped))
    ffn_parts = plane_parts(ffn_parts)
    qkv_grads, vec_qv, grad_low, vec_one = call(
        attend_back_kernel,
        [
            ((nt, rows, 3 * TILE), BF16),
            ((nt, 2, TILE), F32),
            ((rows, width), BF16),
            ((2, width), F32),
        ],
        [info, lengths],
        [numer, gtotal, swapped, q, k, v, prob, attn_full]
        + [own, row(ln1_gain), grad_hidden],
        scratch=[
            pltpu.VMEM((rows, 2 * TILE), F32),
            pltpu.VMEM((2 * rows, 2 * TILE), BF16),
            pltpu.VMEM((2 * rows, 3 * TILE), F32),
            pltpu.VMEM((rows, width), F32),
        ],
        limit=20,
        long=True,
    )
    chunks, grad_low, grad_hidden_low = lax.optimization_barrier(
        (chunks, grad_low, grad_hidden_low)
    )
    attn_near, attn_far = call(
        attend_grads_kernel,
        [((outer, nt * chunk + 16, 4 * TILE), BF16)] * 2,
        [info],
        [normed_one, qkv_grads, grad_hidden_low, mixed, vec_two, vec_up, vec_one, vec_qv],
        scratch=[pltpu.VMEM((width, 4 * TILE), BF16)],
    )
    row_pieces = line_first(grad_low)
    chunks = line_second(chunks)
    attn_far, ffn_parts = lax.optimization_barrier((attn_far, ffn_parts))
    attn_far = swap(attn_far, "dp", 1)
    attn_parts = plane_parts(core_sums(attn_near, attn_far))
    attn_parts, chunks, row_pieces[1] = lax.optimization_barrier(
        (attn_parts, chunks, row_pieces[1])
    )
    (dealt,) = call(
        deal_kernel,
        [((dp, seq_dev, nt // seq_dev, piece, width), BF16)],
        [info, dealing],
        chunks,
        scratch=[pltpu.VMEM((nt, dp, piece, width), BF16)],
    )
    dealt = exchange(dealt, "dp")
    attn_parts = total_of(attn_parts)
    attn_parts, row_pieces[2] = lax.optimization_barrier((attn_parts, row_pieces[2]))
    ffn_parts = total_of(ffn_parts)
    grads = [
        jnp.concatenate(
            [ffn_parts[z].reshape(2 * chunk, hid), attn_parts[z * chunk : (z + 1) * chunk]]
            + [attn_parts[nt * chunk :]]
        )
        for z in range(nt)
    ]
    grads = total_of([grads[0]] + [swap(grads[z], "tensor", z) for z in range(1, nt)])
    vectors = grads[3 * chunk :].astype(F32)
    row_pieces = line_second(row_pieces)
    near = jnp.stack(plane_pieces(grads[: 3 * chunk].reshape(3, chunk, width)))
    (grad_tokens,) = call(
        place_rows_kernel,
        [((nt, rows, width), BF16)],
        [info],
        row_pieces,
        scratch=[pltpu.SemaphoreType.DMA((5,))],
        off_chip=True,
    )
    grad_tokens = grad_tokens.reshape(seq_dev, length, width)
    near, grad_tokens, dealt = lax.optimization_barrier((near, grad_tokens, dealt))
    grads = near, swap(near, "dp", 1)
    g_up, g_down, g_query, g_key, g_value, g_out = call(
        place_grads_kernel,
        [((width, hid), F32), ((hid, width), F32)]
        + [((width, TILE), F32)] * 3
        + [((TILE, width), F32)],
        [info],
        grads,
        scratch=[pltpu.VMEM((width, TILE), F32)],
    )
    (output,) = call(
        settle_kernel,
        [((seq_dev, nt // seq_dev, dp, piece, width), BF16)],
        [],
        [pltpu.with_memory_space_constraint(dealt, pltpu.HBM)],
    )
    output = output.reshape(seq_dev, length, width)
    base = 4 + nt
    g_b_up = lax.dynamic_index_in_dim(vectors[4:base], t, 0, keepdims=False)
    g_b_q = lax.dynamic_index_in_dim(vectors[base + 2].reshape(nt, TILE), t, 0, keepdims=False)
    g_b_v = lax.dynamic_index_in_dim(vectors[base + 3].reshape(nt, TILE), t, 0, keepdims=False)
    return (
        output,
        grad_tokens,
        vectors[base],
        vectors[base + 1],
        g_query,
        g_b_q,
        g_key,
        g_value,
        g_b_v,
        g_out,
        vectors[3],
        vectors[0],
        vectors[1],
        g_up,
        g_b_up,
        g_down,
        vectors[2],
    )


def solution(mesh):
    placed = (
        P("dp", None, None),
        P("dp", None, None),
        P(),
        P(),
        P(),
        P(),
        P(None, "tensor"),
        P("tensor"),
        P(None, "tensor"),
        P(None, "tensor"),
        P("tensor"),
        P("tensor", None),
        P(),
        P(),
        P(),
        P(None, "tensor"),
        P("tensor"),
        P("tensor", None),
        P(),
    )
    return jax.shard_map(
        local,
        mesh=mesh,
        in_specs=placed,
        out_specs=(
            P("dp", None, None),
            P("dp", None, None),
            P(),
            P(),
            P(None, "tensor"),
            P("tensor"),
            P(None, "tensor"),
            P(None, "tensor"),
            P("tensor"),
            P("tensor", None),
            P(),
            P(),
            P(),
            P(None, "tensor"),
            P("tensor"),
            P("tensor", None),
            P(),
        ),
        check_vma=False,
    )
```

```python
import functools

import jax
import jax.numpy as jnp
from jax import lax
from jax.experimental import pallas as pl
from jax.experimental.pallas import tpu as pltpu
from jax.sharding import PartitionSpec as P

F32 = jnp.float32
BF16 = jnp.bfloat16
HEAD_SIZE = 64
BLOCK = 16
TILE = 128
EPS = 1e-05
INV_ROOT_TWO = 0.7071067811865476
INV_ROOT_TAU = 0.3989422804014327
SCALE = HEAD_SIZE ** (-0.5)


def mm(left, right):
    return lax.dot_general(left, right, (((1,), (0,)), ((), ())), preferred_element_type=F32)


def mm_nt(left, right):
    return lax.dot_general(left, right, (((1,), (1,)), ((), ())), preferred_element_type=F32)


def mm_tn(left, right):
    return lax.dot_general(left, right, (((0,), (0,)), ((), ())), preferred_element_type=F32)


def split_low(values):
    high = values.astype(BF16)
    return high, (values - high.astype(F32)).astype(BF16)


def mm_wide(left, values):
    high, low = split_low(values)
    return mm(left, high) + mm(left, low)


def iota(shape, axis):
    return lax.broadcasted_iota(jnp.int32, shape, axis)


def unit_rows(values):
    centred = values - jnp.mean(values, axis=-1, keepdims=True)
    inverse = lax.rsqrt(jnp.mean(centred * centred, axis=-1, keepdims=True) + EPS)
    return centred * inverse, inverse


def norm_back(grad, unit, inverse, gain):
    scaled = grad * gain
    return inverse * (
        scaled
        - jnp.mean(scaled, axis=-1, keepdims=True)
        - unit * jnp.mean(scaled * unit, axis=-1, keepdims=True)
    )


def level_shifts(rows):
    shifts = []
    shift = 1
    while (2 * rows) >> shift >= 2 * BLOCK:
        shifts.append(shift)
        shift += 1
    return shifts


def coarse_map(index, rows):
    shifts = level_shifts(rows)
    shift = jnp.zeros_like(index)
    start = jnp.zeros_like(index)
    offset = 0
    for s in shifts:
        here = index >= offset
        shift = jnp.where(here, s, shift)
        start = jnp.where(here, offset, start)
        offset += rows >> s
    other = index >= offset
    start = jnp.where(other, offset, start)
    return shift, index - start, other


def coarse_counts(index, rows, length, own, partner):
    shift, place, other = coarse_map(index, rows)
    base = jnp.where(other, partner, own)
    left = length - base - lax.shift_left(place, shift)
    return jnp.clip(left, 0, lax.shift_left(jnp.ones_like(shift), shift)).astype(F32), shift


def tile_map(index):
    shift = jnp.zeros_like(index)
    start = jnp.zeros_like(index)
    offset = 0
    for s in range(1, 6):
        here = index >= offset
        shift = jnp.where(here, s, shift)
        start = jnp.where(here, offset, start)
        offset += TILE >> s
    return shift, index - start, index >= offset - (TILE >> 5)


def pool_tile(odd):
    shift, place, last = tile_map(iota((TILE, TILE), 0))
    place = jnp.where(last, place - odd * (TILE >> 5), place)
    hit = lax.shift_right_logical(iota((TILE, TILE), 1), shift) == place
    return hit.astype(F32).astype(BF16)


def spread_tile(odd):
    shift, place, last = tile_map(iota((TILE, TILE), 1))
    place = jnp.where(last, place - odd * (TILE >> 5), place)
    hit = lax.shift_right_logical(iota((TILE, TILE), 0), shift) == place
    return hit.astype(F32).astype(BF16)


def level_places(rows, tile):
    found = []
    local, offset = 0, 0
    for s in level_shifts(rows):
        count = TILE >> s
        found.append((local, count, offset + tile * count))
        local += count
        offset += rows >> s
    return found[:-1], found[-1]


def put_pooled(to_s, rows, tile, pooled):
    levels, (local, count, at) = level_places(rows, tile)
    for start, number, place in levels:
        to_s[place : place + number, :] = pooled[start : start + number]
    at -= (tile % 2) * count
    if tile % 2:
        to_s[at : at + 2 * count, :] += pooled[local : local + 2 * count]
    else:
        to_s[at : at + 2 * count, :] = pooled[local : local + 2 * count]


def take_local(from_s, base, rows, tile):
    levels, (local, count, at) = level_places(rows, tile)
    at -= (tile % 2) * count
    parts = [from_s[base + place : base + place + number, :] for _, number, place in levels]
    return jnp.concatenate(parts + [from_s[base + at : base + at + 2 * count, :]], axis=0)


def stacked_low(values):
    return jnp.concatenate(split_low(values), axis=0)


def top_pool(rows):
    shift = level_shifts(rows)[-1]
    count = rows >> shift
    hit = lax.shift_right_logical(iota((count, rows), 1), shift) == iota((count, rows), 0)
    return hit.astype(F32).astype(BF16)


def head_ones():
    second = (iota((TILE, TILE), 1) >= HEAD_SIZE).astype(F32)
    return (1.0 - second).astype(BF16), second.astype(BF16)


def two_heads(values, first, second):
    return jnp.concatenate([values * first, values * second], axis=0)


def stand(values):
    return jnp.concatenate([values[:, :TILE], values[:, TILE:]], axis=0)


def assemble(info, near_ref, far_ref, to_ref):
    core, plane, line = info[3], info[4], info[5]
    chunk = near_ref.shape[-2]
    for far, ref in enumerate((near_ref, far_ref)):
        for o in range(ref.shape[0]):
            at = ((o ^ plane) * 2 + (far ^ core)) * chunk
            at = pl.ds(pl.multiple_of(at, chunk), chunk)
            for z in range(ref.shape[1]):
                to_ref[z ^ line, at, :] = ref[o, z]


def assemble_feed(info, plan, refs, to_ref):
    core, plane = info[3], info[4]
    for (part, far, chips), ref in zip(plan, refs):
        chunk = ref.shape[-2]
        for i, o in enumerate(chips):
            at = ((o ^ plane) * 2 + (far ^ core)) * chunk
            at = pl.ds(pl.multiple_of(at, chunk), chunk)
            for z in range(ref.shape[1]):
                to_ref[z, part, at, :] = ref[i, z]


def pack_kernel(info, q_ref, k_ref, v_ref, o_ref, up_ref, down_ref, bq_ref, bv_ref, bu_ref, attn_ref, ffn_ref, turn_s):
    chunk = q_ref.shape[0]
    attn_ref[:chunk, 0 * TILE : 1 * TILE] = q_ref[...]
    attn_ref[:chunk, 1 * TILE : 2 * TILE] = k_ref[...]
    attn_ref[:chunk, 2 * TILE : 3 * TILE] = v_ref[...]
    turn_s[...] = o_ref[...].T
    at = pl.ds(pl.multiple_of((info[4] * 2 + info[3]) * chunk, chunk), chunk)
    attn_ref[:chunk, 3 * TILE :] = turn_s[at, :]
    ffn_ref[0] = up_ref[...]
    ffn_ref[1] = down_ref[...]
    lanes = bu_ref.shape[1]
    blank = jnp.zeros((1, lanes - 2 * TILE), F32)
    rest = jnp.concatenate(
        [bu_ref[...], jnp.concatenate([bq_ref[...], bv_ref[...], blank], axis=1)], axis=0
    )
    rows = []
    for _ in range(3):
        part = rest.astype(BF16).astype(F32)
        rows.append(part)
        rest = rest - part
    rows.append(jnp.zeros((10, lanes), F32))
    attn_ref[chunk:, :] = jnp.concatenate(rows, axis=0).astype(BF16)


def stack_kernel(*refs):
    *pieces, weight_ref, bias_ref = refs
    chunk = weight_ref.shape[1]
    for z, ref in enumerate(pieces):
        weight_ref[z] = ref[:chunk, :]
        bias_ref[z] = ref[chunk:, :]


def part_kernel(info, *refs):
    *pieces, up_ref, down_ref = refs
    for where, z, ref in line_sources(info[5], pieces):

        def put(z=z, ref=ref):
            up_ref[z] = ref[0]
            down_ref[z] = ref[1]

        put() if where is None else pl.when(where)(put)


def pair_kernel(near_ref, far_ref, *out_refs):
    for o, ref in enumerate(out_refs):
        ref[0] = near_ref[o]
        ref[1] = far_ref[o]


def bias_row(bias_ref, z, row):
    total = bias_ref[z, row : row + 1, :].astype(F32)
    for part in range(1, 3):
        at = 2 * part + row
        total = total + bias_ref[z, at : at + 1, :].astype(F32)
    return total


def norm_one_kernel(info, lengths, own_ref, other_ref, gain_ref, bias_ref, normed_ref, pooled_ref):
    rows = own_ref.shape[0]
    length, partner = lengths[info[0]], info[2]
    gain, bias = gain_ref[...], bias_ref[...]
    unit, _ = unit_rows(own_ref[...].astype(F32))
    normed_ref[...] = (unit * gain + bias).astype(BF16)
    unit, _ = unit_rows(other_ref[...].astype(F32))
    normed = (unit * gain + bias).astype(BF16)
    pool = top_pool(rows)
    count = pool.shape[0]
    live = (iota((1, rows), 1) + partner < length).astype(F32)
    pool_live = (pool.astype(F32) * live).astype(BF16)
    sums = mm(pool_live, normed)
    counts = jnp.sum(pool_live.astype(F32), axis=-1, keepdims=True)
    mean_live = sums / jnp.maximum(counts, 1.0)
    mean_all = mm(pool, normed) * (count / rows)
    high, low = split_low(mean_all)
    pooled_ref[0 * count : 1 * count, :] = high
    pooled_ref[1 * count : 2 * count, :] = low
    high, low = split_low(mean_live)
    pooled_ref[2 * count : 3 * count, :] = high
    pooled_ref[3 * count : 4 * count, :] = low


def attend_kernel(
    info,
    lengths,
    normed_ref,
    pooled_ref,
    near_ref,
    far_ref,
    bias_ref,
    mixed_ref,
    mixed_wide_ref,
    total_ref,
    q_ref,
    k_ref,
    v_ref,
    prob_ref,
    full_s,
    weight_s,
    mask_s,
    coarse_s,
    numer_s,
):
    rows = normed_ref.shape[0]
    pairs = q_ref.shape[0]
    tiles = 2 * rows // TILE
    half_tiles = rows // TILE
    length, own, partner = lengths[info[0]], info[1], info[2]
    line = info[5]
    assemble(info, near_ref, far_ref, full_s)
    pools = [pool_tile(odd) for odd in range(2)]
    spreads = [jnp.concatenate([spread_tile(odd)] * 2, axis=1) for odd in range(2)]
    lane = iota((1, 2 * TILE), 1) & (TILE - 1)
    for i in range(half_tiles):
        weight_s[i] = (lane + (own + i * TILE) < length).astype(F32)
        counts, _ = coarse_counts(lane + i * TILE, rows, length, own, partner)
        weight_s[half_tiles + i] = counts
    row_at = iota((TILE, 2 * TILE), 0)
    key_at = iota((TILE, 2 * TILE), 1) & (TILE - 1)
    pair_same = (row_at >> 5) == (key_at >> 5)
    apart = (row_at >> 4) != (key_at >> 4)
    mask_s[0] = pair_same.astype(F32)
    mask_s[1] = (pair_same & apart).astype(F32)
    live = (iota((rows, 1), 0) + own < length).astype(F32)
    counts, shift = coarse_counts(iota((rows, 1), 0), rows, length, own, partner)
    key_scale = 1.0 / jnp.maximum(counts, 1.0)
    query_scale = 1.0 / lax.shift_left(jnp.ones_like(shift), shift).astype(F32)
    top = pooled_ref.shape[0] // 4
    counts_other = counts[rows - top :]
    filled = counts_other / jnp.maximum(counts_other, 1.0)
    first, second = head_ones()

    def one_pair(p, carry):
        weight = full_s[p, :, : 3 * TILE]
        wide = mm(normed_ref[...], weight)
        biases = bias_row(bias_ref, p ^ line, 1)
        bq, bv = biases[:, :TILE], biases[:, TILE : 2 * TILE]
        query = (wide[:, :TILE] + bq).astype(BF16)
        key = (wide[:, TILE : 2 * TILE].astype(BF16).astype(F32) * live).astype(BF16)
        value = ((wide[:, 2 * TILE :] + bv).astype(BF16).astype(F32) * live).astype(BF16)
        extra = mm(pooled_ref[...], weight)
        q_other = extra[:top, :TILE] + extra[top : 2 * top, :TILE] + bq
        kv_other = extra[2 * top : 3 * top, TILE:] + extra[3 * top :, TILE:]
        k_other = kv_other[:, :TILE]
        v_other = kv_other[:, TILE:] + bv * filled
        q_ref[p, :rows, :] = query
        k_ref[p, :rows, :] = key
        v_ref[p, :rows, :] = value
        rows_all = jnp.concatenate([query, key, value], axis=1)
        for t in range(half_tiles):
            put_pooled(coarse_s, rows, t, mm(pools[t % 2], rows_all[t * TILE : (t + 1) * TILE]))
        q_ref[p, rows:, :] = (coarse_s[:, :TILE] * query_scale).astype(BF16)
        k_ref[p, rows:, :] = (coarse_s[:, TILE : 2 * TILE] * key_scale).astype(BF16)
        v_ref[p, rows:, :] = (coarse_s[:, 2 * TILE :] * key_scale).astype(BF16)
        q_ref[p, 2 * rows - top :, :] = q_other.astype(BF16)
        k_ref[p, 2 * rows - top :, :] = k_other.astype(BF16)
        v_ref[p, 2 * rows - top :, :] = v_other.astype(BF16)

        def one_tile(i, inner):
            at = pl.ds(pl.multiple_of(i * TILE, TILE), TILE)
            v = v_ref[p, at, :]
            score = mm_nt(q_ref[p, at, :], two_heads(k_ref[p, at, :], first, second)) * SCALE
            mask = mask_s[jnp.where(i >= half_tiles, 1, 0)]
            prob = jnp.where(mask > 0.0, jnp.exp(score) * weight_s[i], 0.0).astype(BF16)
            prob_ref[p, i] = prob
            values = jnp.concatenate(
                [
                    jnp.concatenate([v * first, first], axis=1),
                    jnp.concatenate([v * second, second], axis=1),
                ],
                axis=0,
            )
            numer_s[at, :] = mm(prob, values)
            return inner

        lax.fori_loop(0, tiles, one_tile, 0, unroll=4)
        for t in range(half_tiles):
            at = slice(t * TILE, (t + 1) * TILE)
            both = numer_s[at, :] + mm(
                spreads[t % 2], stacked_low(take_local(numer_s, rows, rows, t))
            )
            total = both[:, TILE:]
            mixed = both[:, :TILE] / total
            total_ref[p, at, :] = total
            mixed_wide_ref[p, at, :] = mixed
            mixed_ref[p, at, :] = mixed.astype(BF16)
        return carry

    lax.fori_loop(0, pairs, one_pair, 0)


def feed_kernel(plan, info, own_ref, mixed_ref, full_s, *refs):
    ffn_refs, refs = refs[: len(plan)], refs[len(plan) :]
    b_out_ref, gain_ref, shift_ref, bias_ref, b_down_ref, hidden_ref, normed_ref = refs[:7]
    act_ref, slope_ref, ffn_s, *out_refs, result_s = refs[7:]
    pairs = mixed_ref.shape[0]
    line = info[5]
    assemble_feed(info, plan, ffn_refs, ffn_s)
    hidden = own_ref[...].astype(F32) + b_out_ref[...]
    for p in range(pairs):
        hidden = hidden + mm_nt(mixed_ref[p], full_s[p, :, 3 * TILE :])
    hidden_ref[...] = hidden
    unit, _ = unit_rows(hidden)
    normed = (unit * gain_ref[...] + shift_ref[...]).astype(BF16)
    normed_ref[...] = normed
    result = hidden + b_down_ref[...]
    for z in range(pairs):
        pre = mm(normed, ffn_s[z, 0]) + bias_row(bias_ref, z ^ line, 0)
        half_erf = 0.5 + 0.5 * lax.erf(pre * INV_ROOT_TWO)
        act = (pre * half_erf).astype(BF16)
        act_ref[z] = act
        slope_ref[z] = (half_erf + pre * jnp.exp(-0.5 * pre * pre) * INV_ROOT_TAU).astype(BF16)
        result = result + mm(act, ffn_s[z, 1])
    result_s[...] = result
    chunk = out_refs[0].shape[1]
    for far, out_ref in enumerate(out_refs):
        for o in range(out_ref.shape[0]):
            at = ((o ^ info[4]) * 2 + (far ^ info[3])) * chunk
            out_ref[o] = result_s[pl.ds(pl.multiple_of(at, chunk), chunk), :].astype(BF16)


def feed_back_kernel(dy_ref, full_s, ffn_s, *refs):
    slope_ref, hidden_ref, gain_ref, mixed_wide_ref, total_ref, grad_pre_ref, grad_hidden_ref = refs[:7]
    grad_hidden_low_ref, numer_ref, gtotal_ref, exchange_ref, vector_ref, b_up_ref = refs[7:13]
    rows = dy_ref.shape[0]
    pairs = slope_ref.shape[0]
    dy = dy_ref[...]
    grad_normed = jnp.zeros((rows, dy.shape[1]), F32)
    for z in range(pairs):
        grad_act = mm_nt(dy, ffn_s[z, 1])
        grad_pre = (grad_act * slope_ref[z].astype(F32)).astype(BF16)
        grad_pre_ref[z] = grad_pre
        b_up_ref[z] = jnp.sum(grad_pre.astype(F32), axis=0, keepdims=True)
        grad_normed = grad_normed + mm_nt(grad_pre, ffn_s[z, 0])
    unit, inverse = unit_rows(hidden_ref[...])
    dy_wide = dy.astype(F32)
    vector_ref[0:1, :] = jnp.sum(grad_normed * unit, axis=0, keepdims=True)
    vector_ref[1:2, :] = jnp.sum(grad_normed, axis=0, keepdims=True)
    vector_ref[2:3, :] = jnp.sum(dy_wide, axis=0, keepdims=True)
    grad_hidden = dy_wide + norm_back(grad_normed, unit, inverse, gain_ref[...])
    vector_ref[3:4, :] = jnp.sum(grad_hidden, axis=0, keepdims=True)
    grad_hidden_ref[...] = grad_hidden
    low = grad_hidden.astype(BF16)
    grad_hidden_low_ref[...] = low
    pool = top_pool(rows)
    top = pool.shape[0]
    same = ((iota((TILE, TILE), 0) // HEAD_SIZE) == (iota((TILE, TILE), 1) // HEAD_SIZE)).astype(F32).astype(BF16)
    for p in range(pairs):
        grad_mixed = mm(low, full_s[p, :, 3 * TILE :]).astype(BF16).astype(F32)
        inv = 1.0 / total_ref[p]
        numer = grad_mixed * inv
        high, rest = split_low(grad_mixed * mixed_wide_ref[p])
        gtotal = -(mm(high, same) + mm(rest, same)) * inv
        numer_ref[p] = numer
        gtotal_ref[p] = gtotal
        exchange_ref[p, :top, :] = mm_wide(pool, numer)
        exchange_ref[p, top:, :] = mm_wide(pool, gtotal)


def give_out(info, near_ref, far_ref, z, part, values_s):
    core, plane = info[3], info[4]
    chunk = near_ref.shape[-2]
    for far, ref in enumerate((near_ref, far_ref)):
        for o in range(ref.shape[0]):
            at = ((o ^ plane) * 2 + (far ^ core)) * chunk
            ref[o, z, part] = values_s[pl.ds(pl.multiple_of(at, chunk), chunk), :]


def feed_grads_kernel(
    info, normed_ref, act_ref, grad_pre_ref, dy_ref, near_ref, far_ref, up_s, down_s
):
    line = info[5]
    for z in range(act_ref.shape[0]):
        up_s[...] = mm_tn(normed_ref[...], grad_pre_ref[z]).astype(BF16)
        give_out(info, near_ref, far_ref, z ^ line, 0, up_s)
        down_s[...] = mm_tn(act_ref[z], dy_ref[...]).astype(BF16)
        give_out(info, near_ref, far_ref, z ^ line, 1, down_s)


def attend_back_kernel(
    info,
    lengths,
    numer_ref,
    gtotal_ref,
    exchange_ref,
    q_ref,
    k_ref,
    v_ref,
    prob_ref,
    full_s,
    own_ref,
    gain_ref,
    grad_hidden_ref,
    grads_ref,
    b_qv_ref,
    grad_tokens_ref,
    vector_ref,
    coarse_s,
    left_s,
    grad_s,
    acc_s,
):
    pairs, rows = numer_ref.shape[0], numer_ref.shape[1]
    tiles = 2 * rows // TILE
    half_tiles = rows // TILE
    length, own, partner = lengths[info[0]], info[1], info[2]
    pools = [jnp.concatenate([pool_tile(odd)] * 2, axis=1) for odd in range(2)]
    spreads = [jnp.concatenate([spread_tile(odd)] * 2, axis=1) for odd in range(2)]
    live = (iota((rows, 1), 0) + own < length).astype(F32)
    counts, shift = coarse_counts(iota((rows, 1), 0), rows, length, own, partner)
    value_scale = 1.0 / jnp.maximum(counts, 1.0)
    query_scale = 1.0 / lax.shift_left(jnp.ones_like(shift), shift).astype(F32)
    first, second = head_ones()
    at_lane = iota((1, TILE), 1) & (HEAD_SIZE - 1)
    pick = (at_lane < 2).astype(F32)
    pick_first = (pick * first.astype(F32)).astype(BF16)
    pick_second = (pick * second.astype(F32)).astype(BF16)
    is_low = at_lane == 1
    top = exchange_ref.shape[1] // 2

    def two_parts(gtotal):
        high = gtotal.astype(BF16).astype(F32)
        return jnp.where(is_low, gtotal - high, high).astype(BF16)

    def one_pair(p, carry):
        for t in range(half_tiles):
            at = slice(t * TILE, (t + 1) * TILE)
            numer, gtotal = numer_ref[p, at, :], gtotal_ref[p, at, :]
            left_s[at, :TILE] = numer.astype(BF16)
            left_s[at, TILE:] = two_parts(gtotal)
            both = jnp.concatenate([numer, gtotal], axis=1)
            put_pooled(coarse_s, rows, t, mm(pools[t % 2], stacked_low(both)))
        coarse_s[rows - top :, :TILE] = exchange_ref[p, :top, :]
        coarse_s[rows - top :, TILE:] = exchange_ref[p, top:, :]
        left_s[rows:, :TILE] = coarse_s[:, :TILE].astype(BF16)
        left_s[rows:, TILE:] = two_parts(coarse_s[:, TILE:])

        def one_tile(i, inner):
            at = pl.ds(pl.multiple_of(i * TILE, TILE), TILE)
            v = v_ref[p, at, :]
            prob = prob_ref[p, i]
            left = left_s[at, :]
            right = jnp.concatenate(
                [
                    jnp.concatenate([v * first, pick_first], axis=1),
                    jnp.concatenate([v * second, pick_second], axis=1),
                ],
                axis=0,
            )
            grad_score = (mm_nt(left, right) * prob.astype(F32)).astype(BF16)
            grad_s[at, :TILE] = mm(grad_score, two_heads(k_ref[p, at, :], first, second))
            grad_s[at, TILE : 2 * TILE] = mm_tn(
                stand(grad_score), two_heads(q_ref[p, at, :], first, second)
            )
            grad_s[at, 2 * TILE :] = mm_tn(stand(prob), two_heads(left[:, :TILE], first, second))
            return inner

        lax.fori_loop(0, tiles, one_tile, 0, unroll=4)
        grad_s[rows:, :TILE] *= query_scale
        grad_s[rows:, TILE:] *= value_scale
        for t in range(half_tiles):
            at = slice(t * TILE, (t + 1) * TILE)
            fine = grad_s[at, :] + mm(
                spreads[t % 2], stacked_low(take_local(grad_s, rows, rows, t))
            )
            gq = (fine[:, :TILE] * SCALE).astype(BF16)
            gk = (fine[:, TILE : 2 * TILE] * (SCALE * live[at])).astype(BF16)
            gv = (fine[:, 2 * TILE :] * live[at]).astype(BF16)
            grads_ref[p, at, :] = jnp.concatenate([gq, gk, gv], axis=1)
        sums = jnp.sum(grads_ref[p].astype(F32), axis=0, keepdims=True)
        b_qv_ref[p, 0:1, :] = sums[:, :TILE]
        b_qv_ref[p, 1:2, :] = sums[:, 2 * TILE :]
        acc_s[...] += mm_nt(grads_ref[p], full_s[p, :, : 3 * TILE])
        return carry

    acc_s[...] = jnp.zeros_like(acc_s)
    lax.fori_loop(0, pairs, one_pair, 0)
    unit, inverse = unit_rows(own_ref[...].astype(F32))
    grad_normed = acc_s[...]
    vector_ref[0:1, :] = jnp.sum(grad_normed * unit, axis=0, keepdims=True)
    vector_ref[1:2, :] = jnp.sum(grad_normed, axis=0, keepdims=True)
    grad_tokens_ref[...] = (
        grad_hidden_ref[...] + norm_back(grad_normed, unit, inverse, gain_ref[...])
    ).astype(BF16)


def attend_grads_kernel(
    info,
    normed_ref,
    grads_ref,
    grad_hidden_ref,
    mixed_ref,
    vec_two_ref,
    vec_up_ref,
    vec_one_ref,
    b_qv_ref,
    near_ref,
    far_ref,
    both_s,
):
    core, plane, line = info[3], info[4], info[5]
    pairs = mixed_ref.shape[0]
    dp = 2 * near_ref.shape[0]
    chunk = both_s.shape[0] // dp
    for z in range(pairs):
        grads = grads_ref[z]
        both_s[:, : 3 * TILE] = mm_tn(normed_ref[...], grads).astype(BF16)
        both_s[:, 3 * TILE :] = mm_tn(grad_hidden_ref[...], mixed_ref[z]).astype(BF16)
        for far, ref in enumerate((near_ref, far_ref)):
            for o in range(ref.shape[0]):
                at = ((o ^ plane) * 2 + (far ^ core)) * chunk
                at = pl.ds(pl.multiple_of(at, chunk), chunk)
                to = pl.ds(pl.multiple_of((z ^ line) * chunk, chunk), chunk)
                ref[o, to, :] = both_s[at, :]
    vectors = [vec_two_ref[...]] + [vec_up_ref[z] for z in range(pairs)] + [vec_one_ref[...]]
    for row in range(2):
        parts = [b_qv_ref[p, row : row + 1, :] for p in range(pairs)]
        vectors.append(jnp.concatenate(parts, axis=1))
    vectors = jnp.concatenate(vectors, axis=0)
    blank = jnp.zeros((near_ref.shape[1] - pairs * chunk - vectors.shape[0], vectors.shape[1]), F32)
    vectors = jnp.concatenate([vectors, blank], axis=0).astype(BF16)
    for ref in (near_ref, far_ref):
        for o in range(ref.shape[0]):
            ref[o, pairs * chunk :, :] = vectors


def place_grads_kernel(info, near_ref, far_ref, up_ref, down_ref, q_ref, k_ref, v_ref, o_ref, turn_s):
    core, plane = info[3], info[4]
    chunk = near_ref.shape[-2]
    for far, ref in enumerate((near_ref, far_ref)):
        for o in range(ref.shape[0]):
            at = ((o ^ plane) * 2 + (far ^ core)) * chunk
            at = pl.ds(pl.multiple_of(at, chunk), chunk)
            up_ref[at, :] = ref[o, 0].astype(F32)
            down_ref[at, :] = ref[o, 1].astype(F32)
            rest = ref[o, 2].astype(F32)
            q_ref[at, :] = rest[:, :TILE]
            k_ref[at, :] = rest[:, TILE : 2 * TILE]
            v_ref[at, :] = rest[:, 2 * TILE : 3 * TILE]
            turn_s[at, :] = rest[:, 3 * TILE :]
    o_ref[...] = turn_s[...].T


def line_sources(line, refs):
    own, one, two, three, passed = refs
    middle = (line == 1) | (line == 2)
    return [
        (None, line, own),
        (None, line ^ 1, one),
        (None, line ^ 2, two),
        (middle, line ^ 3, three),
        (jnp.logical_not(middle), line ^ 3, passed),
    ]


def gather_line(line, refs, to_ref):
    for where, z, ref in line_sources(line, refs):

        def put(z=z, ref=ref):
            to_ref[z] = ref[...]

        put() if where is None else pl.when(where)(put)


def place_rows_kernel(info, *refs):
    *pieces, out_ref, sems = refs
    for step in range(2):
        for n, (where, z, ref) in enumerate(line_sources(info[5], pieces)):

            def move(n=n, z=z, ref=ref):
                copy = pltpu.make_async_copy(ref, out_ref.at[z], sems.at[n])
                copy.wait() if step else copy.start()

            move() if where is None else pl.when(where)(move)


def deal_kernel(info, dealing, *refs):
    *pieces, out_ref, all_s = refs
    gather_line(info[5], pieces, all_s)
    own = info[4] * 2 + info[3]
    for i in range(out_ref.shape[0]):
        for slot in range(out_ref.shape[1]):
            seq = dealing[i * out_ref.shape[1] + slot]
            for half in range(out_ref.shape[2]):
                out_ref[i, slot, half] = all_s[(seq & 1) * 2 + half, (seq >> 1) ^ own]


def settle_kernel(pieces_ref, out_ref):
    dps, slots, halves = pieces_ref.shape[:3]
    for i in range(dps):
        for slot in range(slots):
            for half in range(halves):
                out_ref[slot, half, i] = pieces_ref[i, slot, half]


VMEM_SPEC = pl.BlockSpec(memory_space=pltpu.VMEM)
SMEM_SPEC = pl.BlockSpec(memory_space=pltpu.SMEM)


def call(kernel, outs, scalars, args, scratch=(), limit=16, long=False, flops=1, off_chip=False):
    spec = VMEM_SPEC
    if off_chip:
        spec = pl.BlockSpec(memory_space=pl.ANY)
    return pl.pallas_call(
        kernel,
        out_shape=[jax.ShapeDtypeStruct(shape, dtype) for shape, dtype in outs],
        in_specs=[SMEM_SPEC] * len(scalars) + [spec] * len(args),
        out_specs=[spec] * len(outs),
        scratch_shapes=list(scratch),
        compiler_params=pltpu.CompilerParams(vmem_limit_bytes=limit << 20),
        cost_estimate=pl.CostEstimate(
            flops=10**10 if long else flops, transcendentals=0, bytes_accessed=1
        ),
    )(*scalars, *args)


def exchange(pieces, axis, groups=None):
    return lax.all_to_all(pieces, axis, 0, 0, tiled=True, axis_index_groups=groups)


def gather(piece, axis, count):
    return exchange(jnp.broadcast_to(piece[None], (count,) + piece.shape), axis)


def swap(piece, axis, distance):
    size = lax.axis_size(axis)
    return lax.ppermute(piece, axis, [(i, i ^ distance) for i in range(size)])


def after(value, *others):
    return lax.optimization_barrier((value, others))[0]


def total_of(pieces):
    return functools.reduce(jnp.add, [piece.astype(F32) for piece in pieces]).astype(BF16)


def local(
    tokens,
    cotangent,
    lengths,
    dealing,
    ln1_gain,
    ln1_bias,
    w_query,
    b_query,
    w_key,
    w_value,
    b_value,
    w_out,
    b_out,
    ln2_gain,
    ln2_bias,
    w_up,
    b_up,
    w_down,
    b_down,
):
    seq_dev, length, width = tokens.shape
    dp = lax.axis_size("dp")
    nt = lax.axis_size("tensor")
    d = lax.axis_index("dp")
    t = lax.axis_index("tensor")
    rows = seq_dev * length // nt
    outer = dp // 2
    planes = [[2 * o + c for o in range(outer)] for c in range(2)]
    chunk = width // dp
    hid = w_up.shape[1]

    def near_line(piece):
        return [piece] + [swap(piece, "tensor", z) for z in range(1, nt)]

    def line_first(piece):
        return [piece, swap(piece, "tensor", 1), swap(piece, "tensor", 2)]

    def line_second(pieces):
        piece, one, two = pieces
        three = lax.ppermute(after(piece, two), "tensor", [(1, 2), (2, 1)])
        passed = lax.ppermute(two, "tensor", [(1, 0), (2, 3)])
        return [piece, one, two, three, passed]

    def plane_pieces(piece, others=None):
        return [piece] + [swap(others[o] if others else piece, "dp", 2 * o) for o in range(1, outer)]

    own_base = (t % 2) * rows
    info = jnp.stack([d * seq_dev + t // 2, own_base, rows - own_base, d % 2, d // 2, t])
    row = lambda v: v.reshape(1, -1)

    slice_spec = lambda lanes: pl.BlockSpec((chunk, lanes), lambda i, info: (info[4] * 2 + info[3], 0))
    whole_spec = lambda shape: pl.BlockSpec(shape, lambda i, info: (0,) * len(shape))
    attn_piece, ffn_piece = pl.pallas_call(
        pack_kernel,
        out_shape=[
            jax.ShapeDtypeStruct((chunk + 16, 4 * TILE), BF16),
            jax.ShapeDtypeStruct((2, chunk, hid), BF16),
        ],
        grid_spec=pltpu.PrefetchScalarGridSpec(
            num_scalar_prefetch=1,
            grid=(1,),
            in_specs=[slice_spec(TILE)] * 3
            + [whole_spec((TILE, width)), slice_spec(hid), slice_spec(width)]
            + [whole_spec((1, TILE)), whole_spec((1, TILE)), whole_spec((1, hid))],
            out_specs=[whole_spec((chunk + 16, 4 * TILE)), whole_spec((2, chunk, hid))],
            scratch_shapes=[pltpu.VMEM((width, TILE), BF16)],
        ),
    )(info, w_query, w_key, w_value, w_out, w_up, w_down, row(b_query), row(b_value), row(b_up))
    halves = tokens.reshape(nt, rows, width)
    own = lax.dynamic_index_in_dim(halves, t, 0, keepdims=False)
    other = lax.dynamic_index_in_dim(halves, t ^ 1, 0, keepdims=False)
    dy = lax.dynamic_index_in_dim(cotangent.reshape(nt, rows, width), t, 0, keepdims=False)
    top = rows >> level_shifts(rows)[-1]


    normed_one, pooled = call(
        norm_one_kernel,
        [((rows, width), BF16), ((4 * top, width), BF16)],
        [info, lengths],
        [own, other, row(ln1_gain), row(ln1_bias)],
    )
    attn_line = near_line(attn_piece)
    normed_one, *attn_line = lax.optimization_barrier((normed_one, *attn_line))
    biases = jnp.stack([piece[chunk:] for piece in attn_line])
    ffn_line = line_first(ffn_piece)
    attn_line, biases = call(
        stack_kernel,
        [((nt, chunk, 4 * TILE), BF16), ((nt, 16, 4 * TILE), BF16)],
        [],
        attn_line,
    )
    attn_pieces = plane_pieces(attn_line)
    up_line, down_line = call(
        part_kernel, [((nt, chunk, hid), BF16)] * 2, [info], line_second(ffn_line)
    )
    attn_pieces, up_line, down_line = lax.optimization_barrier((attn_pieces, up_line, down_line))
    attn_near = jnp.stack(attn_pieces)
    attn_w = attn_near, swap(attn_near, "dp", 1)
    ups = [jnp.stack([up_line, swap(up_line, "dp", 2)])]
    downs = [jnp.stack([down_line] + [swap(down_line, "dp", 4 * o) for o in range(1, outer // 2)])]
    ups += [swap(ups[0], "dp", 4 * o) for o in range(1, outer // 2)]
    downs += [swap(downs[0], "dp", 2)]
    plan = [(0, 0, (2 * o, 2 * o + 1)) for o in range(outer // 2)]
    plan += [(1, 0, tuple(range(first, outer, 2))) for first in range(2)]
    plan += [(part, 1, chips) for part, _, chips in plan]

    mixed, mixed_wide, total, q, k, v, prob, attn_full = call(
        attend_kernel,
        [((nt, rows, TILE), BF16), ((nt, rows, TILE), F32), ((nt, rows, TILE), F32)]
        + [((nt, 2 * rows, TILE), BF16)] * 3
        + [((nt, 2 * rows // TILE, TILE, 2 * TILE), BF16)]
        + [((nt, width, 4 * TILE), BF16)],
        [info, lengths],
        [normed_one, pooled, *attn_w, biases],
        scratch=[
            pltpu.VMEM((2 * rows // TILE, 1, 2 * TILE), F32),
            pltpu.VMEM((2, TILE, 2 * TILE), F32),
            pltpu.VMEM((rows, 3 * TILE), F32),
            pltpu.VMEM((2 * rows, 2 * TILE), F32),
        ],
        limit=24,
        long=True,
    )
    ups, downs, mixed = lax.optimization_barrier((ups, downs, mixed))
    ffn_w = ups + downs
    ffn_w += [swap(each, "dp", 1) for each in ffn_w]
    piece = rows // dp
    hidden, normed_two, act, slope, ffn_full, out_near, out_far = call(
        functools.partial(feed_kernel, plan),
        [((rows, width), F32), ((rows, width), BF16)]
        + [((nt, rows, hid), BF16)] * 2
        + [((nt, 2, width, hid), BF16)]
        + [((outer, piece, width), BF16)] * 2,
        [info],
        [own, mixed, attn_full, *ffn_w]
        + [row(b_out), row(ln2_gain), row(ln2_bias), biases, row(b_down)],
        scratch=[pltpu.VMEM((rows, width), F32)],
        limit=28,
    )
    chunks = call(
        pair_kernel, [((2, piece, width), BF16)] * outer, [], [out_near, swap(out_far, "dp", 1)]
    )
    dy, chunks = lax.optimization_barrier((dy, chunks))

    grad_pre, grad_hidden, grad_hidden_low, numer, gtotal, sent, vec_two, vec_up = call(
        feed_back_kernel,
        [
            ((nt, rows, hid), BF16),
            ((rows, width), F32),
            ((rows, width), BF16),
            ((nt, rows, TILE), F32),
            ((nt, rows, TILE), F32),
            ((nt, 2 * top, TILE), F32),
            ((4, width), F32),
            ((nt, 1, hid), F32),
        ],
        [],
        [dy, attn_full, ffn_full, slope, hidden, row(ln2_gain), mixed_wide, total],
        limit=28,
    )
    swapped = swap(sent, "tensor", 1)
    chunks, grad_pre = lax.optimization_barrier(
        (jnp.concatenate(plane_pieces(chunks[0], chunks)), grad_pre)
    )
    chunks = line_first(chunks)
    ffn_grads = call(
        feed_grads_kernel,
        [((outer, nt, 2, chunk, hid), BF16)] * 2,
        [info],
        [normed_two, act, grad_pre, dy],
        scratch=[pltpu.VMEM((width, hid), BF16)] * 2,
    )
    ffn_far = swap(ffn_grads[1], "dp", 1)

    def core_sums(near, far):
        return [total_of([near[o], far[o]]) for o in range(outer)]

    def plane_parts(pieces):
        return [pieces[0]] + [swap(pieces[o], "dp", 2 * o) for o in range(1, outer)]

    ffn_parts = core_sums(ffn_grads[0], ffn_far)
    gtotal, ffn_parts, swapped = lax.optimization_barrier((gtotal, ffn_parts, swapped))
    ffn_parts = plane_parts(ffn_parts)
    qkv_grads, vec_qv, grad_low, vec_one = call(
        attend_back_kernel,
        [
            ((nt, rows, 3 * TILE), BF16),
            ((nt, 2, TILE), F32),
            ((rows, width), BF16),
            ((2, width), F32),
        ],
        [info, lengths],
        [numer, gtotal, swapped, q, k, v, prob, attn_full]
        + [own, row(ln1_gain), grad_hidden],
        scratch=[
            pltpu.VMEM((rows, 2 * TILE), F32),
            pltpu.VMEM((2 * rows, 2 * TILE), BF16),
            pltpu.VMEM((2 * rows, 3 * TILE), F32),
            pltpu.VMEM((rows, width), F32),
        ],
        limit=20,
        long=True,
    )
    chunks, grad_low, grad_hidden_low = lax.optimization_barrier(
        (chunks, grad_low, grad_hidden_low)
    )
    attn_near, attn_far = call(
        attend_grads_kernel,
        [((outer, nt * chunk + 16, 4 * TILE), BF16)] * 2,
        [info],
        [normed_one, qkv_grads, grad_hidden_low, mixed, vec_two, vec_up, vec_one, vec_qv],
        scratch=[pltpu.VMEM((width, 4 * TILE), BF16)],
    )
    row_pieces = line_first(grad_low)
    chunks = line_second(chunks)
    attn_far, ffn_parts = lax.optimization_barrier((attn_far, ffn_parts))
    attn_far = swap(attn_far, "dp", 1)
    cut = (nt * chunk + 16) // 2 // 16 * 16

    def chip_sum(o, rows_of):
        return (attn_near[o, rows_of].astype(F32) + attn_far[o, rows_of].astype(F32)).astype(BF16)

    fore, rest = slice(0, cut), slice(cut, None)
    fore_kept = [chip_sum(o, fore) for o in range(0, outer, 2)]
    fore_got = swap(jnp.stack([chip_sum(o, fore) for o in range(1, outer, 2)]), "dp", 2)
    rest_kept = [chip_sum(o, rest) for o in range(2)]
    rest_got = [
        swap(jnp.stack([chip_sum(2 * o, rest), chip_sum(2 * o + 1, rest)]), "dp", 4 * o)
        for o in range(1, outer // 2)
    ]
    fore_parts = [total_of([kept, fore_got[o]]) for o, kept in enumerate(fore_kept)]
    rest_parts = [total_of([rest_kept[o]] + [each[o] for each in rest_got]) for o in range(2)]
    fore_parts = [fore_parts[0]] + [swap(fore_parts[o], "dp", 4 * o) for o in range(1, outer // 2)]
    rest_parts = [rest_parts[0], swap(rest_parts[1], "dp", 2)]
    fore_parts, rest_parts, chunks = lax.optimization_barrier((fore_parts, rest_parts, chunks))
    (dealt,) = call(
        deal_kernel,
        [((dp, seq_dev, nt // seq_dev, piece, width), BF16)],
        [info, dealing],
        chunks,
        scratch=[pltpu.VMEM((nt, dp, piece, width), BF16)],
    )
    dealt = exchange(dealt, "dp")
    attn_parts = jnp.concatenate([total_of(fore_parts), total_of(rest_parts)])
    attn_parts, row_pieces[2] = lax.optimization_barrier((attn_parts, row_pieces[2]))
    ffn_parts = total_of(ffn_parts)
    grads = [
        jnp.concatenate(
            [ffn_parts[z].reshape(2 * chunk, hid), attn_parts[z * chunk : (z + 1) * chunk]]
            + [attn_parts[nt * chunk :]]
        )
        for z in range(nt)
    ]
    grads = total_of([grads[0]] + [swap(grads[z], "tensor", z) for z in range(1, nt)])
    vectors = grads[3 * chunk :].astype(F32)
    base = 4 + nt
    g_b_up = lax.dynamic_index_in_dim(vectors[4:base], t, 0, keepdims=False)
    g_b_q = lax.dynamic_index_in_dim(vectors[base + 2].reshape(nt, TILE), t, 0, keepdims=False)
    g_b_v = lax.dynamic_index_in_dim(vectors[base + 3].reshape(nt, TILE), t, 0, keepdims=False)
    vectors = [vectors[i] for i in (0, 1, 2, 3, base, base + 1)]
    grads, row_pieces[1] = lax.optimization_barrier((grads, row_pieces[1]))
    row_pieces = line_second(row_pieces)
    near = jnp.stack(plane_pieces(grads[: 3 * chunk].reshape(3, chunk, width)))
    (grad_tokens,) = call(
        place_rows_kernel,
        [((nt, rows, width), BF16)],
        [info],
        row_pieces,
        scratch=[pltpu.SemaphoreType.DMA((5,))],
        off_chip=True,
    )
    grad_tokens = grad_tokens.reshape(seq_dev, length, width)
    near, grad_tokens, dealt, vectors, g_b_up, g_b_q, g_b_v = lax.optimization_barrier(
        (near, grad_tokens, dealt, vectors, g_b_up, g_b_q, g_b_v)
    )
    grads = near, swap(near, "dp", 1)
    g_up, g_down, g_query, g_key, g_value, g_out = call(
        place_grads_kernel,
        [((width, hid), F32), ((hid, width), F32)]
        + [((width, TILE), F32)] * 3
        + [((TILE, width), F32)],
        [info],
        grads,
        scratch=[pltpu.VMEM((width, TILE), F32)],
    )
    (output,) = call(
        settle_kernel,
        [((seq_dev, nt // seq_dev, dp, piece, width), BF16)],
        [],
        [pltpu.with_memory_space_constraint(dealt, pltpu.HBM)],
    )
    output = output.reshape(seq_dev, length, width)
    return (
        output,
        grad_tokens,
        vectors[4],
        vectors[5],
        g_query,
        g_b_q,
        g_key,
        g_value,
        g_b_v,
        g_out,
        vectors[3],
        vectors[0],
        vectors[1],
        g_up,
        g_b_up,
        g_down,
        vectors[2],
    )


def solution(mesh):
    placed = (
        P("dp", None, None),
        P("dp", None, None),
        P(),
        P(),
        P(),
        P(),
        P(None, "tensor"),
        P("tensor"),
        P(None, "tensor"),
        P(None, "tensor"),
        P("tensor"),
        P("tensor", None),
        P(),
        P(),
        P(),
        P(None, "tensor"),
        P("tensor"),
        P("tensor", None),
        P(),
    )
    return jax.shard_map(
        local,
        mesh=mesh,
        in_specs=placed,
        out_specs=(
            P("dp", None, None),
            P("dp", None, None),
            P(),
            P(),
            P(None, "tensor"),
            P("tensor"),
            P(None, "tensor"),
            P(None, "tensor"),
            P("tensor"),
            P("tensor", None),
            P(),
            P(),
            P(),
            P(None, "tensor"),
            P("tensor"),
            P("tensor", None),
            P(),
        ),
        check_vma=False,
    )
```
